256 devices in a mesh: seq: 64 (over z, x, core), fsdp: 4 (over y).
Axes of the slice: x: 4, y: 4, z: 8, core: 2. Of those that a mesh axis runs over, the one named last changes fastest.
Arguments:
- query_rows: bfloat16 [32768, 4096], P('seq', 'fsdp'), may hold values from -6 to 6
- key_rows: bfloat16 [32768, 4096], P('seq', 'fsdp'), may hold values from -0.5390625 to 0.5390625
- value_rows: bfloat16 [32768, 4096], P('seq', 'fsdp'), may hold values from -6 to 6
- norm_gain: float32 [4096], P('fsdp'), may hold values from 0.1 to 1.9
- out_weight: bfloat16 [4096, 4096], P(None, 'fsdp'), may hold values from -0.09375 to 0.09375
Outputs:
- mixed: bfloat16 [32768, 4096], P('seq', 'fsdp')
The draws below stay inside these ranges and needn't reach their ends.
All inputs are finite; a program needn't handle non-finite values.
Results may differ from the reference program's by a relative error of at most 0.012.
Values may be sent and summed in bfloat16 or wider, within the bound.
No kernel may reach another device: no remote copies, remote signals or barrier semaphores. Data moves between devices by JAX's collectives and lax.ppermute only.
A program may use at most 192 MiB of HBM per device.

```python
import jax
import jax.numpy as jnp
from jax import lax

D = 4096
HEADS = 32
DH = 128
BLK = 512
TOKENS = 32768


def block_levels(stream_key, dims, pieces, least, largest):
    def one(axis_at, parts):
        heights = jax.random.uniform(jax.random.fold_in(jax.random.fold_in(stream_key, 6), axis_at), (parts,), jnp.float32, least / len(pieces), largest / len(pieces))
        return jnp.repeat(jnp.exp(heights), dims[axis_at] // parts).reshape((-1,) + (1,) * (len(dims) - axis_at - 1))

    loudness = one(*pieces[0])
    for cut in pieces[1:]:
        loudness = loudness * one(*cut)
    return loudness


def noise(key, dims, width, limit, cuts=(), kind=jnp.bfloat16):
    loudness = block_levels(key, dims, cuts, -0.22, 0.18) if cuts else 1.0
    result = jax.random.normal(key, dims, jnp.float32) * width * loudness
    return jnp.minimum(jnp.maximum(result, -limit), limit).astype(kind)


def setup_inputs(seed: int = 0) -> dict:
    streams_of = jax.random.split(jax.random.key(seed), 6)
    return {
        "query_rows": noise(streams_of[0], (TOKENS, HEADS * DH), 1.0, 6.0, ((0, 64), (1, 4))),
        "key_rows": noise(streams_of[1], (TOKENS, HEADS * DH), 0.09, 0.5390625, ((0, 64), (1, 4))),
        "value_rows": noise(streams_of[2], (TOKENS, HEADS * DH), 1.0, 6.0, ((0, 64), (1, 4))),
        "norm_gain": jnp.clip(1.0 + 0.18 * jax.random.normal(streams_of[3], (HEADS * DH,), jnp.float32), 0.1, 1.9),
        "out_weight": noise(streams_of[4], (HEADS * DH, D), (HEADS * DH) ** -0.5, 0.09375, ((1, 4),)),
    }


def reference(query_rows, key_rows, value_rows, norm_gain, out_weight):
    n_blocks = TOKENS // BLK
    queries_b = query_rows.reshape(n_blocks, BLK, HEADS, DH).astype(jnp.float32)
    keys_b = key_rows.reshape(n_blocks, BLK, HEADS, DH).astype(jnp.float32)
    values_b = value_rows.reshape(n_blocks, BLK, HEADS, DH).astype(jnp.float32)
    position = lax.broadcasted_iota(jnp.int32, (BLK, BLK), 0)
    column = lax.broadcasted_iota(jnp.int32, (BLK, BLK), 1)
    causal_mask = column <= position
    highest = lax.Precision.HIGHEST

    def block_step(carried, block_data):
        query_block, key_block, value_block = block_data
        scores = jnp.einsum('qhd,khd->hqk', query_block, key_block, precision=highest)
        masked_scores = jnp.where(causal_mask[None], scores, 0.0).astype(jnp.bfloat16)
        within_block = jnp.einsum('hqk,khd->qhd', masked_scores.astype(jnp.float32), value_block, precision=highest)
        from_state = jnp.einsum('qhd,hde->qhe', query_block, carried, precision=highest)
        block_state = jnp.einsum('khd,khe->hde', key_block, value_block, precision=highest)
        return (carried + block_state, within_block + from_state)
    start_state = jnp.zeros((HEADS, DH, DH), jnp.float32)
    final_state, attention = lax.scan(block_step, start_state, (queries_b, keys_b, values_b))
    mean_square = lax.optimization_barrier(jnp.mean(attention * attention, axis=-1, keepdims=True))
    normed = attention * lax.rsqrt(mean_square + 1e-06) * norm_gain.reshape(HEADS, DH)
    normed = normed.astype(jnp.bfloat16).reshape(TOKENS, HEADS * DH)
    return jnp.dot(normed, out_weight, preferred_element_type=jnp.float32).astype(jnp.bfloat16)
```

```python
import functools

import jax
import jax.numpy as jnp
from jax import lax
from jax.experimental import pallas as pl
from jax.experimental.pallas import tpu as pltpu
from jax.sharding import PartitionSpec as P

DH = 128
BLK = 512
F32 = jnp.float32
BF16 = jnp.bfloat16


def dot(a, b, dims):
    return lax.dot_general(a, b, (dims, ((), ())), preferred_element_type=F32)


def state_kernel(pos_ref, k_ref, v_ref, keep_ref, send_ref):
    group = pos_ref[0]
    for d in (1, 3, 5, 7, 0, 2, 4, 6):
        cols = pl.ds(pl.multiple_of((group ^ d) * DH, DH), DH)
        state = dot(k_ref[:, cols], v_ref[:, cols], ((0,), (0,)))
        if d % 2:
            send_ref[d // 2] = state.astype(BF16)
        else:
            keep_ref[d // 2] = state


def block_states(pos, k, v):
    vmem = pl.BlockSpec(memory_space=pltpu.VMEM)
    return pl.pallas_call(
        state_kernel,
        name="block_states",
        in_specs=[pl.BlockSpec(memory_space=pltpu.SMEM), vmem, vmem],
        out_specs=[vmem, vmem],
        out_shape=[
            jax.ShapeDtypeStruct((4, DH, DH), F32),
            jax.ShapeDtypeStruct((4, DH, DH), BF16),
        ],
        cost_estimate=pl.CostEstimate(
            flops=2 * 8 * BLK * DH * DH, bytes_accessed=3 * 2**20, transcendentals=0
        ),
    )(pos, k, v)


def within_kernel(q_ref, k_ref, v_ref, out_ref):
    half = BLK // 2
    row = lax.broadcasted_iota(jnp.int32, (half, half), 0)
    col = lax.broadcasted_iota(jnp.int32, (half, half), 1)
    causal = col <= row
    for h in range(q_ref.shape[1] // DH):
        cols = slice(h * DH, (h + 1) * DH)
        q0, q1 = q_ref[:half, cols], q_ref[half:, cols]
        k0, k1 = k_ref[:half, cols], k_ref[half:, cols]
        v0, v1 = v_ref[:half, cols], v_ref[half:, cols]
        nt = ((1,), (1,))
        nn = ((1,), (0,))
        s00 = jnp.where(causal, dot(q0, k0, nt), 0.0).astype(BF16)
        s10 = dot(q1, k0, nt).astype(BF16)
        s11 = jnp.where(causal, dot(q1, k1, nt), 0.0).astype(BF16)
        out_ref[:half, cols] = dot(s00, v0, nn)
        out_ref[half:, cols] = dot(s10, v0, nn) + dot(s11, v1, nn)


def within_block(q, k, v, part, parts):
    width = q.shape[1] // parts
    spec = pl.BlockSpec((BLK, width), lambda i: (0, part))
    return pl.pallas_call(
        within_kernel,
        name="within_block",
        grid=(1,),
        in_specs=[spec] * 3,
        out_specs=pl.BlockSpec((BLK, width), lambda i: (0, 0)),
        out_shape=jax.ShapeDtypeStruct((BLK, width), F32),
        cost_estimate=pl.CostEstimate(
            flops=3 * BLK * BLK * width, bytes_accessed=BLK * width * 10, transcendentals=0
        ),
    )(q, k, v)


def norm_kernel(q_ref, w0_ref, w1_ref, c_ref, g_ref, out_ref):
    for h in range(4):
        cols = slice(h * DH, (h + 1) * DH)
        half = slice((h % 2) * DH, (h % 2 + 1) * DH)
        within = (w0_ref, w1_ref)[h // 2][:, half]
        att = within + dot(q_ref[:, cols], c_ref[h], ((1,), (0,)))
        mean_square = jnp.mean(att * att, axis=1, keepdims=True)
        out_ref[:, cols] = (att * lax.rsqrt(mean_square + 1e-6) * g_ref[:, cols]).astype(BF16)


def normed_part(q, w0, w1, carried, gain, part):
    width = 4 * DH
    full = lambda i: (0, 0)
    return pl.pallas_call(
        norm_kernel,
        name="normed_part",
        grid=(1,),
        in_specs=[
            pl.BlockSpec((BLK, width), lambda i: (0, part)),
            pl.BlockSpec((BLK, 2 * DH), full),
            pl.BlockSpec((BLK, 2 * DH), full),
            pl.BlockSpec((4, DH, DH), lambda i: (part, 0, 0)),
            pl.BlockSpec((1, width), lambda i: (0, part)),
        ],
        out_specs=pl.BlockSpec((BLK, width), full),
        out_shape=jax.ShapeDtypeStruct((BLK, width), BF16),
        cost_estimate=pl.CostEstimate(
            flops=2 * BLK * DH * width, bytes_accessed=BLK * width * 8, transcendentals=BLK * 4
        ),
    )(q, w0, w1, carried, gain)


def mix_kernel(rows_ref, *refs, pieces, first, last):
    del rows_ref
    a_refs, w_refs = refs[:pieces], refs[pieces : 2 * pieces]
    rest = refs[2 * pieces :]
    total = None if first else rest[0][...]
    for a_ref, w_ref in zip(a_refs, w_refs):
        term = dot(a_ref[...], w_ref[...], ((1,), (0,)))
        total = term if total is None else total + term
    rest[-1][...] = total.astype(BF16) if last else total


def mix(w, blocks, arrays, total, last):
    pieces = len(arrays)
    rows, depth = arrays[0].shape
    tile = 256
    cols = w.shape[1]
    in_specs = [pl.BlockSpec((rows, depth), lambda i, r: (0, 0))] * pieces
    in_specs += [
        pl.BlockSpec((depth, tile), functools.partial(lambda p, i, r: (r[p], i), p))
        for p in range(pieces)
    ]
    operands = list(arrays) + [w] * pieces
    if total is not None:
        in_specs.append(pl.BlockSpec((rows, tile), lambda i, r: (0, i)))
        operands.append(total)
    return pl.pallas_call(
        functools.partial(mix_kernel, pieces=pieces, first=total is None, last=last),
        name="mix",
        grid_spec=pltpu.PrefetchScalarGridSpec(
            num_scalar_prefetch=1,
            grid=(cols // tile,),
            in_specs=in_specs,
            out_specs=pl.BlockSpec((rows, tile), lambda i, r: (0, i)),
        ),
        out_shape=jax.ShapeDtypeStruct((rows, cols), BF16 if last else F32),
        cost_estimate=pl.CostEstimate(
            flops=2 * rows * depth * pieces * cols,
            bytes_accessed=pieces * depth * (rows + cols) * 2 + rows * cols * 8,
            transcendentals=0,
        ),
    )(blocks, *operands)


def swap(value, bit, count):
    return lax.ppermute(value, "seq", [(i, i ^ bit) for i in range(count)])


def carried_states(keep, send, index, count):
    def high(bit):
        return ((index & bit) != 0).astype(F32)

    def low(bit):
        return ((index & bit) == 0).astype(F32)

    own0 = keep
    got0 = swap(send, 1, count).astype(F32)
    tot0 = own0 + got0
    own1 = tot0[0::2]
    got1 = swap(tot0[1::2].astype(BF16), 2, count).astype(F32)
    tot1 = own1 + got1
    own2 = tot1[0]
    got2 = swap(tot1[1].astype(BF16), 4, count).astype(F32)
    total = own2 + got2
    before = jnp.zeros_like(total)
    bit = 8
    while bit < count // 2:
        got = swap(total.astype(BF16), bit, count).astype(F32)
        before = before + high(bit) * got
        total = total + got
        bit *= 2
    got = lax.ppermute(
        total.astype(BF16), "seq", [(i, i + bit) for i in range(count) if not i & bit]
    )
    before = before + got.astype(F32)
    back2 = swap((before + low(4) * own2).astype(BF16), 4, count)
    mine2 = before + high(4) * got2
    pre1 = jnp.stack([mine2, back2.astype(F32)])
    back1 = swap((pre1 + low(2) * own1).astype(BF16), 2, count)
    mine1 = pre1 + high(2) * got1
    pre0 = jnp.stack([mine1[0], back1[0].astype(F32), mine1[1], back1[1].astype(F32)])
    back0 = swap((pre0 + low(1) * own0).astype(BF16), 1, count)
    mine0 = (pre0 + high(1) * got0).astype(BF16)
    by_slot = jnp.stack([mine0, back0], axis=1).reshape(8, DH, DH)
    order = (index & 7) ^ jnp.arange(8)
    return by_slot[order]


def along(value, shift, count):
    return lax.ppermute(value, "fsdp", [(i, (i + shift) % count) for i in range(count)])


def shards(q, k, v, gain, w):
    index = lax.axis_index("seq")
    column = lax.axis_index("fsdp")
    count, ways = lax.axis_size("seq"), lax.axis_size("fsdp")
    pos = (index & 7).reshape(1)
    keep, send = block_states(pos, k, v)
    carried = carried_states(keep, send, index, count)
    within = [within_block(q, k, v, part, 4) for part in range(4)]
    gain_row = gain.reshape(1, -1)
    own, left, right, far = [], [], [], []
    for part in range(2):
        mine = normed_part(q, within[2 * part], within[2 * part + 1], carried, gain_row, part)
        from_left = along(mine, 1, ways)
        from_right = along(mine, -1, ways)
        top = along(from_left[: BLK // 2], 1, ways)
        bottom = along(from_right[BLK // 2 :], -1, ways)
        own.append(mine)
        left.append(from_left)
        right.append(from_right)
        far.append(jnp.concatenate([top, bottom]))

    def rows(shift, part):
        return (column + shift + ways) % ways * 2 + part

    def table(*entries):
        return jnp.stack(entries).astype(jnp.int32)

    total = mix(w, table(rows(0, 0), rows(0, 1)), own, None, False)
    for part in range(2):
        total = mix(
            w, table(rows(-1, part), rows(1, part)), [left[part], right[part]], total, False
        )
    return mix(w, table(rows(2, 0), rows(2, 1)), far, total, True)


def solution(mesh):
    placed = (P("seq", "fsdp"), P("seq", "fsdp"), P("seq", "fsdp"), P("fsdp"), P(None, "fsdp"))
    return jax.shard_map(
        shards, mesh=mesh, in_specs=placed, out_specs=P("seq", "fsdp"), check_vma=False
    )
```

```python
import functools

import jax
import jax.numpy as jnp
from jax import lax
from jax.experimental import pallas as pl
from jax.experimental.pallas import tpu as pltpu
from jax.sharding import Mesh
from jax.sharding import PartitionSpec as P

DH = 128
BLK = 512
HALF = BLK // 2
CORES = 2
CHUNKS = ((0, 2), (2, 5), (5, 8))
F32 = jnp.float32
BF16 = jnp.bfloat16
NN, NT, TN = ((1,), (0,)), ((1,), (1,)), ((0,), (0,))
SMEM = pl.BlockSpec(memory_space=pltpu.SMEM)
VMEM = pl.BlockSpec(memory_space=pltpu.VMEM)
PARAMS = pltpu.CompilerParams(vmem_limit_bytes=20 * 2**20)


def dot(a, b, dims):
    return lax.dot_general(a, b, (dims, ((), ())), preferred_element_type=F32)


def in_vmem(value):
    return pltpu.with_memory_space_constraint(value, pltpu.VMEM)


def cost(flops, size):
    return pl.CostEstimate(flops=flops, bytes_accessed=size, transcendentals=0)


def state_kernel(k_ref, v_ref, out_ref):
    for h in range(k_ref.shape[1] // DH):
        cols = slice(h * DH, (h + 1) * DH)
        state = dot(k_ref[:, cols], v_ref[:, cols], TN)
        out_ref[h * DH : (h + 1) * DH, :] = state.astype(BF16)


def block_states(k, v):
    width = k.shape[1]
    return pl.pallas_call(
        state_kernel,
        name="block_states",
        in_specs=[VMEM, VMEM],
        out_specs=VMEM,
        out_shape=pltpu.VMEM((width, DH), BF16),
        compiler_params=PARAMS,
        cost_estimate=cost(2 * BLK * DH * width, 2 * BLK * width * 2),
    )(k, v)


def scan_kernel(core_ref, own_ref, other_ref, out_ref, *, chips):
    rows = own_ref.shape[0] // chips
    second = (core_ref[0] == 1).astype(F32)
    before = jnp.zeros((rows, DH), F32)
    for chip in range(chips):
        at = slice(chip * rows, (chip + 1) * rows)
        other = other_ref[at, :].astype(F32)
        out_ref[at, :] = (before + second * other).astype(BF16)
        before = before + (own_ref[at, :].astype(F32) + other)


def exclusive_sums(core, own, other, chips):
    return pl.pallas_call(
        functools.partial(scan_kernel, chips=chips),
        name="exclusive_sums",
        in_specs=[SMEM, VMEM, VMEM],
        out_specs=VMEM,
        out_shape=pltpu.VMEM(own.shape, BF16),
        compiler_params=PARAMS,
        cost_estimate=cost(own.size * 4, own.size * 6),
    )(core, own, other)


def attention_kernel(q_ref, k_ref, v_ref, carried_ref, gain_ref, out_ref, *, first):
    row = lax.broadcasted_iota(jnp.int32, (HALF, HALF), 0)
    col = lax.broadcasted_iota(jnp.int32, (HALF, HALF), 1)
    causal = col <= row
    mean = jnp.full((DH, DH), 1.0 / DH, BF16)
    for at in range(out_ref.shape[1] // DH):
        h = first + at
        cols = slice(h * DH, (h + 1) * DH)
        q0, q1 = q_ref[:HALF, cols], q_ref[HALF:, cols]
        k0, k1 = k_ref[:HALF, cols], k_ref[HALF:, cols]
        v0, v1 = v_ref[:HALF, cols], v_ref[HALF:, cols]
        s00 = jnp.where(causal, dot(q0, k0, NT), 0.0).astype(BF16)
        s10 = dot(q1, k0, NT).astype(BF16)
        s11 = jnp.where(causal, dot(q1, k1, NT), 0.0).astype(BF16)
        top = dot(s00, v0, NN)
        bottom = dot(s10, v0, NN) + dot(s11, v1, NN)
        state = carried_ref[cols, :]
        for rows, queries, within in ((slice(0, HALF), q0, top), (slice(HALF, BLK), q1, bottom)):
            att = within + dot(queries, state, NN)
            mean_square = dot((att * att).astype(BF16), mean, NN)
            normed = att * lax.rsqrt(mean_square + 1e-6) * gain_ref[:, cols]
            out_ref[rows, at * DH : (at + 1) * DH] = normed.astype(BF16)


def attention(q, k, v, carried, gain, first, last):
    width = (last - first) * DH
    return pl.pallas_call(
        functools.partial(attention_kernel, first=first),
        name="attention",
        in_specs=[VMEM] * 5,
        out_specs=VMEM,
        out_shape=pltpu.VMEM((BLK, width), BF16),
        compiler_params=PARAMS,
        cost_estimate=cost(4 * BLK * BLK * width, BLK * width * 8),
    )(q, k, v, carried, gain)


TILE = 256


def mix_kernel(column_ref, *refs, plan, first, last):
    count = len(plan)
    a_refs, w_ref = refs[:count], refs[count]
    rest = refs[count + 1 :]
    if not first:
        total_ref, rest = rest[0], rest[1:]
    if last:
        out_hbm, out_ref, sems = rest
    else:
        (out_ref,) = rest
    ways = w_ref.shape[0] // (8 * DH)
    copies = []
    for tile in range(w_ref.shape[1] // TILE):
        cols = slice(tile * TILE, (tile + 1) * TILE)
        for low, high in ((0, HALF), (HALF, BLK)):
            total = None if first else total_ref[low:high, cols]
            for a_ref, (shift, head, begin, end) in zip(a_refs, plan):
                if end <= low or begin >= high:
                    continue
                source = lax.rem(column_ref[0] + (shift + ways), ways)
                start = pl.multiple_of(source * (8 * DH) + head * DH, DH)
                weights = w_ref[pl.ds(start, a_ref.shape[1]), cols]
                term = dot(a_ref[low - begin : high - begin, :], weights, NN)
                total = term if total is None else total + term
            out_ref[low:high, cols] = total.astype(out_ref.dtype)
        if last:
            copy = pltpu.make_async_copy(out_ref.at[:, cols], out_hbm.at[:, cols], sems.at[tile])
            copy.start()
            copies.append(copy)
    for copy in copies:
        copy.wait()


def mix(column, w, plan, arrays, total=None, last=False):
    width = w.shape[1]
    operands = [column, *arrays, w] + ([] if total is None else [total])
    depth = sum(a.size for a in arrays)
    if last:
        out_shape = jax.ShapeDtypeStruct((BLK, width), BF16)
        scratch = [pltpu.VMEM((BLK, width), BF16), pltpu.SemaphoreType.DMA((width // TILE,))]
    else:
        out_shape, scratch = pltpu.VMEM((BLK, width), F32), []
    return pl.pallas_call(
        functools.partial(mix_kernel, plan=tuple(plan), first=total is None, last=last),
        name="mix",
        in_specs=[SMEM] + [VMEM] * (len(operands) - 1),
        out_specs=pl.BlockSpec(memory_space=pl.ANY) if last else VMEM,
        out_shape=out_shape,
        scratch_shapes=scratch,
        compiler_params=PARAMS,
        cost_estimate=cost(2 * depth * width, 2 * depth + BLK * width * 8),
    )(*operands)


def along(value, shift, count):
    return lax.ppermute(value, "fsdp", [(i, (i + shift) % count) for i in range(count)])


def shards(q, k, v, gain, w):
    chips, ways = lax.axis_size("chip"), lax.axis_size("fsdp")
    core = lax.axis_index("core").reshape(1)
    column = lax.axis_index("fsdp").reshape(1)
    states = block_states(k, v)
    own = lax.all_to_all(states, "chip", 0, 0, tiled=True)
    other = lax.ppermute(own, "core", [(0, 1), (1, 0)])
    sums = exclusive_sums(core, own, other, chips)
    carried = lax.all_to_all(sums, "chip", 0, 0, tiled=True)
    q, k, v, w = in_vmem(q), in_vmem(k), in_vmem(v), in_vmem(w)
    gain_row = gain.reshape(1, -1)
    total, tail = None, []
    own_plan, own_rows, near = [], [], []
    for first, last in CHUNKS:
        mine = attention(q, k, v, carried, gain_row, first, last)
        from_left = along(mine, 1, ways)
        from_right = along(mine, -1, ways)
        top = along(from_left[:HALF], 1, ways)
        bottom = along(from_right[HALF:], -1, ways)
        own_plan.append((0, first, 0, BLK))
        own_rows.append(mine)
        near.append(([(-1, first, 0, BLK), (1, first, 0, BLK)], [from_left, from_right]))
        tail.append(([(2, first, 0, HALF), (2, first, HALF, BLK)], [top, bottom]))
    total = mix(column, w, own_plan, own_rows)
    steps = [near[0], near[1], tail[0], near[2], tail[1], tail[2]]
    for at, (plan, arrays) in enumerate(steps):
        total = mix(column, w, plan, arrays, total, at == len(steps) - 1)
    return total


def solution(mesh):
    seq, fsdp = mesh.devices.shape
    fine = Mesh(mesh.devices.reshape(seq // CORES, CORES, fsdp), ("chip", "core", "fsdp"))
    rows = ("chip", "core")
    placed = (P(rows, "fsdp"), P(rows, "fsdp"), P(rows, "fsdp"), P("fsdp"), P(None, "fsdp"))
    return jax.shard_map(
        shards, mesh=fine, in_specs=placed, out_specs=P(rows, "fsdp"), check_vma=False
    )
```

```python
import functools

import jax
import jax.numpy as jnp
from jax import lax
from jax.experimental import pallas as pl
from jax.experimental.pallas import tpu as pltpu
from jax.sharding import Mesh
from jax.sharding import PartitionSpec as P

DH = 128
BLK = 512
HALF = BLK // 2
CORES = 2
CHUNKS = ((0, 4), (4, 8))
F32 = jnp.float32
BF16 = jnp.bfloat16
NN, NT, TN = ((1,), (0,)), ((1,), (1,)), ((0,), (0,))
SMEM = pl.BlockSpec(memory_space=pltpu.SMEM)
VMEM = pl.BlockSpec(memory_space=pltpu.VMEM)
HBM = pl.BlockSpec(memory_space=pltpu.HBM)
PARAMS = pltpu.CompilerParams(vmem_limit_bytes=20 * 2**20)


def dot(a, b, dims):
    return lax.dot_general(a, b, (dims, ((), ())), preferred_element_type=F32)


def in_vmem(value):
    return pltpu.with_memory_space_constraint(value, pltpu.VMEM)


def cost(flops, size):
    return pl.CostEstimate(flops=flops, bytes_accessed=size, transcendentals=0)


PARTS = 2


def state_kernel(k_hbm, v_hbm, out_ref, k_ref, v_ref, sems):
    width = k_ref.shape[1] // PARTS
    copies = []
    for part in range(PARTS):
        cols = slice(part * width, (part + 1) * width)
        for at, (hbm, ref) in enumerate(((k_hbm, k_ref), (v_hbm, v_ref))):
            copy = pltpu.make_async_copy(hbm.at[:, cols], ref.at[:, cols], sems.at[part, at])
            copy.start()
            copies.append(copy)
    for part in range(PARTS):
        copies[2 * part].wait()
        copies[2 * part + 1].wait()
        for h in range(part * width // DH, (part + 1) * width // DH):
            cols = slice(h * DH, (h + 1) * DH)
            out_ref[cols, :] = dot(k_ref[:, cols], v_ref[:, cols], TN).astype(BF16)


def block_states(k, v):
    width = k.shape[1]
    return pl.pallas_call(
        state_kernel,
        name="block_states",
        in_specs=[HBM, HBM],
        out_specs=VMEM,
        out_shape=pltpu.VMEM((width, DH), BF16),
        scratch_shapes=[
            pltpu.VMEM(k.shape, BF16),
            pltpu.VMEM(v.shape, BF16),
            pltpu.SemaphoreType.DMA((PARTS, 2)),
        ],
        compiler_params=PARAMS,
        cost_estimate=cost(2 * BLK * DH * width, 2 * BLK * width * 2),
    )(k, v)


def scan_kernel(core_ref, own_ref, other_ref, out_ref, *, chips):
    rows = own_ref.shape[0] // chips
    second = (core_ref[0] == 1).astype(F32)
    before = jnp.zeros((rows, DH), F32)
    for chip in range(chips):
        at = slice(chip * rows, (chip + 1) * rows)
        other = other_ref[at, :].astype(F32)
        out_ref[at, :] = (before + second * other).astype(BF16)
        before = before + (own_ref[at, :].astype(F32) + other)


def exclusive_sums(core, own, other, chips):
    return pl.pallas_call(
        functools.partial(scan_kernel, chips=chips),
        name="exclusive_sums",
        in_specs=[SMEM, VMEM, VMEM],
        out_specs=VMEM,
        out_shape=pltpu.VMEM(own.shape, BF16),
        compiler_params=PARAMS,
        cost_estimate=cost(own.size * 4, own.size * 6),
    )(core, own, other)


def attention_kernel(q_ref, k_ref, v_ref, carried_ref, gain_ref, out_ref, *, first):
    row = lax.broadcasted_iota(jnp.int32, (HALF, HALF), 0)
    col = lax.broadcasted_iota(jnp.int32, (HALF, HALF), 1)
    causal = col <= row
    mean = jnp.full((DH, DH), 1.0 / DH, BF16)
    for at in range(out_ref.shape[1] // DH):
        h = first + at
        cols = slice(h * DH, (h + 1) * DH)
        q0, q1 = q_ref[:HALF, cols], q_ref[HALF:, cols]
        k0, k1 = k_ref[:HALF, cols], k_ref[HALF:, cols]
        v0, v1 = v_ref[:HALF, cols], v_ref[HALF:, cols]
        s00 = jnp.where(causal, dot(q0, k0, NT), 0.0).astype(BF16)
        s10 = dot(q1, k0, NT).astype(BF16)
        s11 = jnp.where(causal, dot(q1, k1, NT), 0.0).astype(BF16)
        top = dot(s00, v0, NN)
        bottom = dot(s10, v0, NN) + dot(s11, v1, NN)
        state = carried_ref[cols, :]
        for rows, queries, within in ((slice(0, HALF), q0, top), (slice(HALF, BLK), q1, bottom)):
            att = within + dot(queries, state, NN)
            mean_square = dot((att * att).astype(BF16), mean, NN)
            normed = att * lax.rsqrt(mean_square + 1e-6) * gain_ref[:, cols]
            out_ref[rows, at * DH : (at + 1) * DH] = normed.astype(BF16)


def attention(q, k, v, carried, gain, first, last):
    width = (last - first) * DH
    return pl.pallas_call(
        functools.partial(attention_kernel, first=first),
        name="attention",
        in_specs=[VMEM] * 5,
        out_specs=VMEM,
        out_shape=pltpu.VMEM((BLK, width), BF16),
        compiler_params=PARAMS,
        cost_estimate=cost(4 * BLK * BLK * width, BLK * width * 8),
    )(q, k, v, carried, gain)


TILE = 256


def mix_kernel(column_ref, *refs, plan, first):
    count = len(plan)
    a_refs, w_hbm, rest = refs[:count], refs[count], refs[count + 1 :]
    if not first:
        total_ref, rest = rest[0], rest[1:]
    out_ref, w_ref, sems = rest
    ways = w_hbm.shape[0] // (8 * DH)
    copies, at = [], 0
    for piece, (a_ref, (shift, head)) in enumerate(zip(a_refs, plan)):
        depth = a_ref.shape[1]
        source = lax.rem(column_ref[0] + (shift + ways), ways)
        start = pl.multiple_of(source * (8 * DH) + head * DH, DH)
        rows = slice(at, at + depth)
        copies.append(
            pltpu.make_async_copy(w_hbm.at[pl.ds(start, depth)], w_ref.at[rows], sems.at[piece])
        )
        copies[-1].start()
        at += depth
    for copy in copies:
        copy.wait()
    for tile in range(out_ref.shape[1] // TILE):
        cols = slice(tile * TILE, (tile + 1) * TILE)
        total, at = None if first else total_ref[:, cols], 0
        for a_ref in a_refs:
            depth = a_ref.shape[1]
            term = dot(a_ref[...], w_ref[at : at + depth, cols], NN)
            total = term if total is None else total + term
            at += depth
        out_ref[:, cols] = total


def mix(column, w, plan, arrays, total=None):
    width = w.shape[1]
    operands = [column, *arrays, w] + ([] if total is None else [total])
    depth = sum(a.shape[1] for a in arrays)
    specs = [SMEM] + [VMEM] * (len(operands) - 1)
    specs[1 + len(arrays)] = HBM
    return pl.pallas_call(
        functools.partial(mix_kernel, plan=tuple(plan), first=total is None),
        name="mix",
        in_specs=specs,
        out_specs=VMEM,
        out_shape=pltpu.VMEM((BLK, width), F32),
        scratch_shapes=[
            pltpu.VMEM((depth, width), BF16),
            pltpu.SemaphoreType.DMA((len(arrays),)),
        ],
        compiler_params=PARAMS,
        cost_estimate=cost(2 * BLK * depth * width, 2 * depth * width),
    )(*operands)


def last_kernel(a_ref, w_ref, total_ref, out_hbm, out_ref, sems):
    copies = []
    for tile in range(w_ref.shape[1] // TILE):
        cols = slice(tile * TILE, (tile + 1) * TILE)
        total = total_ref[:, cols] + dot(a_ref[...], w_ref[:, cols], NN)
        out_ref[:, cols] = total.astype(BF16)
        copy = pltpu.make_async_copy(out_ref.at[:, cols], out_hbm.at[:, cols], sems.at[tile])
        copy.start()
        copies.append(copy)
    for copy in copies:
        copy.wait()


def last_mix(array, w, total):
    depth, width = w.shape
    return pl.pallas_call(
        last_kernel,
        name="last_mix",
        in_specs=[VMEM] * 3,
        out_specs=HBM,
        out_shape=jax.ShapeDtypeStruct((BLK, width), BF16),
        scratch_shapes=[
            pltpu.VMEM((BLK, width), BF16),
            pltpu.SemaphoreType.DMA((width // TILE,)),
        ],
        compiler_params=PARAMS,
        cost_estimate=cost(2 * BLK * depth * width, BLK * width * 4),
    )(array, w, total)


def along(value, shift, count):
    return lax.ppermute(value, "fsdp", [(i, (i + shift) % count) for i in range(count)])


def shards(q, k, v, gain, w):
    chips, ways = lax.axis_size("chip"), lax.axis_size("fsdp")
    core = lax.axis_index("core").reshape(1)
    column = lax.axis_index("fsdp").reshape(1)
    states = block_states(k, v)
    own = lax.all_to_all(states, "chip", 0, 0, tiled=True)
    other = lax.ppermute(own, "core", [(0, 1), (1, 0)])
    sums = exclusive_sums(core, own, other, chips)
    carried = lax.all_to_all(sums, "chip", 0, 0, tiled=True)
    q, k, v = in_vmem(q), in_vmem(k), in_vmem(v)
    gain_row = gain.reshape(1, -1)
    own, near, far = [], [], []
    for at, (first, last) in enumerate(CHUNKS):
        mine = attention(q, k, v, carried, gain_row, first, last)
        left = along(mine, 1, ways)
        right = along(mine, -1, ways)
        far.append(along(right, -1, ways) if at % 2 else along(left, 1, ways))
        own.append(mine)
        near.append([left, right])
    heads = [first for first, _ in CHUNKS]
    total = mix(column, w, [(0, head) for head in heads], own)
    for head, pair in zip(heads, near):
        total = mix(column, w, [(-1, head), (1, head)], pair, total)
    total = mix(column, w, [(2, heads[0])], far[:1], total)
    row = lax.rem(column[0] + ways // 2, ways) * (8 * DH) + heads[1] * DH
    tail = in_vmem(lax.dynamic_slice_in_dim(w, row, far[1].shape[1]))
    return last_mix(far[1], tail, total)


def solution(mesh):
    seq, fsdp = mesh.devices.shape
    fine = Mesh(mesh.devices.reshape(seq // CORES, CORES, fsdp), ("chip", "core", "fsdp"))
    rows = ("chip", "core")
    placed = (P(rows, "fsdp"), P(rows, "fsdp"), P(rows, "fsdp"), P("fsdp"), P(None, "fsdp"))
    return jax.shard_map(
        shards, mesh=fine, in_specs=placed, out_specs=P(rows, "fsdp"), check_vma=False
    )
```

```python
import functools

import jax
import jax.numpy as jnp
from jax import lax
from jax.experimental import pallas as pl
from jax.experimental.pallas import tpu as pltpu
from jax.sharding import Mesh
from jax.sharding import PartitionSpec as P

DH = 128
BLK = 512
HALF = BLK // 2
CORES = 2
HEADS = 8
LATE = 5
EARLY = HEADS - LATE
GAIN_ROWS = 16
CALLS = (((0, 1), (1, 2)), ((2, 3), (3, 5)))
F32 = jnp.float32
BF16 = jnp.bfloat16
NN, NT, TN = ((1,), (0,)), ((1,), (1,)), ((0,), (0,))
SMEM = pl.BlockSpec(memory_space=pltpu.SMEM)
VMEM = pl.BlockSpec(memory_space=pltpu.VMEM)
HBM = pl.BlockSpec(memory_space=pltpu.HBM)
PARAMS = pltpu.CompilerParams(vmem_limit_bytes=20 * 2**20)


def dot(a, b, dims):
    return lax.dot_general(a, b, (dims, ((), ())), preferred_element_type=F32)


def in_vmem(value):
    return pltpu.with_memory_space_constraint(value, pltpu.VMEM)


def in_hbm(value):
    return pltpu.with_memory_space_constraint(value, pltpu.HBM)


def cost(flops, size):
    return pl.CostEstimate(flops=flops, bytes_accessed=size, transcendentals=0)


def within_block(q_ref, k_ref, v_ref, h, causal, shift=0):
    cols, query_cols = slice(h * DH, (h + 1) * DH), slice((h - shift) * DH, (h - shift + 1) * DH)
    q0, q1 = q_ref[:HALF, query_cols], q_ref[HALF:, query_cols]
    k0, k1 = k_ref[:HALF, cols], k_ref[HALF:, cols]
    v0, v1 = v_ref[:HALF, cols], v_ref[HALF:, cols]
    s00 = jnp.where(causal, dot(q0, k0, NT), 0.0).astype(BF16)
    s10 = dot(q1, k0, NT).astype(BF16)
    s11 = jnp.where(causal, dot(q1, k1, NT), 0.0).astype(BF16)
    return dot(s00, v0, NN), dot(s10, v0, NN) + dot(s11, v1, NN)


def causal_mask():
    row = lax.broadcasted_iota(jnp.int32, (HALF, HALF), 0)
    col = lax.broadcasted_iota(jnp.int32, (HALF, HALF), 1)
    return col <= row


def finish(queries, within, state, gain):
    att = within + dot(queries, state, NN)
    mean = jnp.full((DH, DH), 1.0 / DH, BF16)
    mean_square = dot((att * att).astype(BF16), mean, NN)
    return (att * lax.rsqrt(mean_square + 1e-6) * gain).astype(BF16)


def state_kernel(q_hbm, k_hbm, v_hbm, gain_ref, out_ref, early_ref, q_ref, k_ref, v_ref, sems):
    early = slice(LATE * DH, HEADS * DH)
    late = slice(0, LATE * DH)
    copies = [
        pltpu.make_async_copy(hbm.at[:, cols], ref.at[:, cols], sems.at[at])
        for at, (hbm, ref, cols) in enumerate(
            (
                (k_hbm, k_ref, early),
                (v_hbm, v_ref, early),
                (k_hbm, k_ref, late),
                (v_hbm, v_ref, late),
            )
        )
    ]
    copies.append(pltpu.make_async_copy(q_hbm.at[:, early], q_ref, sems.at[4]))
    for copy in copies:
        copy.start()
    gain = gain_ref[:, early]
    high = gain.astype(BF16)
    rest = gain - high.astype(F32)
    middle = rest.astype(BF16)
    low = (rest - middle.astype(F32)).astype(BF16)
    blank = jnp.zeros((GAIN_ROWS - 3, EARLY * DH), BF16)
    early_ref[BLK:, : EARLY * DH] = jnp.concatenate([high, middle, low, blank])
    early_ref[BLK:, EARLY * DH :] = jnp.zeros((GAIN_ROWS, EARLY * DH), BF16)
    causal = causal_mask()

    def state(h):
        cols = slice(h * DH, (h + 1) * DH)
        out_ref[cols, :] = dot(k_ref[:, cols], v_ref[:, cols], TN).astype(BF16)

    copies[0].wait()
    copies[1].wait()
    for h in range(LATE, HEADS):
        state(h)
    copies[4].wait()
    early_ref[:BLK, : EARLY * DH] = q_ref[...]
    for h in range(LATE, HEADS):
        top, bottom = within_block(q_ref, k_ref, v_ref, h, causal, LATE)
        cols = slice((EARLY + h - LATE) * DH, (EARLY + h - LATE + 1) * DH)
        early_ref[:HALF, cols] = top.astype(BF16)
        early_ref[HALF:BLK, cols] = bottom.astype(BF16)
    copies[2].wait()
    copies[3].wait()
    for h in range(LATE):
        state(h)


def block_states(q, k, v, gain):
    width = k.shape[1]
    return pl.pallas_call(
        state_kernel,
        name="block_states",
        in_specs=[HBM, HBM, HBM, VMEM],
        out_specs=[VMEM, VMEM],
        out_shape=[
            pltpu.VMEM((width, DH), BF16),
            jax.ShapeDtypeStruct((BLK + GAIN_ROWS, 2 * EARLY * DH), BF16),
        ],
        scratch_shapes=[
            pltpu.VMEM((BLK, EARLY * DH), BF16),
            pltpu.VMEM(k.shape, BF16),
            pltpu.VMEM(v.shape, BF16),
            pltpu.SemaphoreType.DMA((5,)),
        ],
        compiler_params=PARAMS,
        cost_estimate=cost(2 * BLK * DH * width, 2 * BLK * width * 2),
    )(in_hbm(q), in_hbm(k), in_hbm(v), gain)


def scan_kernel(core_ref, own_ref, other_ref, out_ref, *, chips):
    rows = own_ref.shape[0] // chips
    second = (core_ref[0] == 1).astype(F32)
    before = jnp.zeros((rows, DH), F32)
    for chip in range(chips):
        at = slice(chip * rows, (chip + 1) * rows)
        other = other_ref[at, :].astype(F32)
        out_ref[at, :] = (before + second * other).astype(BF16)
        before = before + (own_ref[at, :].astype(F32) + other)


def exclusive_sums(core, own, other, chips):
    return pl.pallas_call(
        functools.partial(scan_kernel, chips=chips),
        name="exclusive_sums",
        in_specs=[SMEM, VMEM, VMEM],
        out_specs=VMEM,
        out_shape=pltpu.VMEM(own.shape, BF16),
        compiler_params=PARAMS,
        cost_estimate=cost(own.size * 4, own.size * 6),
    )(core, own, other)


def attention_kernel(q_ref, k_ref, v_ref, carried_ref, gain_ref, *out_refs, groups, states):
    causal = causal_mask()
    for out_ref, (first, last) in zip(out_refs, groups):
        for h in range(first, last):
            cols = slice(h * DH, (h + 1) * DH)
            out_cols = slice((h - first) * DH, (h - first + 1) * DH)
            parts = within_block(q_ref, k_ref, v_ref, h, causal)
            for rows, within in zip((slice(0, HALF), slice(HALF, BLK)), parts):
                out_ref[rows, out_cols] = finish(
                    q_ref[rows, cols], within, carried_ref[cols, :], gain_ref[:, cols]
                )
    if states:
        out_refs[0][BLK:, :] = carried_ref[LATE * DH :, :]


def attention(q, k, v, carried, gain, groups, states=False):
    heads = sum(last - first for first, last in groups)
    shapes = [(BLK, (last - first) * DH) for first, last in groups]
    if states:
        shapes[0] = (BLK + EARLY * DH, DH)
    return pl.pallas_call(
        functools.partial(attention_kernel, groups=groups, states=states),
        name="attention",
        in_specs=[VMEM] * 5,
        out_specs=[VMEM] * len(shapes),
        out_shape=[pltpu.VMEM(shape, BF16) for shape in shapes],
        compiler_params=PARAMS,
        cost_estimate=cost(4 * BLK * BLK * DH * heads, BLK * DH * heads * 8),
    )(q, k, v, carried, gain)


TILE = 256


def mix_kernel(column_ref, *refs, plan, first, early):
    count = len(plan)
    a_refs, rest = refs[:count], refs[count:]
    if early:
        g_hbm, rest = rest[0], rest[1:]
    w_hbm, rest = rest[0], rest[1:]
    if not first:
        total_ref, rest = rest[0], rest[1:]
    out_ref, w_ref, sems, rest = rest[0], rest[1], rest[2], rest[3:]
    if early:
        g_ref, normed_ref, g_sems = rest
    ways = w_hbm.shape[0] // (HEADS * DH)
    copies, g_copies, at = [], [], 0
    for piece, (shift, head, heads) in enumerate(plan):
        depth = heads * DH
        source = lax.rem(column_ref[0] + (shift + ways), ways)
        start = pl.multiple_of(source * (HEADS * DH) + head * DH, DH)
        copies.append(
            pltpu.make_async_copy(
                w_hbm.at[pl.ds(start, depth)], w_ref.at[at : at + depth], sems.at[piece]
            )
        )
        at += depth
        if early:
            height = BLK + GAIN_ROWS
            g_rows = pl.ds(pl.multiple_of(source * height, GAIN_ROWS), height)
            g_copies.append(
                pltpu.make_async_copy(g_hbm.at[g_rows], g_ref.at[piece], g_sems.at[piece])
            )
    for copy in g_copies + copies:
        copy.start()
    if early:
        for piece, a_ref in enumerate(a_refs):
            g_copies[piece].wait()
            for h in range(EARLY):
                cols = slice(h * DH, (h + 1) * DH)
                terms = g_ref[piece, BLK:, cols].astype(F32)
                gain = terms[0:1] + terms[1:2] + terms[2:3]
                within = g_ref[piece, :BLK, (EARLY + h) * DH : (EARLY + h + 1) * DH]
                state = a_ref[BLK + h * DH : BLK + (h + 1) * DH, :]
                normed_ref[piece, :, cols] = finish(
                    g_ref[piece, :BLK, cols], within.astype(F32), state, gain
                )
    for copy in copies:
        copy.wait()
    for tile in range(out_ref.shape[1] // TILE):
        cols = slice(tile * TILE, (tile + 1) * TILE)
        total, at = None if first else total_ref[:, cols], 0
        for piece, (a_ref, (_, _, heads)) in enumerate(zip(a_refs, plan)):
            depth = heads * DH
            rows = normed_ref[piece] if early else a_ref[:BLK, :]
            term = dot(rows, w_ref[at : at + depth, cols], NN)
            total = term if total is None else total + term
            at += depth
        out_ref[:, cols] = total


def mix(column, w, plan, arrays, total=None, gathered=None):
    width, early = w.shape[1], gathered is not None
    operands = [column, *arrays]
    specs = [SMEM] + [VMEM] * len(arrays)
    for value in ([gathered] if early else []) + [w]:
        operands.append(value)
        specs.append(HBM)
    if total is not None:
        operands.append(total)
        specs.append(VMEM)
    depth = sum(heads for _, _, heads in plan) * DH
    scratch = [
        pltpu.VMEM((depth, width), BF16),
        pltpu.SemaphoreType.DMA((len(arrays),)),
    ]
    if early:
        scratch += [
            pltpu.VMEM((len(arrays), BLK + GAIN_ROWS, 2 * EARLY * DH), BF16),
            pltpu.VMEM((len(arrays), BLK, EARLY * DH), BF16),
            pltpu.SemaphoreType.DMA((len(arrays),)),
        ]
    return pl.pallas_call(
        functools.partial(mix_kernel, plan=tuple(plan), first=total is None, early=early),
        name="mix_early" if early else "mix",
        in_specs=specs,
        out_specs=VMEM,
        out_shape=pltpu.VMEM((BLK, width), F32),
        scratch_shapes=scratch,
        compiler_params=PARAMS,
        cost_estimate=cost(2 * BLK * depth * width, 2 * depth * width),
    )(*operands)


def last_kernel(*refs):
    *a_refs, w_ref, total_ref, out_hbm, out_ref, sems = refs
    copies = []
    for tile in range(w_ref.shape[1] // TILE):
        cols = slice(tile * TILE, (tile + 1) * TILE)
        total, at = total_ref[:, cols], 0
        for a_ref in a_refs:
            depth = a_ref.shape[1]
            total = total + dot(a_ref[...], w_ref[at : at + depth, cols], NN)
            at += depth
        out_ref[:, cols] = total.astype(BF16)
        copy = pltpu.make_async_copy(out_ref.at[:, cols], out_hbm.at[:, cols], sems.at[tile])
        copy.start()
        copies.append(copy)
    for copy in copies:
        copy.wait()


def last_mix(arrays, w, total):
    depth, width = w.shape
    return pl.pallas_call(
        last_kernel,
        name="last_mix",
        in_specs=[VMEM] * (len(arrays) + 2),
        out_specs=HBM,
        out_shape=jax.ShapeDtypeStruct((BLK, width), BF16),
        scratch_shapes=[
            pltpu.VMEM((BLK, width), BF16),
            pltpu.SemaphoreType.DMA((width // TILE,)),
        ],
        compiler_params=PARAMS,
        cost_estimate=cost(2 * BLK * depth * width, BLK * width * 4),
    )(*arrays, w, total)


def along(value, shift, count):
    return lax.ppermute(value, "fsdp", [(i, (i + shift) % count) for i in range(count)])


def shards(q, k, v, gain, w):
    chips, ways = lax.axis_size("chip"), lax.axis_size("fsdp")
    core = lax.axis_index("core").reshape(1)
    column = lax.axis_index("fsdp").reshape(1)
    gain_row = gain.reshape(1, -1)
    states, early = block_states(q, k, v, gain_row)
    gathered = in_hbm(lax.all_gather(early, "fsdp", axis=0, tiled=True))
    own = lax.all_to_all(states, "chip", 0, 0, tiled=True)
    other = lax.ppermute(own, "core", [(0, 1), (1, 0)])
    sums = exclusive_sums(core, own, other, chips)
    carried = lax.all_to_all(sums, "chip", 0, 0, tiled=True)
    q, k, v, weights = in_vmem(q), in_vmem(k), in_vmem(v), in_hbm(w)
    groups, mine, left, right, far = [], [], [], [], []
    for call, pair in enumerate(CALLS):
        groups += pair
        mine += attention(q, k, v, carried, gain_row, pair, call == 0)
    for at, value in enumerate(mine):
        left.append(along(value, 1, ways))
        right.append(along(value, -1, ways))
        far.append(along(right[at], -1, ways) if at % 2 else along(left[at], 1, ways))
    mine += attention(q, k, v, carried, gain_row, ((LATE, HEADS),))

    def plan(shift, groups):
        return [(shift, first, last - first) for first, last in groups]

    early_rows = ((LATE, HEADS),)
    total = mix(column, weights, plan(0, (*groups, *early_rows)), mine)
    sides = plan(-1, early_rows) + plan(1, early_rows)
    total = mix(column, weights, sides, [left[0], right[0]], total, gathered)
    for a, b in ((0, 2), (2, 4)):
        sides = plan(-1, groups[a:b]) + plan(1, groups[a:b])
        total = mix(column, weights, sides, left[a:b] + right[a:b], total)
    total = mix(column, weights, plan(2, early_rows), far[:1], total, gathered)
    total = mix(column, weights, plan(2, groups[:2]), far[:2], total)
    row = lax.rem(column[0] + ways // 2, ways) * (HEADS * DH) + groups[2][0] * DH
    depth = (groups[3][1] - groups[2][0]) * DH
    tail = in_vmem(lax.dynamic_slice_in_dim(w, row, depth))
    return last_mix(far[2:], tail, total)


def solution(mesh):
    seq, fsdp = mesh.devices.shape
    fine = Mesh(mesh.devices.reshape(seq // CORES, CORES, fsdp), ("chip", "core", "fsdp"))
    rows = ("chip", "core")
    placed = (P(rows, "fsdp"), P(rows, "fsdp"), P(rows, "fsdp"), P("fsdp"), P(None, "fsdp"))
    return jax.shard_map(
        shards, mesh=fine, in_specs=placed, out_specs=P(rows, "fsdp"), check_vma=False
    )
```

```python
import functools

import jax
import jax.numpy as jnp
from jax import lax
from jax.experimental import pallas as pl
from jax.experimental.pallas import tpu as pltpu
from jax.sharding import Mesh
from jax.sharding import PartitionSpec as P

DH = 128
BLK = 512
HALF = BLK // 2
CORES = 2
HEADS = 8
CALLS = (((0, 2), (2, 4)), ((4, 6), (6, 8)))
F32 = jnp.float32
BF16 = jnp.bfloat16
NN, NT, TN = ((1,), (0,)), ((1,), (1,)), ((0,), (0,))
SMEM = pl.BlockSpec(memory_space=pltpu.SMEM)
VMEM = pl.BlockSpec(memory_space=pltpu.VMEM)
HBM = pl.BlockSpec(memory_space=pltpu.HBM)
PARAMS = pltpu.CompilerParams(vmem_limit_bytes=20 * 2**20)


def dot(a, b, dims):
    return lax.dot_general(a, b, (dims, ((), ())), preferred_element_type=F32)


def in_vmem(value):
    return pltpu.with_memory_space_constraint(value, pltpu.VMEM)


def in_hbm(value):
    return pltpu.with_memory_space_constraint(value, pltpu.HBM)


def cost(flops, size):
    return pl.CostEstimate(flops=flops, bytes_accessed=size, transcendentals=0)


def within_block(q_ref, k_ref, v_ref, h, causal):
    cols = slice(h * DH, (h + 1) * DH)
    q0, q1 = q_ref[:HALF, cols], q_ref[HALF:, cols]
    k0, k1 = k_ref[:HALF, cols], k_ref[HALF:, cols]
    v0, v1 = v_ref[:HALF, cols], v_ref[HALF:, cols]
    s00 = jnp.where(causal, dot(q0, k0, NT), 0.0).astype(BF16)
    s10 = dot(q1, k0, NT).astype(BF16)
    s11 = jnp.where(causal, dot(q1, k1, NT), 0.0).astype(BF16)
    return dot(s00, v0, NN), dot(s10, v0, NN) + dot(s11, v1, NN)


def causal_mask():
    row = lax.broadcasted_iota(jnp.int32, (HALF, HALF), 0)
    col = lax.broadcasted_iota(jnp.int32, (HALF, HALF), 1)
    return col <= row


def finish(queries, within, state, gain):
    att = within + dot(queries, state, NN)
    mean = jnp.full((DH, DH), 1.0 / DH, BF16)
    mean_square = dot((att * att).astype(BF16), mean, NN)
    return (att * lax.rsqrt(mean_square + 1e-6) * gain).astype(BF16)


PARTS = 2


def state_kernel(k_hbm, v_hbm, out_ref, k_ref, v_ref, sems):
    width = k_ref.shape[1] // PARTS
    copies = []
    for part in range(PARTS):
        cols = slice(part * width, (part + 1) * width)
        for at, (hbm, ref) in enumerate(((k_hbm, k_ref), (v_hbm, v_ref))):
            copy = pltpu.make_async_copy(hbm.at[:, cols], ref.at[:, cols], sems.at[part, at])
            copy.start()
            copies.append(copy)
    for part in range(PARTS):
        copies[2 * part].wait()
        copies[2 * part + 1].wait()
        for h in range(part * width // DH, (part + 1) * width // DH):
            cols = slice(h * DH, (h + 1) * DH)
            out_ref[cols, :] = dot(k_ref[:, cols], v_ref[:, cols], TN).astype(BF16)


def block_states(k, v):
    width = k.shape[1]
    return pl.pallas_call(
        state_kernel,
        name="block_states",
        in_specs=[HBM, HBM],
        out_specs=VMEM,
        out_shape=pltpu.VMEM((width, DH), BF16),
        scratch_shapes=[
            pltpu.VMEM(k.shape, BF16),
            pltpu.VMEM(v.shape, BF16),
            pltpu.SemaphoreType.DMA((PARTS, 2)),
        ],
        compiler_params=PARAMS,
        cost_estimate=cost(2 * BLK * DH * width, 2 * BLK * width * 2),
    )(in_hbm(k), in_hbm(v))


def scan_kernel(core_ref, own_ref, other_ref, out_ref, *, chips):
    rows = own_ref.shape[0] // chips
    second = (core_ref[0] == 1).astype(F32)
    before = jnp.zeros((rows, DH), F32)
    for chip in range(chips):
        at = slice(chip * rows, (chip + 1) * rows)
        other = other_ref[at, :].astype(F32)
        out_ref[at, :] = (before + second * other).astype(BF16)
        before = before + (own_ref[at, :].astype(F32) + other)


def exclusive_sums(core, own, other, chips):
    return pl.pallas_call(
        functools.partial(scan_kernel, chips=chips),
        name="exclusive_sums",
        in_specs=[SMEM, VMEM, VMEM],
        out_specs=VMEM,
        out_shape=pltpu.VMEM(own.shape, BF16),
        compiler_params=PARAMS,
        cost_estimate=cost(own.size * 4, own.size * 6),
    )(core, own, other)


def attention_kernel(q_ref, k_ref, v_ref, carried_ref, gain_ref, *out_refs, groups):
    causal = causal_mask()
    for out_ref, (first, last) in zip(out_refs, groups):
        for h in range(first, last):
            cols = slice(h * DH, (h + 1) * DH)
            out_cols = slice((h - first) * DH, (h - first + 1) * DH)
            parts = within_block(q_ref, k_ref, v_ref, h, causal)
            for rows, within in zip((slice(0, HALF), slice(HALF, BLK)), parts):
                out_ref[rows, out_cols] = finish(
                    q_ref[rows, cols], within, carried_ref[cols, :], gain_ref[:, cols]
                )


def attention(q, k, v, carried, gain, groups):
    heads = sum(last - first for first, last in groups)
    return pl.pallas_call(
        functools.partial(attention_kernel, groups=groups),
        name="attention",
        in_specs=[VMEM] * 5,
        out_specs=[VMEM] * len(groups),
        out_shape=[pltpu.VMEM((BLK, (last - first) * DH), BF16) for first, last in groups],
        compiler_params=PARAMS,
        cost_estimate=cost(4 * BLK * BLK * DH * heads, BLK * DH * heads * 8),
    )(q, k, v, carried, gain)


TILE = 256


def mix_kernel(column_ref, *refs, plan, first):
    count = len(plan)
    a_refs, w_hbm, rest = refs[:count], refs[count], refs[count + 1 :]
    if not first:
        total_ref, rest = rest[0], rest[1:]
    out_ref, w_ref, sems = rest
    ways = w_hbm.shape[0] // (HEADS * DH)
    tiles = [slice(at, at + TILE) for at in range(0, out_ref.shape[1], TILE)]
    copies = {}
    for tile, cols in enumerate(tiles):
        at = 0
        for piece, (a_ref, (shift, head)) in enumerate(zip(a_refs, plan)):
            depth = a_ref.shape[1]
            source = lax.rem(column_ref[0] + (shift + ways), ways)
            start = pl.multiple_of(source * (HEADS * DH) + head * DH, DH)
            copy = pltpu.make_async_copy(
                w_hbm.at[pl.ds(start, depth), cols],
                w_ref.at[at : at + depth, cols],
                sems.at[tile, piece],
            )
            copy.start()
            copies[tile, piece] = copy
            at += depth
    for tile, cols in enumerate(tiles):
        total, at = None if first else total_ref[:, cols], 0
        for piece, a_ref in enumerate(a_refs):
            copies[tile, piece].wait()
            depth = a_ref.shape[1]
            term = dot(a_ref[...], w_ref[at : at + depth, cols], NN)
            total = term if total is None else total + term
            at += depth
        out_ref[:, cols] = total


def mix(column, w, plan, arrays, total=None):
    width = w.shape[1]
    operands = [column, *arrays, w] + ([] if total is None else [total])
    depth = sum(a.shape[1] for a in arrays)
    specs = [SMEM] + [VMEM] * (len(operands) - 1)
    specs[1 + len(arrays)] = HBM
    return pl.pallas_call(
        functools.partial(mix_kernel, plan=tuple(plan), first=total is None),
        name="mix",
        in_specs=specs,
        out_specs=VMEM,
        out_shape=pltpu.VMEM((BLK, width), F32),
        scratch_shapes=[
            pltpu.VMEM((depth, width), BF16),
            pltpu.SemaphoreType.DMA((width // TILE, len(arrays))),
        ],
        compiler_params=PARAMS,
        cost_estimate=cost(2 * BLK * depth * width, 2 * depth * width),
    )(*operands)


def last_kernel(*refs):
    *a_refs, w_ref, total_ref, out_hbm, out_ref, sems = refs
    copies = []
    for tile in range(w_ref.shape[1] // TILE):
        cols = slice(tile * TILE, (tile + 1) * TILE)
        total, at = total_ref[:, cols], 0
        for a_ref in a_refs:
            depth = a_ref.shape[1]
            total = total + dot(a_ref[...], w_ref[at : at + depth, cols], NN)
            at += depth
        out_ref[:, cols] = total.astype(BF16)
        copy = pltpu.make_async_copy(out_ref.at[:, cols], out_hbm.at[:, cols], sems.at[tile])
        copy.start()
        copies.append(copy)
    for copy in copies:
        copy.wait()


def last_mix(arrays, w, total):
    depth, width = w.shape
    return pl.pallas_call(
        last_kernel,
        name="last_mix",
        in_specs=[VMEM] * (len(arrays) + 2),
        out_specs=HBM,
        out_shape=jax.ShapeDtypeStruct((BLK, width), BF16),
        scratch_shapes=[
            pltpu.VMEM((BLK, width), BF16),
            pltpu.SemaphoreType.DMA((width // TILE,)),
        ],
        compiler_params=PARAMS,
        cost_estimate=cost(2 * BLK * depth * width, BLK * width * 4),
    )(*arrays, w, total)


def along(value, shift, count):
    return lax.ppermute(value, "fsdp", [(i, (i + shift) % count) for i in range(count)])


def shards(q, k, v, gain, w):
    chips, ways = lax.axis_size("chip"), lax.axis_size("fsdp")
    core = lax.axis_index("core").reshape(1)
    column = lax.axis_index("fsdp").reshape(1)
    states = block_states(k, v)
    own = lax.all_to_all(states, "chip", 0, 0, tiled=True)
    other = lax.ppermute(own, "core", [(0, 1), (1, 0)])
    sums = exclusive_sums(core, own, other, chips)
    carried = lax.all_to_all(sums, "chip", 0, 0, tiled=True)
    q, k, v, weights = in_vmem(q), in_vmem(k), in_vmem(v), in_hbm(w)
    gain_row = gain.reshape(1, -1)
    heads, mine, left, right, far = [], [], [], [], []
    for groups in CALLS:
        heads += [first for first, _ in groups]
        mine += attention(q, k, v, carried, gain_row, groups)
    for value in mine:
        left.append(along(value, 1, ways))
        right.append(along(value, -1, ways))

    def plan(shift, begin, end):
        return [(shift, head) for head in heads[begin:end]]

    total = mix(column, weights, plan(0, 0, 4), mine)
    left[0], right[1], total = lax.optimization_barrier((left[0], right[1], total))
    for at in range(4):
        far.append(along(right[at], -1, ways) if at % 2 else along(left[at], 1, ways))
    for a, b in ((0, 2), (2, 4)):
        sides = plan(-1, a, b) + plan(1, a, b)
        total = mix(column, weights, sides, left[a:b] + right[a:b], total)
    total = mix(column, weights, plan(2, 0, 2), far[:2], total)
    row = lax.rem(column[0] + ways // 2, ways) * (HEADS * DH) + heads[2] * DH
    tail = in_vmem(lax.dynamic_slice_in_dim(w, row, (HEADS - heads[2]) * DH))
    return last_mix(far[2:], tail, total)


def solution(mesh):
    seq, fsdp = mesh.devices.shape
    fine = Mesh(mesh.devices.reshape(seq // CORES, CORES, fsdp), ("chip", "core", "fsdp"))
    rows = ("chip", "core")
    placed = (P(rows, "fsdp"), P(rows, "fsdp"), P(rows, "fsdp"), P("fsdp"), P(None, "fsdp"))
    return jax.shard_map(
        shards, mesh=fine, in_specs=placed, out_specs=P(rows, "fsdp"), check_vma=False
    )
```

```python
import functools

import jax
import jax.numpy as jnp
from jax import lax
from jax.experimental import pallas as pl
from jax.experimental.pallas import tpu as pltpu
from jax.sharding import Mesh
from jax.sharding import PartitionSpec as P

DH = 128
BLK = 512
HALF = BLK // 2
CORES = 2
HEADS = 8
CALLS = (((0, 4),), ((4, 8),))
F32 = jnp.float32
BF16 = jnp.bfloat16
NN, NT, TN = ((1,), (0,)), ((1,), (1,)), ((0,), (0,))
SMEM = pl.BlockSpec(memory_space=pltpu.SMEM)
VMEM = pl.BlockSpec(memory_space=pltpu.VMEM)
HBM = pl.BlockSpec(memory_space=pltpu.HBM)
PARAMS = pltpu.CompilerParams(vmem_limit_bytes=20 * 2**20)


def dot(a, b, dims):
    return lax.dot_general(a, b, (dims, ((), ())), preferred_element_type=F32)


def in_vmem(value):
    return pltpu.with_memory_space_constraint(value, pltpu.VMEM)


def in_hbm(value):
    return pltpu.with_memory_space_constraint(value, pltpu.HBM)


def cost(flops, size):
    return pl.CostEstimate(flops=flops, bytes_accessed=size, transcendentals=0)


def within_block(q_ref, k_ref, v_ref, h, causal):
    cols = slice(h * DH, (h + 1) * DH)
    q0, q1 = q_ref[:HALF, cols], q_ref[HALF:, cols]
    k0, k1 = k_ref[:HALF, cols], k_ref[HALF:, cols]
    v0, v1 = v_ref[:HALF, cols], v_ref[HALF:, cols]
    s00 = jnp.where(causal, dot(q0, k0, NT), 0.0).astype(BF16)
    s10 = dot(q1, k0, NT).astype(BF16)
    s11 = jnp.where(causal, dot(q1, k1, NT), 0.0).astype(BF16)
    return dot(s00, v0, NN), dot(s10, v0, NN) + dot(s11, v1, NN)


def causal_mask():
    row = lax.broadcasted_iota(jnp.int32, (HALF, HALF), 0)
    col = lax.broadcasted_iota(jnp.int32, (HALF, HALF), 1)
    return col <= row


def finish(queries, within, state, gain):
    att = within + dot(queries, state, NN)
    mean = jnp.full((DH, DH), 1.0 / DH, BF16)
    mean_square = dot((att * att).astype(BF16), mean, NN)
    return (att * lax.rsqrt(mean_square + 1e-6) * gain).astype(BF16)


PARTS = 2


def state_kernel(k_hbm, v_hbm, out_ref, k_ref, v_ref, sems):
    width = k_ref.shape[1] // PARTS
    copies = []
    for part in range(PARTS):
        cols = slice(part * width, (part + 1) * width)
        for at, (hbm, ref) in enumerate(((k_hbm, k_ref), (v_hbm, v_ref))):
            copy = pltpu.make_async_copy(hbm.at[:, cols], ref.at[:, cols], sems.at[part, at])
            copy.start()
            copies.append(copy)
    for part in range(PARTS):
        copies[2 * part].wait()
        copies[2 * part + 1].wait()
        for h in range(part * width // DH, (part + 1) * width // DH):
            cols = slice(h * DH, (h + 1) * DH)
            out_ref[cols, :] = dot(k_ref[:, cols], v_ref[:, cols], TN).astype(BF16)


def block_states(k, v):
    width = k.shape[1]
    return pl.pallas_call(
        state_kernel,
        name="block_states",
        in_specs=[HBM, HBM],
        out_specs=VMEM,
        out_shape=pltpu.VMEM((width, DH), BF16),
        scratch_shapes=[
            pltpu.VMEM(k.shape, BF16),
            pltpu.VMEM(v.shape, BF16),
            pltpu.SemaphoreType.DMA((PARTS, 2)),
        ],
        compiler_params=PARAMS,
        cost_estimate=cost(2 * BLK * DH * width, 2 * BLK * width * 2),
    )(in_hbm(k), in_hbm(v))


def scan_kernel(core_ref, own_ref, other_ref, out_ref, *, chips):
    rows = own_ref.shape[0] // chips
    second = (core_ref[0] == 1).astype(F32)
    before = jnp.zeros((rows, DH), F32)
    for chip in range(chips):
        at = slice(chip * rows, (chip + 1) * rows)
        other = other_ref[at, :].astype(F32)
        out_ref[at, :] = (before + second * other).astype(BF16)
        before = before + (own_ref[at, :].astype(F32) + other)


def exclusive_sums(core, own, other, chips):
    return pl.pallas_call(
        functools.partial(scan_kernel, chips=chips),
        name="exclusive_sums",
        in_specs=[SMEM, VMEM, VMEM],
        out_specs=VMEM,
        out_shape=pltpu.VMEM(own.shape, BF16),
        compiler_params=PARAMS,
        cost_estimate=cost(own.size * 4, own.size * 6),
    )(core, own, other)


def attention_kernel(q_ref, k_ref, v_ref, carried_ref, gain_ref, *out_refs, groups):
    causal = causal_mask()
    for out_ref, (first, last) in zip(out_refs, groups):
        for h in range(first, last):
            cols = slice(h * DH, (h + 1) * DH)
            out_cols = slice((h - first) * DH, (h - first + 1) * DH)
            parts = within_block(q_ref, k_ref, v_ref, h, causal)
            for rows, within in zip((slice(0, HALF), slice(HALF, BLK)), parts):
                out_ref[rows, out_cols] = finish(
                    q_ref[rows, cols], within, carried_ref[cols, :], gain_ref[:, cols]
                )


def attention(q, k, v, carried, gain, groups):
    heads = sum(last - first for first, last in groups)
    return pl.pallas_call(
        functools.partial(attention_kernel, groups=groups),
        name="attention",
        in_specs=[VMEM] * 5,
        out_specs=[VMEM] * len(groups),
        out_shape=[pltpu.VMEM((BLK, (last - first) * DH), BF16) for first, last in groups],
        compiler_params=PARAMS,
        cost_estimate=cost(4 * BLK * BLK * DH * heads, BLK * DH * heads * 8),
    )(q, k, v, carried, gain)


TILE = 256


def own_kernel(column_ref, *refs):
    *a_refs, w_hbm, total_ref, w_ref, sems = refs
    depth = HEADS * DH
    ways = w_hbm.shape[0] // depth
    copies, starts = [], []
    for shift in range(ways):
        start = pl.multiple_of(lax.rem(column_ref[0] + shift, ways) * depth, depth)
        rows = pl.ds(start, depth)
        copies.append(pltpu.make_async_copy(w_hbm.at[rows], w_ref.at[rows], sems.at[shift]))
        copies[-1].start()
        starts.append(start)
    copies[0].wait()
    for tile in range(total_ref.shape[1] // TILE):
        cols = slice(tile * TILE, (tile + 1) * TILE)
        total, at = None, 0
        for a_ref in a_refs:
            width = a_ref.shape[1]
            rows = pl.ds(pl.multiple_of(starts[0] + at, DH), width)
            term = dot(a_ref[...], w_ref[rows, cols], NN)
            total = term if total is None else total + term
            at += width
        total_ref[:, cols] = total
    for copy in copies[1:]:
        copy.wait()


def own_mix(column, w, arrays):
    width, ways = w.shape[1], w.shape[0] // (HEADS * DH)
    return pl.pallas_call(
        own_kernel,
        name="own_mix",
        in_specs=[SMEM] + [VMEM] * len(arrays) + [HBM],
        out_specs=[VMEM, VMEM],
        out_shape=[pltpu.VMEM((BLK, width), F32), pltpu.VMEM(w.shape, BF16)],
        scratch_shapes=[pltpu.SemaphoreType.DMA((ways,))],
        compiler_params=PARAMS,
        cost_estimate=cost(2 * BLK * HEADS * DH * width, 2 * w.size),
    )(column, *arrays, in_hbm(w))


def mix_kernel(column_ref, *refs, plan, first, last):
    count = len(plan)
    a_refs, w_ref, rest = refs[:count], refs[count], refs[count + 1 :]
    if not first:
        total_ref, rest = rest[0], rest[1:]
    if last:
        out_hbm, out_ref, sems = rest
    else:
        (out_ref,) = rest
    ways = w_ref.shape[0] // (HEADS * DH)
    copies = []
    for tile in range(out_ref.shape[1] // TILE):
        cols = slice(tile * TILE, (tile + 1) * TILE)
        total = None if first else total_ref[:, cols]
        for a_ref, (shift, head) in zip(a_refs, plan):
            source = lax.rem(column_ref[0] + (shift + ways), ways)
            start = pl.multiple_of(source * (HEADS * DH) + head * DH, DH)
            term = dot(a_ref[...], w_ref[pl.ds(start, a_ref.shape[1]), cols], NN)
            total = term if total is None else total + term
        out_ref[:, cols] = total.astype(out_ref.dtype)
        if last:
            copy = pltpu.make_async_copy(out_ref.at[:, cols], out_hbm.at[:, cols], sems.at[tile])
            copy.start()
            copies.append(copy)
    for copy in copies:
        copy.wait()


def mix(column, w, plan, arrays, total=None, last=False):
    width = w.shape[1]
    operands = [column, *arrays, w] + ([] if total is None else [total])
    depth = sum(a.shape[1] for a in arrays)
    if last:
        out_shape = jax.ShapeDtypeStruct((BLK, width), BF16)
        scratch = [pltpu.VMEM((BLK, width), BF16), pltpu.SemaphoreType.DMA((width // TILE,))]
    else:
        out_shape, scratch = pltpu.VMEM((BLK, width), F32), []
    return pl.pallas_call(
        functools.partial(mix_kernel, plan=tuple(plan), first=total is None, last=last),
        name="mix",
        in_specs=[SMEM] + [VMEM] * (len(operands) - 1),
        out_specs=HBM if last else VMEM,
        out_shape=out_shape,
        scratch_shapes=scratch,
        compiler_params=PARAMS,
        cost_estimate=cost(2 * BLK * depth * width, 2 * depth * width),
    )(*operands)


def along(value, shift, count):
    return lax.ppermute(value, "fsdp", [(i, (i + shift) % count) for i in range(count)])


def shards(q, k, v, gain, w):
    chips, ways = lax.axis_size("chip"), lax.axis_size("fsdp")
    core = lax.axis_index("core").reshape(1)
    column = lax.axis_index("fsdp").reshape(1)
    states = block_states(k, v)
    own = lax.all_to_all(states, "chip", 0, 0, tiled=True)
    other = lax.ppermute(own, "core", [(0, 1), (1, 0)])
    sums = exclusive_sums(core, own, other, chips)
    carried = lax.all_to_all(sums, "chip", 0, 0, tiled=True)
    q, k, v = in_vmem(q), in_vmem(k), in_vmem(v)
    gain_row = gain.reshape(1, -1)
    heads, mine, left, right, far = [], [], [], [], []
    for groups in CALLS:
        heads += [first for first, _ in groups]
        mine += attention(q, k, v, carried, gain_row, groups)
    for at, value in enumerate(mine):
        sides = along(value, 1, ways), along(value, -1, ways)
        sides = lax.optimization_barrier(sides)
        left.append(sides[0])
        right.append(sides[1])
        far.append(along(sides[1], -1, ways) if at % 2 else along(sides[0], 1, ways))

    def plan(shift, begin, end):
        return [(shift, head) for head in heads[begin:end]]

    total, w = own_mix(column, w, mine)
    for at in range(2):
        sides = plan(-1, at, at + 1) + plan(1, at, at + 1)
        total = mix(column, w, sides, [left[at], right[at]], total)
    total = mix(column, w, plan(2, 0, 1), far[:1], total)
    return mix(column, w, plan(2, 1, 2), far[1:], total, True)


def solution(mesh):
    seq, fsdp = mesh.devices.shape
    fine = Mesh(mesh.devices.reshape(seq // CORES, CORES, fsdp), ("chip", "core", "fsdp"))
    rows = ("chip", "core")
    placed = (P(rows, "fsdp"), P(rows, "fsdp"), P(rows, "fsdp"), P("fsdp"), P(None, "fsdp"))
    return jax.shard_map(
        shards, mesh=fine, in_specs=placed, out_specs=P(rows, "fsdp"), check_vma=False
    )
```

```python
import functools

import jax
import jax.numpy as jnp
from jax import lax
from jax.experimental import pallas as pl
from jax.experimental.pallas import tpu as pltpu
from jax.sharding import Mesh
from jax.sharding import PartitionSpec as P

DH = 128
BLK = 512
HALF = BLK // 2
CORES = 2
HEADS = 8
LATE = 6
EARLY = HEADS - LATE
GAIN_ROWS = 16
CALLS = ((0, 3), (3, 6))
F32 = jnp.float32
BF16 = jnp.bfloat16
NN, NT, TN = ((1,), (0,)), ((1,), (1,)), ((0,), (0,))
SMEM = pl.BlockSpec(memory_space=pltpu.SMEM)
VMEM = pl.BlockSpec(memory_space=pltpu.VMEM)
HBM = pl.BlockSpec(memory_space=pltpu.HBM)
PARAMS = pltpu.CompilerParams(vmem_limit_bytes=20 * 2**20)


def dot(a, b, dims):
    return lax.dot_general(a, b, (dims, ((), ())), preferred_element_type=F32)


def in_vmem(value):
    return pltpu.with_memory_space_constraint(value, pltpu.VMEM)


def in_hbm(value):
    return pltpu.with_memory_space_constraint(value, pltpu.HBM)


def cost(flops, size):
    return pl.CostEstimate(flops=flops, bytes_accessed=size, transcendentals=0)


def within_block(q_ref, k_ref, v_ref, h, causal, shift=0):
    cols, query_cols = slice(h * DH, (h + 1) * DH), slice((h - shift) * DH, (h - shift + 1) * DH)
    q0, q1 = q_ref[:HALF, query_cols], q_ref[HALF:, query_cols]
    k0, k1 = k_ref[:HALF, cols], k_ref[HALF:, cols]
    v0, v1 = v_ref[:HALF, cols], v_ref[HALF:, cols]
    s00 = jnp.where(causal, dot(q0, k0, NT), 0.0).astype(BF16)
    s10 = dot(q1, k0, NT).astype(BF16)
    s11 = jnp.where(causal, dot(q1, k1, NT), 0.0).astype(BF16)
    return dot(s00, v0, NN), dot(s10, v0, NN) + dot(s11, v1, NN)


def causal_mask():
    row = lax.broadcasted_iota(jnp.int32, (HALF, HALF), 0)
    col = lax.broadcasted_iota(jnp.int32, (HALF, HALF), 1)
    return col <= row


def finish(queries, within, state, gain):
    att = within + dot(queries, state, NN)
    mean = jnp.full((DH, DH), 1.0 / DH, BF16)
    mean_square = dot((att * att).astype(BF16), mean, NN)
    return (att * lax.rsqrt(mean_square + 1e-6) * gain).astype(BF16)


def state_kernel(q_hbm, k_hbm, v_hbm, gain_ref, out_ref, early_hbm, q_ref, k_ref, v_ref, early_ref, sems):
    early = slice(LATE * DH, HEADS * DH)
    late = slice(0, LATE * DH)
    copies = [
        pltpu.make_async_copy(hbm.at[:, cols], ref.at[:, cols], sems.at[at])
        for at, (hbm, ref, cols) in enumerate(
            (
                (k_hbm, k_ref, early),
                (v_hbm, v_ref, early),
                (k_hbm, k_ref, late),
                (v_hbm, v_ref, late),
            )
        )
    ]
    copies.append(pltpu.make_async_copy(q_hbm.at[:, early], q_ref, sems.at[4]))
    for at in (4, 0, 1, 2, 3):
        copies[at].start()
    gain = gain_ref[:, early]
    high = gain.astype(BF16)
    rest = gain - high.astype(F32)
    middle = rest.astype(BF16)
    low = (rest - middle.astype(F32)).astype(BF16)
    blank = jnp.zeros((GAIN_ROWS - 3, EARLY * DH), BF16)
    early_ref[BLK:, : EARLY * DH] = jnp.concatenate([high, middle, low, blank])
    early_ref[BLK:, EARLY * DH :] = jnp.zeros((GAIN_ROWS, EARLY * DH), BF16)
    causal = causal_mask()

    def state(h):
        cols = slice(h * DH, (h + 1) * DH)
        out_ref[cols, :] = dot(k_ref[:, cols], v_ref[:, cols], TN).astype(BF16)

    copies[4].wait()
    early_ref[:BLK, : EARLY * DH] = q_ref[...]
    copies[0].wait()
    copies[1].wait()
    for h in range(LATE, HEADS):
        top, bottom = within_block(q_ref, k_ref, v_ref, h, causal, LATE)
        cols = slice((EARLY + h - LATE) * DH, (EARLY + h - LATE + 1) * DH)
        early_ref[:HALF, cols] = top.astype(BF16)
        early_ref[HALF:BLK, cols] = bottom.astype(BF16)
    out = pltpu.make_async_copy(early_ref, early_hbm, sems.at[5])
    out.start()
    for h in range(LATE, HEADS):
        state(h)
    copies[2].wait()
    copies[3].wait()
    for h in range(LATE):
        state(h)
    out.wait()


def block_states(q, k, v, gain):
    width = k.shape[1]
    early = (BLK + GAIN_ROWS, 2 * EARLY * DH)
    return pl.pallas_call(
        state_kernel,
        name="block_states",
        in_specs=[HBM, HBM, HBM, VMEM],
        out_specs=[VMEM, HBM],
        out_shape=[pltpu.VMEM((width, DH), BF16), pltpu.HBM(early, BF16)],
        scratch_shapes=[
            pltpu.VMEM((BLK, EARLY * DH), BF16),
            pltpu.VMEM(k.shape, BF16),
            pltpu.VMEM(v.shape, BF16),
            pltpu.VMEM(early, BF16),
            pltpu.SemaphoreType.DMA((6,)),
        ],
        compiler_params=PARAMS,
        cost_estimate=cost(2 * BLK * DH * width, 2 * BLK * width * 2),
    )(in_hbm(q), in_hbm(k), in_hbm(v), gain)


def scan_kernel(core_ref, own_ref, other_ref, out_ref, *, chips):
    rows = own_ref.shape[0] // chips
    second = (core_ref[0] == 1).astype(F32)
    before = jnp.zeros((rows, DH), F32)
    for chip in range(chips):
        at = slice(chip * rows, (chip + 1) * rows)
        other = other_ref[at, :].astype(F32)
        out_ref[at, :] = (before + second * other).astype(BF16)
        before = before + (own_ref[at, :].astype(F32) + other)


def exclusive_sums(core, own, other, chips):
    return pl.pallas_call(
        functools.partial(scan_kernel, chips=chips),
        name="exclusive_sums",
        in_specs=[SMEM, VMEM, VMEM],
        out_specs=VMEM,
        out_shape=jax.ShapeDtypeStruct(own.shape, BF16),
        compiler_params=PARAMS,
        cost_estimate=cost(own.size * 4, own.size * 6),
    )(core, own, other)


def within_kernel(q_hbm, k_hbm, v_hbm, q_ref, out_ref, k_ref, v_ref, sems):
    copies, split = [], CALLS[0][1] * DH
    parts = (slice(0, split), slice(split, LATE * DH))
    for part, cols in enumerate(parts):
        for at, (hbm, ref) in enumerate(((q_hbm, q_ref), (k_hbm, k_ref), (v_hbm, v_ref))):
            copies.append(
                pltpu.make_async_copy(hbm.at[:, cols], ref.at[:, cols], sems.at[part, at])
            )
            copies[-1].start()
    causal = causal_mask()
    for part, (first, last) in enumerate(CALLS):
        for copy in copies[3 * part : 3 * part + 3]:
            copy.wait()
        for h in range(first, last):
            cols = slice(h * DH, (h + 1) * DH)
            top, bottom = within_block(q_ref, k_ref, v_ref, h, causal)
            out_ref[:HALF, cols] = top
            out_ref[HALF:, cols] = bottom


def within_late(q, k, v):
    shape = (BLK, LATE * DH)
    return pl.pallas_call(
        within_kernel,
        name="within_late",
        in_specs=[HBM] * 3,
        out_specs=[VMEM, VMEM],
        out_shape=[pltpu.VMEM(shape, BF16), pltpu.VMEM(shape, F32)],
        scratch_shapes=[
            pltpu.VMEM(shape, BF16),
            pltpu.VMEM(shape, BF16),
            pltpu.SemaphoreType.DMA((2, 3)),
        ],
        compiler_params=PARAMS,
        cost_estimate=cost(4 * BLK * BLK * DH * LATE, BLK * DH * LATE * 10),
    )(in_hbm(q), in_hbm(k), in_hbm(v))


def finish_kernel(q_ref, within_ref, carried_ref, gain_ref, out_ref, *, first, last):
    for h in range(first, last):
        cols = slice(h * DH, (h + 1) * DH)
        out_cols = slice((h - first) * DH, (h - first + 1) * DH)
        out_ref[:BLK, out_cols] = finish(
            q_ref[:, cols], within_ref[:, cols], carried_ref[cols, :], gain_ref[:, cols]
        )
    if out_ref.shape[0] > BLK:
        out_ref[BLK:, EARLY * DH :] = jnp.zeros((DH, out_ref.shape[1] - EARLY * DH), BF16)
        for h in range(EARLY):
            state = carried_ref[(LATE + h) * DH : (LATE + h + 1) * DH, :]
            out_ref[BLK:, h * DH : (h + 1) * DH] = state


def finish_heads(q, within, carried, gain, first, last, states=False):
    heads = last - first
    return pl.pallas_call(
        functools.partial(finish_kernel, first=first, last=last),
        name="finish_heads",
        in_specs=[VMEM] * 4,
        out_specs=VMEM,
        out_shape=jax.ShapeDtypeStruct((BLK + DH if states else BLK, heads * DH), BF16),
        compiler_params=PARAMS,
        cost_estimate=cost(4 * BLK * DH * DH * heads, BLK * DH * heads * 8),
    )(q, within, carried, gain)


def early_kernel(*refs, count):
    hbm_refs, a_refs, rest = refs[:count], refs[count : 2 * count], refs[2 * count :]
    out_refs, e_ref, sems = rest[:count], rest[count], rest[count + 1]
    copies = [
        pltpu.make_async_copy(hbm, e_ref.at[at], sems.at[at]) for at, hbm in enumerate(hbm_refs)
    ]
    for copy in copies:
        copy.start()
    for at, (a_ref, out_ref) in enumerate(zip(a_refs, out_refs)):
        copies[at].wait()
        for h in range(EARLY):
            cols = slice(h * DH, (h + 1) * DH)
            terms = e_ref[at, BLK:, cols].astype(F32)
            gain = terms[0:1] + terms[1:2] + terms[2:3]
            within = e_ref[at, :BLK, (EARLY + h) * DH : (EARLY + h + 1) * DH].astype(F32)
            out_ref[:, cols] = finish(e_ref[at, :BLK, cols], within, a_ref[BLK:, cols], gain)


def early_heads(early, chunks):
    count = len(early)
    return pl.pallas_call(
        functools.partial(early_kernel, count=count),
        name="early_heads",
        in_specs=[pl.BlockSpec(memory_space=pl.ANY)] * count + [VMEM] * count,
        out_specs=[VMEM] * count,
        out_shape=[jax.ShapeDtypeStruct((BLK, EARLY * DH), BF16)] * count,
        scratch_shapes=[
            pltpu.VMEM((count, *early[0].shape), BF16),
            pltpu.SemaphoreType.DMA((count,)),
        ],
        compiler_params=PARAMS,
        cost_estimate=cost(4 * BLK * DH * DH * EARLY * count, BLK * DH * EARLY * count * 6),
    )(*early, *chunks)


TILE = 256


def own_kernel(column_ref, *refs):
    *a_refs, w_hbm, total_ref, w_ref, sems = refs
    depth = HEADS * DH
    ways = w_hbm.shape[0] // depth
    copies, starts = [], []
    for shift in range(ways):
        start = pl.multiple_of(lax.rem(column_ref[0] + shift, ways) * depth, depth)
        rows = pl.ds(start, depth)
        copies.append(pltpu.make_async_copy(w_hbm.at[rows], w_ref.at[rows], sems.at[shift]))
        copies[-1].start()
        starts.append(start)
    copies[0].wait()
    for tile in range(total_ref.shape[1] // TILE):
        cols = slice(tile * TILE, (tile + 1) * TILE)
        total, at = None, 0
        for a_ref in a_refs:
            width = a_ref.shape[1]
            rows = pl.ds(pl.multiple_of(starts[0] + at, DH), width)
            term = dot(a_ref[:BLK, :], w_ref[rows, cols], NN)
            total = term if total is None else total + term
            at += width
        total_ref[:, cols] = total
    for copy in copies[1:]:
        copy.wait()


def own_mix(column, w, arrays):
    width, ways = w.shape[1], w.shape[0] // (HEADS * DH)
    return pl.pallas_call(
        own_kernel,
        name="own_mix",
        in_specs=[SMEM] + [VMEM] * len(arrays) + [HBM],
        out_specs=[VMEM, VMEM],
        out_shape=[pltpu.VMEM((BLK, width), F32), pltpu.VMEM(w.shape, BF16)],
        scratch_shapes=[pltpu.SemaphoreType.DMA((ways,))],
        compiler_params=PARAMS,
        cost_estimate=cost(2 * BLK * HEADS * DH * width, 2 * w.size),
    )(column, *arrays, in_hbm(w))


def mix_kernel(column_ref, *refs, plan, first, last):
    count = len(plan)
    a_refs, w_ref, rest = refs[:count], refs[count], refs[count + 1 :]
    if not first:
        total_ref, rest = rest[0], rest[1:]
    if last:
        out_hbm, out_ref, sems = rest
    else:
        (out_ref,) = rest
    ways = w_ref.shape[0] // (HEADS * DH)
    copies = []
    for tile in range(out_ref.shape[1] // TILE):
        cols = slice(tile * TILE, (tile + 1) * TILE)
        total = None if first else total_ref[:, cols]
        for a_ref, (shift, head) in zip(a_refs, plan):
            source = lax.rem(column_ref[0] + (shift + ways), ways)
            start = pl.multiple_of(source * (HEADS * DH) + head * DH, DH)
            term = dot(a_ref[:BLK, :], w_ref[pl.ds(start, a_ref.shape[1]), cols], NN)
            total = term if total is None else total + term
        out_ref[:, cols] = total.astype(out_ref.dtype)
        if last:
            copy = pltpu.make_async_copy(out_ref.at[:, cols], out_hbm.at[:, cols], sems.at[tile])
            copy.start()
            copies.append(copy)
    for copy in copies:
        copy.wait()


def mix(column, w, plan, arrays, total=None, last=False):
    width = w.shape[1]
    operands = [column, *arrays, w] + ([] if total is None else [total])
    depth = sum(a.shape[1] for a in arrays)
    if last:
        out_shape = jax.ShapeDtypeStruct((BLK, width), BF16)
        scratch = [pltpu.VMEM((BLK, width), BF16), pltpu.SemaphoreType.DMA((width // TILE,))]
    else:
        out_shape, scratch = pltpu.VMEM((BLK, width), F32), []
    return pl.pallas_call(
        functools.partial(mix_kernel, plan=tuple(plan), first=total is None, last=last),
        name="mix",
        in_specs=[SMEM] + [VMEM] * (len(operands) - 1),
        out_specs=HBM if last else VMEM,
        out_shape=out_shape,
        scratch_shapes=scratch,
        compiler_params=PARAMS,
        cost_estimate=cost(2 * BLK * depth * width, 2 * depth * width),
    )(*operands)


def along(value, shift, count):
    return lax.ppermute(value, "fsdp", [(i, (i + shift) % count) for i in range(count)])


def shards(q, k, v, gain, w):
    chips, ways = lax.axis_size("chip"), lax.axis_size("fsdp")
    core = lax.axis_index("core").reshape(1)
    column = lax.axis_index("fsdp").reshape(1)
    gain_row = gain.reshape(1, -1)
    states, early = block_states(q, k, v, gain_row)
    own = lax.all_to_all(states, "chip", 0, 0, tiled=True)
    own, *near_e = lax.optimization_barrier((own, along(early, 1, ways), along(early, -1, ways)))
    across_e = along(early, ways // 2, ways)
    other = lax.ppermute(own, "core", [(0, 1), (1, 0)])
    sums = exclusive_sums(core, own, other, chips)
    carried = lax.all_to_all(sums, "chip", 0, 0, tiled=True)
    q_late, within = within_late(q, k, v)
    carried, across_e, q_late, within = lax.optimization_barrier(
        (carried, across_e, q_late, within)
    )
    (a0, a1), (b0, b1) = CALLS
    mine_a = finish_heads(q_late, within, carried, gain_row, a0, a1, True)
    left_a, right_a = lax.optimization_barrier((along(mine_a, 1, ways), along(mine_a, -1, ways)))
    far_a = along(left_a, 1, ways)
    mine_b = finish_heads(q_late, within, carried, gain_row, b0, b1)
    mine_e, left_e, right_e = early_heads([early, *near_e], [mine_a, left_a, right_a])
    left_b, right_b, mine_e, left_e, right_e = lax.optimization_barrier(
        (along(mine_b, 1, ways), along(mine_b, -1, ways), mine_e, left_e, right_e)
    )
    far_b = along(right_b, -1, ways)
    total, w = own_mix(column, w, [mine_a, mine_b, mine_e])
    plan = [(-1, a0), (-1, LATE), (1, a0), (1, LATE)]
    total = mix(column, w, plan, [left_a, left_e, right_a, right_e], total)
    total = mix(column, w, [(-1, b0), (1, b0)], [left_b, right_b], total)
    (far_e,) = early_heads([across_e], [far_a])
    total = mix(column, w, [(2, a0), (2, LATE)], [far_a, far_e], total)
    return mix(column, w, [(2, b0)], [far_b], total, True)


def solution(mesh):
    seq, fsdp = mesh.devices.shape
    fine = Mesh(mesh.devices.reshape(seq // CORES, CORES, fsdp), ("chip", "core", "fsdp"))
    rows = ("chip", "core")
    placed = (P(rows, "fsdp"), P(rows, "fsdp"), P(rows, "fsdp"), P("fsdp"), P(None, "fsdp"))
    return jax.shard_map(
        shards, mesh=fine, in_specs=placed, out_specs=P(rows, "fsdp"), check_vma=False
    )
```

```python
import functools

import jax
import jax.numpy as jnp
from jax import lax
from jax.experimental import pallas as pl
from jax.experimental.pallas import tpu as pltpu
from jax.sharding import Mesh
from jax.sharding import PartitionSpec as P

DH = 128
BLK = 512
HALF = BLK // 2
CORES = 2
HEADS = 8
LATE = 6
EARLY = HEADS - LATE
GAIN_ROWS = 16
CALLS = ((0, 3), (3, 6))
F32 = jnp.float32
BF16 = jnp.bfloat16
NN, NT, TN = ((1,), (0,)), ((1,), (1,)), ((0,), (0,))
SMEM = pl.BlockSpec(memory_space=pltpu.SMEM)
VMEM = pl.BlockSpec(memory_space=pltpu.VMEM)
HBM = pl.BlockSpec(memory_space=pltpu.HBM)
PARAMS = pltpu.CompilerParams(vmem_limit_bytes=20 * 2**20)


def dot(a, b, dims):
    return lax.dot_general(a, b, (dims, ((), ())), preferred_element_type=F32)


def in_vmem(value):
    return pltpu.with_memory_space_constraint(value, pltpu.VMEM)


def in_hbm(value):
    return pltpu.with_memory_space_constraint(value, pltpu.HBM)


def cost(flops, size):
    return pl.CostEstimate(flops=flops, bytes_accessed=size, transcendentals=0)


def within_block(q_ref, k_ref, v_ref, h, causal, shift=0):
    cols, query_cols = slice(h * DH, (h + 1) * DH), slice((h - shift) * DH, (h - shift + 1) * DH)
    q0, q1 = q_ref[:HALF, query_cols], q_ref[HALF:, query_cols]
    k0, k1 = k_ref[:HALF, cols], k_ref[HALF:, cols]
    v0, v1 = v_ref[:HALF, cols], v_ref[HALF:, cols]
    s00 = jnp.where(causal, dot(q0, k0, NT), 0.0).astype(BF16)
    s10 = dot(q1, k0, NT).astype(BF16)
    s11 = jnp.where(causal, dot(q1, k1, NT), 0.0).astype(BF16)
    return dot(s00, v0, NN), dot(s10, v0, NN) + dot(s11, v1, NN)


def causal_mask():
    row = lax.broadcasted_iota(jnp.int32, (HALF, HALF), 0)
    col = lax.broadcasted_iota(jnp.int32, (HALF, HALF), 1)
    return col <= row


def finish(queries, within, state, gain):
    att = within + dot(queries, state, NN)
    mean = jnp.full((DH, DH), 1.0 / DH, BF16)
    mean_square = dot((att * att).astype(BF16), mean, NN)
    return (att * lax.rsqrt(mean_square + 1e-6) * gain).astype(BF16)


def state_kernel(
    q_hbm, k_hbm, v_hbm, gain_hbm, out_ref, early_hbm, q_ref, k_ref, v_ref, gain_ref, early_ref, sems
):
    early = slice(LATE * DH, HEADS * DH)
    late = slice(0, LATE * DH)
    copies = [
        pltpu.make_async_copy(hbm.at[:, cols], ref.at[:, cols], sems.at[at])
        for at, (hbm, ref, cols) in enumerate(
            (
                (k_hbm, k_ref, early),
                (v_hbm, v_ref, early),
                (k_hbm, k_ref, late),
                (v_hbm, v_ref, late),
            )
        )
    ]
    copies.append(pltpu.make_async_copy(q_hbm.at[:, early], q_ref, sems.at[4]))
    copies.append(pltpu.make_async_copy(gain_hbm, gain_ref, sems.at[5]))
    for at in (5, 4, 0, 1, 2, 3):
        copies[at].start()
    copies[5].wait()
    gain = gain_ref[:, early]
    high = gain.astype(BF16)
    rest = gain - high.astype(F32)
    middle = rest.astype(BF16)
    low = (rest - middle.astype(F32)).astype(BF16)
    blank = jnp.zeros((GAIN_ROWS - 3, EARLY * DH), BF16)
    early_ref[BLK:, : EARLY * DH] = jnp.concatenate([high, middle, low, blank])
    early_ref[BLK:, EARLY * DH :] = jnp.zeros((GAIN_ROWS, EARLY * DH), BF16)
    causal = causal_mask()

    def state(h):
        cols = slice(h * DH, (h + 1) * DH)
        out_ref[cols, :] = dot(k_ref[:, cols], v_ref[:, cols], TN).astype(BF16)

    copies[4].wait()
    early_ref[:BLK, : EARLY * DH] = q_ref[...]
    copies[0].wait()
    copies[1].wait()
    for h in range(LATE, HEADS):
        top, bottom = within_block(q_ref, k_ref, v_ref, h, causal, LATE)
        cols = slice((EARLY + h - LATE) * DH, (EARLY + h - LATE + 1) * DH)
        early_ref[:HALF, cols] = top.astype(BF16)
        early_ref[HALF:BLK, cols] = bottom.astype(BF16)
    out = pltpu.make_async_copy(early_ref, early_hbm, sems.at[6])
    out.start()
    for h in range(LATE, HEADS):
        state(h)
    copies[2].wait()
    copies[3].wait()
    for h in range(LATE):
        state(h)
    out.wait()


def block_states(q, k, v, gain):
    width = k.shape[1]
    early = (BLK + GAIN_ROWS, 2 * EARLY * DH)
    return pl.pallas_call(
        state_kernel,
        name="block_states",
        in_specs=[HBM] * 4,
        out_specs=[VMEM, HBM],
        out_shape=[pltpu.VMEM((width, DH), BF16), pltpu.HBM(early, BF16)],
        scratch_shapes=[
            pltpu.VMEM((BLK, EARLY * DH), BF16),
            pltpu.VMEM(k.shape, BF16),
            pltpu.VMEM(v.shape, BF16),
            pltpu.VMEM(gain.shape, F32),
            pltpu.VMEM(early, BF16),
            pltpu.SemaphoreType.DMA((7,)),
        ],
        compiler_params=PARAMS,
        cost_estimate=cost(2 * BLK * DH * width, 2 * BLK * width * 2),
    )(in_hbm(q), in_hbm(k), in_hbm(v), in_hbm(gain))


def scan_kernel(core_ref, own_ref, other_ref, out_ref, *, chips):
    rows = own_ref.shape[0] // chips
    second = (core_ref[0] == 1).astype(F32)
    before = jnp.zeros((rows, DH), F32)
    for chip in range(chips):
        at = slice(chip * rows, (chip + 1) * rows)
        other = other_ref[at, :].astype(F32)
        out_ref[at, :] = (before + second * other).astype(BF16)
        before = before + (own_ref[at, :].astype(F32) + other)


def exclusive_sums(core, own, other, chips):
    return pl.pallas_call(
        functools.partial(scan_kernel, chips=chips),
        name="exclusive_sums",
        in_specs=[SMEM, VMEM, VMEM],
        out_specs=VMEM,
        out_shape=jax.ShapeDtypeStruct(own.shape, BF16),
        compiler_params=PARAMS,
        cost_estimate=cost(own.size * 4, own.size * 6),
    )(core, own, other)


def within_kernel(q_hbm, k_hbm, v_hbm, q_ref, out_ref, k_ref, v_ref, sems):
    copies, split = [], CALLS[0][1] * DH
    parts = (slice(0, split), slice(split, LATE * DH))
    for part, cols in enumerate(parts):
        for at, (hbm, ref) in enumerate(((q_hbm, q_ref), (k_hbm, k_ref), (v_hbm, v_ref))):
            copies.append(
                pltpu.make_async_copy(hbm.at[:, cols], ref.at[:, cols], sems.at[part, at])
            )
            copies[-1].start()
    causal = causal_mask()
    for part, (first, last) in enumerate(CALLS):
        for copy in copies[3 * part : 3 * part + 3]:
            copy.wait()
        for h in range(first, last):
            cols = slice(h * DH, (h + 1) * DH)
            top, bottom = within_block(q_ref, k_ref, v_ref, h, causal)
            out_ref[:HALF, cols] = top
            out_ref[HALF:, cols] = bottom


def within_late(q, k, v):
    shape = (BLK, LATE * DH)
    return pl.pallas_call(
        within_kernel,
        name="within_late",
        in_specs=[HBM] * 3,
        out_specs=[VMEM, VMEM],
        out_shape=[pltpu.VMEM(shape, BF16), pltpu.VMEM(shape, F32)],
        scratch_shapes=[
            pltpu.VMEM(shape, BF16),
            pltpu.VMEM(shape, BF16),
            pltpu.SemaphoreType.DMA((2, 3)),
        ],
        compiler_params=PARAMS,
        cost_estimate=cost(4 * BLK * BLK * DH * LATE, BLK * DH * LATE * 10),
    )(in_hbm(q), in_hbm(k), in_hbm(v))


def finish_kernel(q_ref, within_ref, carried_ref, gain_ref, out_ref, *, first, last):
    for h in range(first, last):
        cols = slice(h * DH, (h + 1) * DH)
        out_cols = slice((h - first) * DH, (h - first + 1) * DH)
        out_ref[:BLK, out_cols] = finish(
            q_ref[:, cols], within_ref[:, cols], carried_ref[cols, :], gain_ref[:, cols]
        )
    if out_ref.shape[0] > BLK:
        out_ref[BLK:, EARLY * DH :] = jnp.zeros((DH, out_ref.shape[1] - EARLY * DH), BF16)
        for h in range(EARLY):
            state = carried_ref[(LATE + h) * DH : (LATE + h + 1) * DH, :]
            out_ref[BLK:, h * DH : (h + 1) * DH] = state


def finish_heads(q, within, carried, gain, first, last, states=False):
    heads = last - first
    return pl.pallas_call(
        functools.partial(finish_kernel, first=first, last=last),
        name="finish_heads",
        in_specs=[VMEM] * 4,
        out_specs=VMEM,
        out_shape=jax.ShapeDtypeStruct((BLK + DH if states else BLK, heads * DH), BF16),
        compiler_params=PARAMS,
        cost_estimate=cost(4 * BLK * DH * DH * heads, BLK * DH * heads * 8),
    )(q, within, carried, gain)


def early_kernel(*refs, count):
    hbm_refs, a_refs, rest = refs[:count], refs[count : 2 * count], refs[2 * count :]
    out_refs, e_ref, sems = rest[:count], rest[count], rest[count + 1]
    copies = [
        pltpu.make_async_copy(hbm, e_ref.at[at], sems.at[at]) for at, hbm in enumerate(hbm_refs)
    ]
    for copy in copies:
        copy.start()
    for at, (a_ref, out_ref) in enumerate(zip(a_refs, out_refs)):
        copies[at].wait()
        for h in range(EARLY):
            cols = slice(h * DH, (h + 1) * DH)
            terms = e_ref[at, BLK:, cols].astype(F32)
            gain = terms[0:1] + terms[1:2] + terms[2:3]
            within = e_ref[at, :BLK, (EARLY + h) * DH : (EARLY + h + 1) * DH].astype(F32)
            out_ref[:, cols] = finish(e_ref[at, :BLK, cols], within, a_ref[BLK:, cols], gain)


def early_heads(early, chunks):
    count = len(early)
    return pl.pallas_call(
        functools.partial(early_kernel, count=count),
        name="early_heads",
        in_specs=[pl.BlockSpec(memory_space=pl.ANY)] * count + [VMEM] * count,
        out_specs=[VMEM] * count,
        out_shape=[jax.ShapeDtypeStruct((BLK, EARLY * DH), BF16)] * count,
        scratch_shapes=[
            pltpu.VMEM((count, *early[0].shape), BF16),
            pltpu.SemaphoreType.DMA((count,)),
        ],
        compiler_params=PARAMS,
        cost_estimate=cost(4 * BLK * DH * DH * EARLY * count, BLK * DH * EARLY * count * 6),
    )(*early, *chunks)


TILE = 256


def own_kernel(column_ref, *refs):
    *a_refs, w_hbm, total_ref, w_ref, sems = refs
    depth = HEADS * DH
    ways = w_hbm.shape[0] // depth
    copies, starts = [], []
    for shift in range(ways):
        start = pl.multiple_of(lax.rem(column_ref[0] + shift, ways) * depth, depth)
        rows = pl.ds(start, depth)
        copies.append(pltpu.make_async_copy(w_hbm.at[rows], w_ref.at[rows], sems.at[shift]))
        copies[-1].start()
        starts.append(start)
    copies[0].wait()
    for tile in range(total_ref.shape[1] // TILE):
        cols = slice(tile * TILE, (tile + 1) * TILE)
        total, at = None, 0
        for a_ref in a_refs:
            width = a_ref.shape[1]
            rows = pl.ds(pl.multiple_of(starts[0] + at, DH), width)
            term = dot(a_ref[:BLK, :], w_ref[rows, cols], NN)
            total = term if total is None else total + term
            at += width
        total_ref[:, cols] = total
    for copy in copies[1:]:
        copy.wait()


def own_mix(column, w, arrays):
    width, ways = w.shape[1], w.shape[0] // (HEADS * DH)
    return pl.pallas_call(
        own_kernel,
        name="own_mix",
        in_specs=[SMEM] + [VMEM] * len(arrays) + [HBM],
        out_specs=[VMEM, VMEM],
        out_shape=[pltpu.VMEM((BLK, width), F32), pltpu.VMEM(w.shape, BF16)],
        scratch_shapes=[pltpu.SemaphoreType.DMA((ways,))],
        compiler_params=PARAMS,
        cost_estimate=cost(2 * BLK * HEADS * DH * width, 2 * w.size),
    )(column, *arrays, in_hbm(w))


def mix_kernel(column_ref, *refs, plan, first, last):
    count = len(plan)
    a_refs, w_ref, rest = refs[:count], refs[count], refs[count + 1 :]
    if not first:
        total_ref, rest = rest[0], rest[1:]
    if last:
        out_hbm, out_ref, sems = rest
    else:
        (out_ref,) = rest
    ways = w_ref.shape[0] // (HEADS * DH)
    copies = []
    for tile in range(out_ref.shape[1] // TILE):
        cols = slice(tile * TILE, (tile + 1) * TILE)
        total = None if first else total_ref[:, cols]
        for a_ref, (shift, head) in zip(a_refs, plan):
            source = lax.rem(column_ref[0] + (shift + ways), ways)
            start = pl.multiple_of(source * (HEADS * DH) + head * DH, DH)
            term = dot(a_ref[:BLK, :], w_ref[pl.ds(start, a_ref.shape[1]), cols], NN)
            total = term if total is None else total + term
        out_ref[:, cols] = total.astype(out_ref.dtype)
        if last:
            copy = pltpu.make_async_copy(out_ref.at[:, cols], out_hbm.at[:, cols], sems.at[tile])
            copy.start()
            copies.append(copy)
    for copy in copies:
        copy.wait()


def mix(column, w, plan, arrays, total=None, last=False):
    width = w.shape[1]
    operands = [column, *arrays, w] + ([] if total is None else [total])
    depth = sum(a.shape[1] for a in arrays)
    if last:
        out_shape = jax.ShapeDtypeStruct((BLK, width), BF16)
        scratch = [pltpu.VMEM((BLK, width), BF16), pltpu.SemaphoreType.DMA((width // TILE,))]
    else:
        out_shape, scratch = pltpu.VMEM((BLK, width), F32), []
    return pl.pallas_call(
        functools.partial(mix_kernel, plan=tuple(plan), first=total is None, last=last),
        name="mix",
        in_specs=[SMEM] + [VMEM] * (len(operands) - 1),
        out_specs=HBM if last else VMEM,
        out_shape=out_shape,
        scratch_shapes=scratch,
        compiler_params=PARAMS,
        cost_estimate=cost(2 * BLK * depth * width, 2 * depth * width),
    )(*operands)


def along(value, shift, count):
    return lax.ppermute(value, "fsdp", [(i, (i + shift) % count) for i in range(count)])


def shards(q, k, v, gain, w):
    chips, ways = lax.axis_size("chip"), lax.axis_size("fsdp")
    core = lax.axis_index("core").reshape(1)
    column = lax.axis_index("fsdp").reshape(1)
    gain_row = gain.reshape(1, -1)
    states, early = block_states(q, k, v, gain_row)
    own = lax.all_to_all(states, "chip", 0, 0, tiled=True)
    near_e = along(early, 1, ways), along(early, -1, ways)
    other = lax.ppermute(own, "core", [(0, 1), (1, 0)])
    across_e = along(early, ways // 2, ways)
    own, other, *near_e = lax.optimization_barrier((own, other, *near_e))
    sums = exclusive_sums(core, own, other, chips)
    carried = lax.all_to_all(sums, "chip", 0, 0, tiled=True)
    q_late, within = within_late(q, k, v)
    carried, across_e, q_late, within = lax.optimization_barrier(
        (carried, across_e, q_late, within)
    )
    (a0, a1), (b0, b1) = CALLS
    mine_a = finish_heads(q_late, within, carried, gain_row, a0, a1, True)
    left_a, right_a = lax.optimization_barrier((along(mine_a, 1, ways), along(mine_a, -1, ways)))
    far_a = along(left_a, 1, ways)
    mine_b = finish_heads(q_late, within, carried, gain_row, b0, b1)
    mine_e, left_e, right_e = early_heads([early, *near_e], [mine_a, left_a, right_a])
    left_b = along(mine_b, 1, ways)
    right_b, mine_e, left_e, right_e = lax.optimization_barrier(
        (along(mine_b, -1, ways), mine_e, left_e, right_e)
    )
    far_b = along(right_b, -1, ways)
    total, w = own_mix(column, w, [mine_a, mine_b, mine_e])
    plan = [(-1, a0), (-1, LATE), (1, a0), (1, LATE)]
    total = mix(column, w, plan, [left_a, left_e, right_a, right_e], total)
    total = mix(column, w, [(-1, b0), (1, b0)], [left_b, right_b], total)
    (far_e,) = early_heads([across_e], [far_a])
    total = mix(column, w, [(2, a0), (2, LATE)], [far_a, far_e], total)
    return mix(column, w, [(2, b0)], [far_b], total, True)


def solution(mesh):
    seq, fsdp = mesh.devices.shape
    fine = Mesh(mesh.devices.reshape(seq // CORES, CORES, fsdp), ("chip", "core", "fsdp"))
    rows = ("chip", "core")
    placed = (P(rows, "fsdp"), P(rows, "fsdp"), P(rows, "fsdp"), P("fsdp"), P(None, "fsdp"))
    return jax.shard_map(
        shards, mesh=fine, in_specs=placed, out_specs=P(rows, "fsdp"), check_vma=False
    )
```

```python
import functools

import jax
import jax.numpy as jnp
from jax import lax
from jax.experimental import pallas as pl
from jax.experimental.pallas import tpu as pltpu
from jax.sharding import Mesh
from jax.sharding import PartitionSpec as P

DH = 128
BLK = 512
HALF = BLK // 2
CORES = 2
HEADS = 8
LATE = 6
EARLY = HEADS - LATE
GAIN_ROWS = 16
CALLS = ((0, 3), (3, 6))
F32 = jnp.float32
BF16 = jnp.bfloat16
NN, NT, TN = ((1,), (0,)), ((1,), (1,)), ((0,), (0,))
SMEM = pl.BlockSpec(memory_space=pltpu.SMEM)
VMEM = pl.BlockSpec(memory_space=pltpu.VMEM)
HBM = pl.BlockSpec(memory_space=pltpu.HBM)
PARAMS = pltpu.CompilerParams(vmem_limit_bytes=20 * 2**20)


def dot(a, b, dims):
    return lax.dot_general(a, b, (dims, ((), ())), preferred_element_type=F32)


def in_vmem(value):
    return pltpu.with_memory_space_constraint(value, pltpu.VMEM)


def in_hbm(value):
    return pltpu.with_memory_space_constraint(value, pltpu.HBM)


def cost(flops, size):
    return pl.CostEstimate(flops=flops, bytes_accessed=size, transcendentals=0)


def within_block(q_ref, k_ref, v_ref, h, causal):
    cols = slice(h * DH, (h + 1) * DH)
    q0, q1 = q_ref[:HALF, cols], q_ref[HALF:, cols]
    k0, k1 = k_ref[:HALF, cols], k_ref[HALF:, cols]
    v0, v1 = v_ref[:HALF, cols], v_ref[HALF:, cols]
    s00 = jnp.where(causal, dot(q0, k0, NT), 0.0).astype(BF16)
    s10 = dot(q1, k0, NT).astype(BF16)
    s11 = jnp.where(causal, dot(q1, k1, NT), 0.0).astype(BF16)
    return dot(s00, v0, NN), dot(s10, v0, NN) + dot(s11, v1, NN)


def causal_mask():
    row = lax.broadcasted_iota(jnp.int32, (HALF, HALF), 0)
    col = lax.broadcasted_iota(jnp.int32, (HALF, HALF), 1)
    return col <= row


def finish(queries, within, state, gain):
    att = within + dot(queries, state, NN)
    mean = jnp.full((DH, DH), 1.0 / DH, BF16)
    mean_square = dot((att * att).astype(BF16), mean, NN)
    return (att * lax.rsqrt(mean_square + 1e-6) * gain).astype(BF16)


PARTS = 2


def state_kernel(k_hbm, v_hbm, out_ref, k_ref, v_ref, sems):
    width = k_ref.shape[1] // PARTS
    copies = []
    for part in range(PARTS):
        cols = slice(part * width, (part + 1) * width)
        for at, (hbm, ref) in enumerate(((k_hbm, k_ref), (v_hbm, v_ref))):
            copy = pltpu.make_async_copy(hbm.at[:, cols], ref.at[:, cols], sems.at[part, at])
            copy.start()
            copies.append(copy)
    for part in range(PARTS):
        copies[2 * part].wait()
        copies[2 * part + 1].wait()
        for h in range(part * width // DH, (part + 1) * width // DH):
            cols = slice(h * DH, (h + 1) * DH)
            out_ref[cols, :] = dot(k_ref[:, cols], v_ref[:, cols], TN).astype(BF16)


def block_states(k, v):
    width = k.shape[1]
    return pl.pallas_call(
        state_kernel,
        name="block_states",
        in_specs=[HBM, HBM],
        out_specs=VMEM,
        out_shape=jax.ShapeDtypeStruct((width, DH), BF16),
        scratch_shapes=[
            pltpu.VMEM(k.shape, BF16),
            pltpu.VMEM(v.shape, BF16),
            pltpu.SemaphoreType.DMA((PARTS, 2)),
        ],
        compiler_params=PARAMS,
        cost_estimate=cost(2 * BLK * DH * width, 2 * BLK * width * 2),
    )(in_hbm(k), in_hbm(v))


def within_early_kernel(q_hbm, k_hbm, v_hbm, gain_hbm, *refs):
    out_hbm, (q_ref, k_ref, v_ref, gain_ref, early_ref, sems) = refs[:EARLY], refs[EARLY:]
    early = slice(LATE * DH, HEADS * DH)
    sources = (q_hbm.at[:, early], k_hbm.at[:, early], v_hbm.at[:, early], gain_hbm)
    targets = (q_ref, k_ref, v_ref, gain_ref)
    copies = [
        pltpu.make_async_copy(source, target, sems.at[at])
        for at, (source, target) in enumerate(zip(sources, targets))
    ]
    for copy in copies:
        copy.start()
    for copy in copies:
        copy.wait()
    causal = causal_mask()
    blank = jnp.zeros((GAIN_ROWS - 3, DH), BF16)
    outs = []
    for h in range(EARLY):
        cols = slice(h * DH, (h + 1) * DH)
        gain = gain_ref[:, (LATE + h) * DH : (LATE + h + 1) * DH]
        high = gain.astype(BF16)
        rest = gain - high.astype(F32)
        middle = rest.astype(BF16)
        low = (rest - middle.astype(F32)).astype(BF16)
        top, bottom = within_block(q_ref, k_ref, v_ref, h, causal)
        early_ref[h, :BLK, :DH] = q_ref[:, cols]
        early_ref[h, :HALF, DH:] = top.astype(BF16)
        early_ref[h, HALF:BLK, DH:] = bottom.astype(BF16)
        early_ref[h, BLK:, :DH] = jnp.concatenate([high, middle, low, blank])
        early_ref[h, BLK:, DH:] = jnp.zeros((GAIN_ROWS, DH), BF16)
        outs.append(pltpu.make_async_copy(early_ref.at[h], out_hbm[h], sems.at[4 + h]))
        outs[-1].start()
    for copy in outs:
        copy.wait()


def within_early(q, k, v, gain):
    shape, block = (BLK, EARLY * DH), (BLK + GAIN_ROWS, 2 * DH)
    return pl.pallas_call(
        within_early_kernel,
        name="within_early",
        in_specs=[HBM] * 4,
        out_specs=[HBM] * EARLY,
        out_shape=[jax.ShapeDtypeStruct(block, BF16)] * EARLY,
        scratch_shapes=[
            pltpu.VMEM(shape, BF16),
            pltpu.VMEM(shape, BF16),
            pltpu.VMEM(shape, BF16),
            pltpu.VMEM(gain.shape, F32),
            pltpu.VMEM((EARLY, *block), BF16),
            pltpu.SemaphoreType.DMA((4 + EARLY,)),
        ],
        compiler_params=PARAMS,
        cost_estimate=cost(4 * BLK * BLK * DH * EARLY, BLK * DH * EARLY * 10),
    )(in_hbm(q), in_hbm(k), in_hbm(v), in_hbm(gain))


def scan_kernel(core_ref, own_ref, other_ref, out_ref, *, chips):
    rows = own_ref.shape[0] // chips
    second = (core_ref[0] == 1).astype(F32)
    before = jnp.zeros((rows, DH), F32)
    for chip in range(chips):
        at = slice(chip * rows, (chip + 1) * rows)
        other = other_ref[at, :].astype(F32)
        out_ref[at, :] = (before + second * other).astype(BF16)
        before = before + (own_ref[at, :].astype(F32) + other)


def exclusive_sums(core, own, other, chips):
    return pl.pallas_call(
        functools.partial(scan_kernel, chips=chips),
        name="exclusive_sums",
        in_specs=[SMEM, VMEM, VMEM],
        out_specs=VMEM,
        out_shape=jax.ShapeDtypeStruct(own.shape, BF16),
        compiler_params=PARAMS,
        cost_estimate=cost(own.size * 4, own.size * 6),
    )(core, own, other)


def within_kernel(q_hbm, k_hbm, v_hbm, q_ref, out_ref, k_ref, v_ref, sems):
    copies, split = [], CALLS[0][1] * DH
    parts = (slice(0, split), slice(split, LATE * DH))
    for part, cols in enumerate(parts):
        for at, (hbm, ref) in enumerate(((q_hbm, q_ref), (k_hbm, k_ref), (v_hbm, v_ref))):
            copies.append(
                pltpu.make_async_copy(hbm.at[:, cols], ref.at[:, cols], sems.at[part, at])
            )
            copies[-1].start()
    causal = causal_mask()
    for part, (first, last) in enumerate(CALLS):
        for copy in copies[3 * part : 3 * part + 3]:
            copy.wait()
        for h in range(first, last):
            cols = slice(h * DH, (h + 1) * DH)
            top, bottom = within_block(q_ref, k_ref, v_ref, h, causal)
            out_ref[:HALF, cols] = top
            out_ref[HALF:, cols] = bottom


def within_late(q, k, v):
    shape = (BLK, LATE * DH)
    return pl.pallas_call(
        within_kernel,
        name="within_late",
        in_specs=[HBM] * 3,
        out_specs=[VMEM, VMEM],
        out_shape=[pltpu.VMEM(shape, BF16), pltpu.VMEM(shape, F32)],
        scratch_shapes=[
            pltpu.VMEM(shape, BF16),
            pltpu.VMEM(shape, BF16),
            pltpu.SemaphoreType.DMA((2, 3)),
        ],
        compiler_params=PARAMS,
        cost_estimate=cost(4 * BLK * BLK * DH * LATE, BLK * DH * LATE * 10),
    )(in_hbm(q), in_hbm(k), in_hbm(v))


def finish_kernel(q_ref, within_ref, carried_ref, gain_ref, out_ref, *, first, last):
    for h in range(first, last):
        cols = slice(h * DH, (h + 1) * DH)
        out_cols = slice((h - first) * DH, (h - first + 1) * DH)
        out_ref[:BLK, out_cols] = finish(
            q_ref[:, cols], within_ref[:, cols], carried_ref[cols, :], gain_ref[:, cols]
        )
    if out_ref.shape[0] > BLK:
        out_ref[BLK:, EARLY * DH :] = jnp.zeros((DH, out_ref.shape[1] - EARLY * DH), BF16)
        for h in range(EARLY):
            state = carried_ref[(LATE + h) * DH : (LATE + h + 1) * DH, :]
            out_ref[BLK:, h * DH : (h + 1) * DH] = state


def finish_heads(q, within, carried, gain, first, last, states=False):
    heads = last - first
    return pl.pallas_call(
        functools.partial(finish_kernel, first=first, last=last),
        name="finish_heads",
        in_specs=[VMEM] * 4,
        out_specs=VMEM,
        out_shape=jax.ShapeDtypeStruct((BLK + DH if states else BLK, heads * DH), BF16),
        compiler_params=PARAMS,
        cost_estimate=cost(4 * BLK * DH * DH * heads, BLK * DH * heads * 8),
    )(q, within, carried, gain)


def early_kernel(*refs, count):
    hbm_refs, rest = refs[: count * EARLY], refs[count * EARLY :]
    a_refs, out_refs, (e_ref, sems) = rest[:count], rest[count : 2 * count], rest[2 * count :]
    copies = [
        pltpu.make_async_copy(hbm, e_ref.at[at], sems.at[at]) for at, hbm in enumerate(hbm_refs)
    ]
    for copy in copies:
        copy.start()
    for source, (a_ref, out_ref) in enumerate(zip(a_refs, out_refs)):
        for h in range(EARLY):
            at = source * EARLY + h
            copies[at].wait()
            cols = slice(h * DH, (h + 1) * DH)
            terms = e_ref[at, BLK:, :DH].astype(F32)
            gain = terms[0:1] + terms[1:2] + terms[2:3]
            within = e_ref[at, :BLK, DH:].astype(F32)
            out_ref[:, cols] = finish(e_ref[at, :BLK, :DH], within, a_ref[BLK:, cols], gain)


def early_heads(early, chunks):
    count = len(chunks)
    early = [value for pair in early for value in pair]
    return pl.pallas_call(
        functools.partial(early_kernel, count=count),
        name="early_heads",
        in_specs=[pl.BlockSpec(memory_space=pl.ANY)] * len(early) + [VMEM] * count,
        out_specs=[VMEM] * count,
        out_shape=[jax.ShapeDtypeStruct((BLK, EARLY * DH), BF16)] * count,
        scratch_shapes=[
            pltpu.VMEM((len(early), *early[0].shape), BF16),
            pltpu.SemaphoreType.DMA((len(early),)),
        ],
        compiler_params=PARAMS,
        cost_estimate=cost(4 * BLK * DH * DH * EARLY * count, BLK * DH * EARLY * count * 6),
    )(*early, *chunks)


TILE = 256


def weight_rows(w_hbm, column_ref, shift):
    depth = HEADS * DH
    ways = w_hbm.shape[0] // depth
    source = lax.rem(column_ref[0] + (shift + ways), ways)
    return w_hbm.at[pl.ds(pl.multiple_of(source * depth, depth), depth)]


def own_kernel(column_ref, *refs):
    *a_refs, w_hbm, total_ref, w_ref, sems = refs
    source = weight_rows(w_hbm, column_ref, 0)
    copies, rows, at = [], [], 0
    for piece, a_ref in enumerate(a_refs):
        rows.append(slice(at, at + a_ref.shape[1]))
        at += a_ref.shape[1]
        copies.append(
            pltpu.make_async_copy(source.at[rows[-1]], w_ref.at[rows[-1]], sems.at[piece])
        )
        copies[-1].start()
    for piece, a_ref in enumerate(a_refs):
        copies[piece].wait()
        for tile in range(total_ref.shape[1] // TILE):
            cols = slice(tile * TILE, (tile + 1) * TILE)
            term = dot(a_ref[:BLK, :], w_ref[rows[piece], cols], NN)
            total_ref[:, cols] = term if piece == 0 else total_ref[:, cols] + term


def own_mix(column, w, arrays):
    width, depth = w.shape[1], HEADS * DH
    return pl.pallas_call(
        own_kernel,
        name="own_mix",
        in_specs=[SMEM] + [VMEM] * len(arrays) + [HBM],
        out_specs=VMEM,
        out_shape=pltpu.VMEM((BLK, width), F32),
        scratch_shapes=[
            pltpu.VMEM((depth, width), BF16),
            pltpu.SemaphoreType.DMA((len(arrays),)),
        ],
        compiler_params=PARAMS,
        cost_estimate=cost(2 * BLK * depth * width, 2 * depth * width),
    )(column, *arrays, in_hbm(w))


def add_products(total_ref, out_ref, a_refs, w_ref, starts, cols):
    total = total_ref[:, cols]
    for a_ref, start in zip(a_refs, starts):
        total = total + dot(a_ref[:BLK, :], w_ref[start : start + a_ref.shape[1], cols], NN)
    out_ref[:, cols] = total.astype(out_ref.dtype)


SIDES = (-1, 1, 2)


def side_kernel(column_ref, *refs, starts):
    *a_refs, w_hbm, total_ref, out_ref, w_ref, sems = refs
    depth = HEADS * DH
    copies = []
    for at, shift in enumerate(SIDES):
        rows = slice(at * depth, (at + 1) * depth)
        copies.append(
            pltpu.make_async_copy(
                weight_rows(w_hbm, column_ref, shift), w_ref.at[rows], sems.at[at]
            )
        )
        copies[-1].start()
    half = len(a_refs) // 2
    for side in range(2):
        copies[side].wait()
        mine = slice(side * half, (side + 1) * half)
        for tile in range(out_ref.shape[1] // TILE):
            cols = slice(tile * TILE, (tile + 1) * TILE)
            source = out_ref if side else total_ref
            add_products(source, out_ref, a_refs[mine], w_ref, starts[mine], cols)
    copies[2].wait()


def side_mix(column, w, starts, arrays, total):
    width, depth = w.shape[1], len(SIDES) * HEADS * DH
    return pl.pallas_call(
        functools.partial(side_kernel, starts=starts),
        name="side_mix",
        in_specs=[SMEM] + [VMEM] * len(arrays) + [HBM, VMEM],
        out_specs=[VMEM, VMEM],
        out_shape=[pltpu.VMEM((BLK, width), F32), pltpu.VMEM((depth, width), BF16)],
        scratch_shapes=[pltpu.SemaphoreType.DMA((len(SIDES),))],
        compiler_params=PARAMS,
        cost_estimate=cost(2 * BLK * depth * width, 2 * depth * width),
    )(column, *arrays, in_hbm(w), total)


def mix_kernel(*refs, count, starts, last):
    a_refs, (w_ref, total_ref), rest = refs[:count], refs[count : count + 2], refs[count + 2 :]
    if last:
        out_hbm, out_ref, sems = rest
    else:
        (out_ref,) = rest
    copies = []
    for tile in range(out_ref.shape[1] // TILE):
        cols = slice(tile * TILE, (tile + 1) * TILE)
        add_products(total_ref, out_ref, a_refs, w_ref, starts, cols)
        if last:
            copy = pltpu.make_async_copy(out_ref.at[:, cols], out_hbm.at[:, cols], sems.at[tile])
            copy.start()
            copies.append(copy)
    for copy in copies:
        copy.wait()


def mix(w, starts, arrays, total, last=False):
    width = w.shape[1]
    depth = sum(a.shape[1] for a in arrays)
    if last:
        out_shape = jax.ShapeDtypeStruct((BLK, width), BF16)
        scratch = [pltpu.VMEM((BLK, width), BF16), pltpu.SemaphoreType.DMA((width // TILE,))]
    else:
        out_shape, scratch = pltpu.VMEM((BLK, width), F32), []
    return pl.pallas_call(
        functools.partial(mix_kernel, count=len(arrays), starts=starts, last=last),
        name="mix",
        in_specs=[VMEM] * (len(arrays) + 2),
        out_specs=HBM if last else VMEM,
        out_shape=out_shape,
        scratch_shapes=scratch,
        compiler_params=PARAMS,
        cost_estimate=cost(2 * BLK * depth * width, 2 * depth * width),
    )(*arrays, w, total)


def along(value, shift, count):
    return lax.ppermute(value, "fsdp", [(i, (i + shift) % count) for i in range(count)])


def shards(q, k, v, gain, w):
    chips, ways = lax.axis_size("chip"), lax.axis_size("fsdp")
    core = lax.axis_index("core").reshape(1)
    column = lax.axis_index("fsdp").reshape(1)
    gain_row = gain.reshape(1, -1)
    states = block_states(k, v)
    own = lax.all_to_all(states, "chip", 0, 0, tiled=True)
    early = within_early(q, k, v, gain_row)
    left_q = [along(value, 1, ways) for value in early]
    right_q = [along(value, -1, ways) for value in early]
    other = lax.ppermute(own, "core", [(0, 1), (1, 0)])
    own, other, left_q, right_q = lax.optimization_barrier((own, other, left_q, right_q))
    far_q = [along(left_q[0], 1, ways), along(right_q[1], -1, ways)]
    sums = exclusive_sums(core, own, other, chips)
    carried = lax.all_to_all(sums, "chip", 0, 0, tiled=True)
    q_late, within = within_late(q, k, v)
    carried, far_q, q_late, within = lax.optimization_barrier((carried, far_q, q_late, within))
    (a0, a1), (b0, b1) = CALLS
    mine_a = finish_heads(q_late, within, carried, gain_row, a0, a1, True)
    mine_b = finish_heads(q_late, within, carried, gain_row, b0, b1)
    (mine_e,) = early_heads([early], [mine_a])
    total = own_mix(column, w, [mine_a, mine_b, mine_e])
    left_a, right_a, total = lax.optimization_barrier(
        (along(mine_a, 1, ways), along(mine_a, -1, ways), total)
    )
    far_a = along(left_a, 1, ways)
    left_e, right_e = early_heads([left_q, right_q], [left_a, right_a])
    left_b = along(mine_b, 1, ways)
    right_b, left_e, right_e = lax.optimization_barrier(
        (along(mine_b, -1, ways), left_e, right_e)
    )
    far_b = along(right_b, -1, ways)
    depth = HEADS * DH
    at_a, at_b, at_e = a0 * DH, b0 * DH, LATE * DH
    starts = (at_a, at_e, depth + at_a, depth + at_e)
    total, w = side_mix(column, w, starts, [left_a, left_e, right_a, right_e], total)
    (far_e,) = early_heads([far_q], [far_a])
    total = mix(w, (2 * depth + at_a, 2 * depth + at_e), [far_a, far_e], total)
    total = mix(w, (at_b, depth + at_b), [left_b, right_b], total)
    return mix(w, (2 * depth + at_b,), [far_b], total, True)


def solution(mesh):
    seq, fsdp = mesh.devices.shape
    fine = Mesh(mesh.devices.reshape(seq // CORES, CORES, fsdp), ("chip", "core", "fsdp"))
    rows = ("chip", "core")
    placed = (P(rows, "fsdp"), P(rows, "fsdp"), P(rows, "fsdp"), P("fsdp"), P(None, "fsdp"))
    return jax.shard_map(
        shards, mesh=fine, in_specs=placed, out_specs=P(rows, "fsdp"), check_vma=False
    )
```

```python
import functools

import jax
import jax.numpy as jnp
from jax import lax
from jax.experimental import pallas as pl
from jax.experimental.pallas import tpu as pltpu
from jax.sharding import Mesh
from jax.sharding import PartitionSpec as P

DH = 128
BLK = 512
HALF = BLK // 2
CORES = 2
HEADS = 8
LATE = 6
EARLY = HEADS - LATE
GAIN_ROWS = 16
CALLS = ((0, 3), (3, 6))
F32 = jnp.float32
BF16 = jnp.bfloat16
NN, NT, TN = ((1,), (0,)), ((1,), (1,)), ((0,), (0,))
SMEM = pl.BlockSpec(memory_space=pltpu.SMEM)
VMEM = pl.BlockSpec(memory_space=pltpu.VMEM)
HBM = pl.BlockSpec(memory_space=pltpu.HBM)
PARAMS = pltpu.CompilerParams(vmem_limit_bytes=20 * 2**20)


def dot(a, b, dims):
    return lax.dot_general(a, b, (dims, ((), ())), preferred_element_type=F32)


def in_vmem(value):
    return pltpu.with_memory_space_constraint(value, pltpu.VMEM)


def in_hbm(value):
    return pltpu.with_memory_space_constraint(value, pltpu.HBM)


def cost(flops, size):
    return pl.CostEstimate(flops=flops, bytes_accessed=size, transcendentals=0)


def within_block(q_ref, k_ref, v_ref, h, causal):
    cols = slice(h * DH, (h + 1) * DH)
    q0, q1 = q_ref[:HALF, cols], q_ref[HALF:, cols]
    k0, k1 = k_ref[:HALF, cols], k_ref[HALF:, cols]
    v0, v1 = v_ref[:HALF, cols], v_ref[HALF:, cols]
    s00 = jnp.where(causal, dot(q0, k0, NT), 0.0).astype(BF16)
    s10 = dot(q1, k0, NT).astype(BF16)
    s11 = jnp.where(causal, dot(q1, k1, NT), 0.0).astype(BF16)
    return dot(s00, v0, NN), dot(s10, v0, NN) + dot(s11, v1, NN)


def causal_mask():
    row = lax.broadcasted_iota(jnp.int32, (HALF, HALF), 0)
    col = lax.broadcasted_iota(jnp.int32, (HALF, HALF), 1)
    return col <= row


def finish(queries, within, state, gain):
    att = within + dot(queries, state, NN)
    mean = jnp.full((DH, DH), 1.0 / DH, BF16)
    mean_square = dot((att * att).astype(BF16), mean, NN)
    return (att * lax.rsqrt(mean_square + 1e-6) * gain).astype(BF16)


PARTS = 2


def state_kernel(k_hbm, v_hbm, out_ref, k_ref, v_ref, sems):
    width = k_ref.shape[1] // PARTS
    copies = []
    for part in range(PARTS):
        cols = slice(part * width, (part + 1) * width)
        for at, (hbm, ref) in enumerate(((k_hbm, k_ref), (v_hbm, v_ref))):
            copy = pltpu.make_async_copy(hbm.at[:, cols], ref.at[:, cols], sems.at[part, at])
            copy.start()
            copies.append(copy)
    for part in range(PARTS):
        copies[2 * part].wait()
        copies[2 * part + 1].wait()
        for h in range(part * width // DH, (part + 1) * width // DH):
            cols = slice(h * DH, (h + 1) * DH)
            out_ref[cols, :] = dot(k_ref[:, cols], v_ref[:, cols], TN).astype(BF16)


def block_states(k, v):
    width = k.shape[1]
    return pl.pallas_call(
        state_kernel,
        name="block_states",
        in_specs=[HBM, HBM],
        out_specs=VMEM,
        out_shape=jax.ShapeDtypeStruct((width, DH), BF16),
        scratch_shapes=[
            pltpu.VMEM(k.shape, BF16),
            pltpu.VMEM(v.shape, BF16),
            pltpu.SemaphoreType.DMA((PARTS, 2)),
        ],
        compiler_params=PARAMS,
        cost_estimate=cost(2 * BLK * DH * width, 2 * BLK * width * 2),
    )(in_hbm(k), in_hbm(v))


def within_early_kernel(q_hbm, k_hbm, v_hbm, gain_hbm, *refs):
    out_hbm, (q_ref, k_ref, v_ref, gain_ref, early_ref, sems) = refs[:EARLY], refs[EARLY:]
    early = slice(LATE * DH, HEADS * DH)
    sources = (q_hbm.at[:, early], k_hbm.at[:, early], v_hbm.at[:, early], gain_hbm)
    targets = (q_ref, k_ref, v_ref, gain_ref)
    copies = [
        pltpu.make_async_copy(source, target, sems.at[at])
        for at, (source, target) in enumerate(zip(sources, targets))
    ]
    for copy in copies:
        copy.start()
    for copy in copies:
        copy.wait()
    causal = causal_mask()
    blank = jnp.zeros((GAIN_ROWS - 3, DH), BF16)
    outs = []
    for h in range(EARLY):
        cols = slice(h * DH, (h + 1) * DH)
        gain = gain_ref[:, (LATE + h) * DH : (LATE + h + 1) * DH]
        high = gain.astype(BF16)
        rest = gain - high.astype(F32)
        middle = rest.astype(BF16)
        low = (rest - middle.astype(F32)).astype(BF16)
        top, bottom = within_block(q_ref, k_ref, v_ref, h, causal)
        early_ref[h, :BLK, :DH] = q_ref[:, cols]
        early_ref[h, :HALF, DH:] = top.astype(BF16)
        early_ref[h, HALF:BLK, DH:] = bottom.astype(BF16)
        early_ref[h, BLK:, :DH] = jnp.concatenate([high, middle, low, blank])
        early_ref[h, BLK:, DH:] = jnp.zeros((GAIN_ROWS, DH), BF16)
        outs.append(pltpu.make_async_copy(early_ref.at[h], out_hbm[h], sems.at[4 + h]))
        outs[-1].start()
    for copy in outs:
        copy.wait()


def within_early(q, k, v, gain):
    shape, block = (BLK, EARLY * DH), (BLK + GAIN_ROWS, 2 * DH)
    return pl.pallas_call(
        within_early_kernel,
        name="within_early",
        in_specs=[HBM] * 4,
        out_specs=[HBM] * EARLY,
        out_shape=[jax.ShapeDtypeStruct(block, BF16)] * EARLY,
        scratch_shapes=[
            pltpu.VMEM(shape, BF16),
            pltpu.VMEM(shape, BF16),
            pltpu.VMEM(shape, BF16),
            pltpu.VMEM(gain.shape, F32),
            pltpu.VMEM((EARLY, *block), BF16),
            pltpu.SemaphoreType.DMA((4 + EARLY,)),
        ],
        compiler_params=PARAMS,
        cost_estimate=cost(4 * BLK * BLK * DH * EARLY, BLK * DH * EARLY * 10),
    )(in_hbm(q), in_hbm(k), in_hbm(v), in_hbm(gain))


def scan_kernel(core_ref, own_ref, other_ref, out_ref, *, chips):
    rows = own_ref.shape[0] // chips
    second = (core_ref[0] == 1).astype(F32)
    before = jnp.zeros((rows, DH), F32)
    for chip in range(chips):
        at = slice(chip * rows, (chip + 1) * rows)
        other = other_ref[at, :].astype(F32)
        out_ref[at, :] = (before + second * other).astype(BF16)
        before = before + (own_ref[at, :].astype(F32) + other)


def exclusive_sums(core, own, other, chips):
    return pl.pallas_call(
        functools.partial(scan_kernel, chips=chips),
        name="exclusive_sums",
        in_specs=[SMEM, VMEM, VMEM],
        out_specs=VMEM,
        out_shape=jax.ShapeDtypeStruct(own.shape, BF16),
        compiler_params=PARAMS,
        cost_estimate=cost(own.size * 4, own.size * 6),
    )(core, own, other)


def within_kernel(q_hbm, k_hbm, v_hbm, q_ref, out_ref, k_ref, v_ref, sems):
    copies, split = [], CALLS[0][1] * DH
    parts = (slice(0, split), slice(split, LATE * DH))
    for part, cols in enumerate(parts):
        for at, (hbm, ref) in enumerate(((q_hbm, q_ref), (k_hbm, k_ref), (v_hbm, v_ref))):
            copies.append(
                pltpu.make_async_copy(hbm.at[:, cols], ref.at[:, cols], sems.at[part, at])
            )
            copies[-1].start()
    causal = causal_mask()
    for part, (first, last) in enumerate(CALLS):
        for copy in copies[3 * part : 3 * part + 3]:
            copy.wait()
        for h in range(first, last):
            cols = slice(h * DH, (h + 1) * DH)
            top, bottom = within_block(q_ref, k_ref, v_ref, h, causal)
            out_ref[:HALF, cols] = top
            out_ref[HALF:, cols] = bottom


def within_late(q, k, v):
    shape = (BLK, LATE * DH)
    return pl.pallas_call(
        within_kernel,
        name="within_late",
        in_specs=[HBM] * 3,
        out_specs=[VMEM, VMEM],
        out_shape=[pltpu.VMEM(shape, BF16), pltpu.VMEM(shape, F32)],
        scratch_shapes=[
            pltpu.VMEM(shape, BF16),
            pltpu.VMEM(shape, BF16),
            pltpu.SemaphoreType.DMA((2, 3)),
        ],
        compiler_params=PARAMS,
        cost_estimate=cost(4 * BLK * BLK * DH * LATE, BLK * DH * LATE * 10),
    )(in_hbm(q), in_hbm(k), in_hbm(v))


def finish_kernel(q_ref, within_ref, carried_ref, gain_ref, out_ref, *, first, last):
    for h in range(first, last):
        cols = slice(h * DH, (h + 1) * DH)
        out_cols = slice((h - first) * DH, (h - first + 1) * DH)
        out_ref[:BLK, out_cols] = finish(
            q_ref[:, cols], within_ref[:, cols], carried_ref[cols, :], gain_ref[:, cols]
        )
    if out_ref.shape[0] > BLK:
        out_ref[BLK:, EARLY * DH :] = jnp.zeros((DH, out_ref.shape[1] - EARLY * DH), BF16)
        for h in range(EARLY):
            state = carried_ref[(LATE + h) * DH : (LATE + h + 1) * DH, :]
            out_ref[BLK:, h * DH : (h + 1) * DH] = state


def finish_heads(q, within, carried, gain, first, last, states=False):
    heads = last - first
    return pl.pallas_call(
        functools.partial(finish_kernel, first=first, last=last),
        name="finish_heads",
        in_specs=[VMEM] * 4,
        out_specs=VMEM,
        out_shape=jax.ShapeDtypeStruct((BLK + DH if states else BLK, heads * DH), BF16),
        compiler_params=PARAMS,
        cost_estimate=cost(4 * BLK * DH * DH * heads, BLK * DH * heads * 8),
    )(q, within, carried, gain)


def early_kernel(*refs, count):
    hbm_refs, rest = refs[: count * EARLY], refs[count * EARLY :]
    a_refs, out_refs, (e_ref, sems) = rest[:count], rest[count : 2 * count], rest[2 * count :]
    copies = [
        pltpu.make_async_copy(hbm, e_ref.at[at], sems.at[at]) for at, hbm in enumerate(hbm_refs)
    ]
    for copy in copies:
        copy.start()
    for source, (a_ref, out_ref) in enumerate(zip(a_refs, out_refs)):
        for h in range(EARLY):
            at = source * EARLY + h
            copies[at].wait()
            cols = slice(h * DH, (h + 1) * DH)
            terms = e_ref[at, BLK:, :DH].astype(F32)
            gain = terms[0:1] + terms[1:2] + terms[2:3]
            within = e_ref[at, :BLK, DH:].astype(F32)
            out_ref[:, cols] = finish(e_ref[at, :BLK, :DH], within, a_ref[BLK:, cols], gain)


def early_heads(early, chunks):
    count = len(chunks)
    early = [value for pair in early for value in pair]
    return pl.pallas_call(
        functools.partial(early_kernel, count=count),
        name="early_heads",
        in_specs=[pl.BlockSpec(memory_space=pl.ANY)] * len(early) + [VMEM] * count,
        out_specs=[VMEM] * count,
        out_shape=[jax.ShapeDtypeStruct((BLK, EARLY * DH), BF16)] * count,
        scratch_shapes=[
            pltpu.VMEM((len(early), *early[0].shape), BF16),
            pltpu.SemaphoreType.DMA((len(early),)),
        ],
        compiler_params=PARAMS,
        cost_estimate=cost(4 * BLK * DH * DH * EARLY * count, BLK * DH * EARLY * count * 6),
    )(*early, *chunks)


TILE = 256


def weight_rows(w_hbm, column_ref, shift):
    depth = HEADS * DH
    ways = w_hbm.shape[0] // depth
    source = lax.rem(column_ref[0] + (shift + ways), ways)
    return w_hbm.at[pl.ds(pl.multiple_of(source * depth, depth), depth)]


def own_kernel(column_ref, *refs):
    *a_refs, w_hbm, total_ref, w_ref, sems = refs
    source = weight_rows(w_hbm, column_ref, 0)
    copies, rows, at = [], [], 0
    for piece, a_ref in enumerate(a_refs):
        rows.append(slice(at, at + a_ref.shape[1]))
        at += a_ref.shape[1]
        copies.append(
            pltpu.make_async_copy(source.at[rows[-1]], w_ref.at[rows[-1]], sems.at[piece])
        )
        copies[-1].start()
    for piece, a_ref in enumerate(a_refs):
        copies[piece].wait()
        for tile in range(total_ref.shape[1] // TILE):
            cols = slice(tile * TILE, (tile + 1) * TILE)
            term = dot(a_ref[:BLK, :], w_ref[rows[piece], cols], NN)
            total_ref[:, cols] = term if piece == 0 else total_ref[:, cols] + term


def own_mix(column, w, arrays):
    width, depth = w.shape[1], HEADS * DH
    return pl.pallas_call(
        own_kernel,
        name="own_mix",
        in_specs=[SMEM] + [VMEM] * len(arrays) + [HBM],
        out_specs=VMEM,
        out_shape=pltpu.VMEM((BLK, width), F32),
        scratch_shapes=[
            pltpu.VMEM((depth, width), BF16),
            pltpu.SemaphoreType.DMA((len(arrays),)),
        ],
        compiler_params=PARAMS,
        cost_estimate=cost(2 * BLK * depth * width, 2 * depth * width),
    )(column, *arrays, in_hbm(w))


def add_products(total_ref, out_ref, a_refs, w_ref, starts, cols):
    total = total_ref[:, cols]
    for a_ref, start in zip(a_refs, starts):
        total = total + dot(a_ref[:BLK, :], w_ref[start : start + a_ref.shape[1], cols], NN)
    out_ref[:, cols] = total.astype(out_ref.dtype)


SIDES = (-1, 1, 2)


def side_kernel(column_ref, *refs, starts):
    *a_refs, w_hbm, total_ref, out_ref, w_ref, sems = refs
    depth = HEADS * DH
    copies = []
    for at, shift in enumerate(SIDES):
        rows = slice(at * depth, (at + 1) * depth)
        copies.append(
            pltpu.make_async_copy(
                weight_rows(w_hbm, column_ref, shift), w_ref.at[rows], sems.at[at]
            )
        )
        copies[-1].start()
    half = len(a_refs) // 2
    for side in range(2):
        copies[side].wait()
        mine = slice(side * half, (side + 1) * half)
        for tile in range(out_ref.shape[1] // TILE):
            cols = slice(tile * TILE, (tile + 1) * TILE)
            source = out_ref if side else total_ref
            add_products(source, out_ref, a_refs[mine], w_ref, starts[mine], cols)
    copies[2].wait()


def side_mix(column, w, starts, arrays, total):
    width, depth = w.shape[1], len(SIDES) * HEADS * DH
    return pl.pallas_call(
        functools.partial(side_kernel, starts=starts),
        name="side_mix",
        in_specs=[SMEM] + [VMEM] * len(arrays) + [HBM, VMEM],
        out_specs=[VMEM, VMEM],
        out_shape=[pltpu.VMEM((BLK, width), F32), pltpu.VMEM((depth, width), BF16)],
        scratch_shapes=[pltpu.SemaphoreType.DMA((len(SIDES),))],
        compiler_params=PARAMS,
        cost_estimate=cost(2 * BLK * depth * width, 2 * depth * width),
    )(column, *arrays, in_hbm(w), total)


def mix_kernel(*refs, count, starts, last):
    a_refs, (w_ref, total_ref), rest = refs[:count], refs[count : count + 2], refs[count + 2 :]
    if last:
        out_hbm, out_ref, sems = rest
    else:
        (out_ref,) = rest
    copies = []
    for tile in range(out_ref.shape[1] // TILE):
        cols = slice(tile * TILE, (tile + 1) * TILE)
        add_products(total_ref, out_ref, a_refs, w_ref, starts, cols)
        if last:
            copy = pltpu.make_async_copy(out_ref.at[:, cols], out_hbm.at[:, cols], sems.at[tile])
            copy.start()
            copies.append(copy)
    for copy in copies:
        copy.wait()


def mix(w, starts, arrays, total, last=False):
    width = w.shape[1]
    depth = sum(a.shape[1] for a in arrays)
    if last:
        out_shape = jax.ShapeDtypeStruct((BLK, width), BF16)
        scratch = [pltpu.VMEM((BLK, width), BF16), pltpu.SemaphoreType.DMA((width // TILE,))]
    else:
        out_shape, scratch = pltpu.VMEM((BLK, width), F32), []
    return pl.pallas_call(
        functools.partial(mix_kernel, count=len(arrays), starts=starts, last=last),
        name="mix",
        in_specs=[VMEM] * (len(arrays) + 2),
        out_specs=HBM if last else VMEM,
        out_shape=out_shape,
        scratch_shapes=scratch,
        compiler_params=PARAMS,
        cost_estimate=cost(2 * BLK * depth * width, 2 * depth * width),
    )(*arrays, w, total)


def along(value, shift, count):
    return lax.ppermute(value, "fsdp", [(i, (i + shift) % count) for i in range(count)])


def shards(q, k, v, gain, w):
    chips, ways = lax.axis_size("chip"), lax.axis_size("fsdp")
    core = lax.axis_index("core").reshape(1)
    column = lax.axis_index("fsdp").reshape(1)
    gain_row = gain.reshape(1, -1)
    states = block_states(k, v)
    own = lax.all_to_all(states, "chip", 0, 0, tiled=True)
    early = within_early(q, k, v, gain_row)
    left_q = [along(value, 1, ways) for value in early]
    right_q = [along(value, -1, ways) for value in early]
    own, *early = lax.optimization_barrier((own, *early))
    other = lax.ppermute(own, "core", [(0, 1), (1, 0)])
    left_q, right_q = lax.optimization_barrier((left_q, right_q))
    far_q = [along(left_q[0], 1, ways), along(right_q[1], -1, ways)]
    sums = exclusive_sums(core, own, other, chips)
    carried = lax.all_to_all(sums, "chip", 0, 0, tiled=True)
    q_late, within = within_late(q, k, v)
    carried, far_q, q_late, within = lax.optimization_barrier((carried, far_q, q_late, within))
    (a0, a1), (b0, b1) = CALLS
    mine_a = finish_heads(q_late, within, carried, gain_row, a0, a1, True)
    mine_b = finish_heads(q_late, within, carried, gain_row, b0, b1)
    (mine_e,) = early_heads([early], [mine_a])
    total = own_mix(column, w, [mine_a, mine_b, mine_e])
    left_a, right_a, total = lax.optimization_barrier(
        (along(mine_a, 1, ways), along(mine_a, -1, ways), total)
    )
    far_a = along(left_a, 1, ways)
    left_e, right_e = early_heads([left_q, right_q], [left_a, right_a])
    left_b = along(mine_b, 1, ways)
    right_b, left_e, right_e = lax.optimization_barrier(
        (along(mine_b, -1, ways), left_e, right_e)
    )
    far_b = along(right_b, -1, ways)
    depth = HEADS * DH
    at_a, at_b, at_e = a0 * DH, b0 * DH, LATE * DH
    starts = (at_a, at_e, depth + at_a, depth + at_e)
    total, w = side_mix(column, w, starts, [left_a, left_e, right_a, right_e], total)
    (far_e,) = early_heads([far_q], [far_a])
    total = mix(w, (2 * depth + at_a, 2 * depth + at_e), [far_a, far_e], total)
    total = mix(w, (at_b, depth + at_b), [left_b, right_b], total)
    return mix(w, (2 * depth + at_b,), [far_b], total, True)


def solution(mesh):
    seq, fsdp = mesh.devices.shape
    fine = Mesh(mesh.devices.reshape(seq // CORES, CORES, fsdp), ("chip", "core", "fsdp"))
    rows = ("chip", "core")
    placed = (P(rows, "fsdp"), P(rows, "fsdp"), P(rows, "fsdp"), P("fsdp"), P(None, "fsdp"))
    return jax.shard_map(
        shards, mesh=fine, in_specs=placed, out_specs=P(rows, "fsdp"), check_vma=False
    )
```

```python
import functools

import jax
import jax.numpy as jnp
from jax import lax
from jax.experimental import pallas as pl
from jax.experimental.pallas import tpu as pltpu
from jax.sharding import Mesh
from jax.sharding import PartitionSpec as P

DH = 128
BLK = 512
HALF = BLK // 2
CORES = 2
HEADS = 8
CALLS = ((0, 4), (4, 8))
F32 = jnp.float32
BF16 = jnp.bfloat16
NN, NT, TN = ((1,), (0,)), ((1,), (1,)), ((0,), (0,))
SMEM = pl.BlockSpec(memory_space=pltpu.SMEM)
VMEM = pl.BlockSpec(memory_space=pltpu.VMEM)
HBM = pl.BlockSpec(memory_space=pltpu.HBM)
PARAMS = pltpu.CompilerParams(vmem_limit_bytes=20 * 2**20)


def dot(a, b, dims):
    return lax.dot_general(a, b, (dims, ((), ())), preferred_element_type=F32)


def in_vmem(value):
    return pltpu.with_memory_space_constraint(value, pltpu.VMEM)


def in_hbm(value):
    return pltpu.with_memory_space_constraint(value, pltpu.HBM)


def cost(flops, size):
    return pl.CostEstimate(flops=flops, bytes_accessed=size, transcendentals=0)


def within_block(q_ref, k_ref, v_ref, h, causal):
    cols = slice(h * DH, (h + 1) * DH)
    q0, q1 = q_ref[:HALF, cols], q_ref[HALF:, cols]
    k0, k1 = k_ref[:HALF, cols], k_ref[HALF:, cols]
    v0, v1 = v_ref[:HALF, cols], v_ref[HALF:, cols]
    s00 = jnp.where(causal, dot(q0, k0, NT), 0.0).astype(BF16)
    s10 = dot(q1, k0, NT).astype(BF16)
    s11 = jnp.where(causal, dot(q1, k1, NT), 0.0).astype(BF16)
    return dot(s00, v0, NN), dot(s10, v0, NN) + dot(s11, v1, NN)


def causal_mask():
    row = lax.broadcasted_iota(jnp.int32, (HALF, HALF), 0)
    col = lax.broadcasted_iota(jnp.int32, (HALF, HALF), 1)
    return col <= row


def finish(queries, within, state, gain):
    att = within + dot(queries, state, NN)
    mean = jnp.full((DH, DH), 1.0 / DH, BF16)
    mean_square = dot((att * att).astype(BF16), mean, NN)
    return (att * lax.rsqrt(mean_square + 1e-6) * gain).astype(BF16)


PARTS = 2


def state_kernel(k_hbm, v_hbm, out_ref, k_ref, v_ref, sems):
    width = k_ref.shape[1] // PARTS
    copies = []
    for part in range(PARTS):
        cols = slice(part * width, (part + 1) * width)
        for at, (hbm, ref) in enumerate(((k_hbm, k_ref), (v_hbm, v_ref))):
            copy = pltpu.make_async_copy(hbm.at[:, cols], ref.at[:, cols], sems.at[part, at])
            copy.start()
            copies.append(copy)
    for part in range(PARTS):
        copies[2 * part].wait()
        copies[2 * part + 1].wait()
        for h in range(part * width // DH, (part + 1) * width // DH):
            cols = slice(h * DH, (h + 1) * DH)
            out_ref[cols, :] = dot(k_ref[:, cols], v_ref[:, cols], TN).astype(BF16)


def block_states(k, v):
    width = k.shape[1]
    return pl.pallas_call(
        state_kernel,
        name="block_states",
        in_specs=[HBM, HBM],
        out_specs=VMEM,
        out_shape=jax.ShapeDtypeStruct((width, DH), BF16),
        scratch_shapes=[
            pltpu.VMEM(k.shape, BF16),
            pltpu.VMEM(v.shape, BF16),
            pltpu.SemaphoreType.DMA((PARTS, 2)),
        ],
        compiler_params=PARAMS,
        cost_estimate=cost(2 * BLK * DH * width, 2 * BLK * width * 2),
    )(in_hbm(k), in_hbm(v))


def scan_kernel(core_ref, own_ref, other_ref, out_ref, *, chips):
    rows = own_ref.shape[0] // chips
    second = (core_ref[0] == 1).astype(F32)
    before = jnp.zeros((rows, DH), F32)
    for chip in range(chips):
        at = slice(chip * rows, (chip + 1) * rows)
        other = other_ref[at, :].astype(F32)
        out_ref[at, :] = (before + second * other).astype(BF16)
        before = before + (own_ref[at, :].astype(F32) + other)


def exclusive_sums(core, own, other, chips):
    return pl.pallas_call(
        functools.partial(scan_kernel, chips=chips),
        name="exclusive_sums",
        in_specs=[SMEM, VMEM, VMEM],
        out_specs=VMEM,
        out_shape=jax.ShapeDtypeStruct(own.shape, BF16),
        compiler_params=PARAMS,
        cost_estimate=cost(own.size * 4, own.size * 6),
    )(core, own, other)


def within_kernel(q_hbm, k_hbm, v_hbm, q_ref, out_ref, k_ref, v_ref, sems):
    copies, split = [], CALLS[0][1] * DH
    parts = (slice(0, split), slice(split, HEADS * DH))
    for part, cols in enumerate(parts):
        for at, (hbm, ref) in enumerate(((q_hbm, q_ref), (k_hbm, k_ref), (v_hbm, v_ref))):
            copies.append(
                pltpu.make_async_copy(hbm.at[:, cols], ref.at[:, cols], sems.at[part, at])
            )
            copies[-1].start()
    causal = causal_mask()
    for part, (first, last) in enumerate(CALLS):
        for copy in copies[3 * part : 3 * part + 3]:
            copy.wait()
        for h in range(first, last):
            cols = slice(h * DH, (h + 1) * DH)
            top, bottom = within_block(q_ref, k_ref, v_ref, h, causal)
            out_ref[:HALF, cols] = top
            out_ref[HALF:, cols] = bottom


def within_all(q, k, v):
    shape = (BLK, HEADS * DH)
    return pl.pallas_call(
        within_kernel,
        name="within_all",
        in_specs=[HBM] * 3,
        out_specs=[VMEM, VMEM],
        out_shape=[pltpu.VMEM(shape, BF16), pltpu.VMEM(shape, F32)],
        scratch_shapes=[
            pltpu.VMEM(shape, BF16),
            pltpu.VMEM(shape, BF16),
            pltpu.SemaphoreType.DMA((2, 3)),
        ],
        compiler_params=PARAMS,
        cost_estimate=cost(4 * BLK * BLK * DH * HEADS, BLK * DH * HEADS * 10),
    )(in_hbm(q), in_hbm(k), in_hbm(v))


def finish_kernel(q_ref, within_ref, carried_ref, gain_ref, out_ref, *, first, last):
    for h in range(first, last):
        cols = slice(h * DH, (h + 1) * DH)
        out_cols = slice((h - first) * DH, (h - first + 1) * DH)
        out_ref[:, out_cols] = finish(
            q_ref[:, cols], within_ref[:, cols], carried_ref[cols, :], gain_ref[:, cols]
        )


def finish_heads(q, within, carried, gain, first, last):
    heads = last - first
    return pl.pallas_call(
        functools.partial(finish_kernel, first=first, last=last),
        name="finish_heads",
        in_specs=[VMEM] * 4,
        out_specs=VMEM,
        out_shape=jax.ShapeDtypeStruct((BLK, heads * DH), BF16),
        compiler_params=PARAMS,
        cost_estimate=cost(4 * BLK * DH * DH * heads, BLK * DH * heads * 8),
    )(q, within, carried, gain)


TILE = 256


def weight_rows(w_hbm, column_ref, shift):
    depth = HEADS * DH
    ways = w_hbm.shape[0] // depth
    source = lax.rem(column_ref[0] + (shift + ways), ways)
    return w_hbm.at[pl.ds(pl.multiple_of(source * depth, depth), depth)]


def own_kernel(column_ref, *refs):
    *a_refs, w_hbm, total_ref, w_ref, sems = refs
    source = weight_rows(w_hbm, column_ref, 0)
    copies, rows, at = [], [], 0
    for piece, a_ref in enumerate(a_refs):
        rows.append(slice(at, at + a_ref.shape[1]))
        at += a_ref.shape[1]
        copies.append(
            pltpu.make_async_copy(source.at[rows[-1]], w_ref.at[rows[-1]], sems.at[piece])
        )
        copies[-1].start()
    for piece, a_ref in enumerate(a_refs):
        copies[piece].wait()
        for tile in range(total_ref.shape[1] // TILE):
            cols = slice(tile * TILE, (tile + 1) * TILE)
            term = dot(a_ref[...], w_ref[rows[piece], cols], NN)
            total_ref[:, cols] = term if piece == 0 else total_ref[:, cols] + term


def own_mix(column, w, arrays):
    width, depth = w.shape[1], HEADS * DH
    return pl.pallas_call(
        own_kernel,
        name="own_mix",
        in_specs=[SMEM] + [VMEM] * len(arrays) + [HBM],
        out_specs=VMEM,
        out_shape=pltpu.VMEM((BLK, width), F32),
        scratch_shapes=[
            pltpu.VMEM((depth, width), BF16),
            pltpu.SemaphoreType.DMA((len(arrays),)),
        ],
        compiler_params=PARAMS,
        cost_estimate=cost(2 * BLK * depth * width, 2 * depth * width),
    )(column, *arrays, in_hbm(w))


def add_products(total_ref, out_ref, a_refs, w_ref, starts, cols):
    total = total_ref[:, cols]
    for a_ref, start in zip(a_refs, starts):
        total = total + dot(a_ref[...], w_ref[start : start + a_ref.shape[1], cols], NN)
    out_ref[:, cols] = total.astype(out_ref.dtype)


SIDES = (-1, 1, 2)


def side_kernel(column_ref, *refs, starts):
    *a_refs, w_hbm, total_ref, out_ref, w_ref, sems = refs
    depth = HEADS * DH
    copies = []
    for at, shift in enumerate(SIDES):
        rows = slice(at * depth, (at + 1) * depth)
        copies.append(
            pltpu.make_async_copy(
                weight_rows(w_hbm, column_ref, shift), w_ref.at[rows], sems.at[at]
            )
        )
        copies[-1].start()
    half = len(a_refs) // 2
    for side in range(2):
        copies[side].wait()
        mine = slice(side * half, (side + 1) * half)
        for tile in range(out_ref.shape[1] // TILE):
            cols = slice(tile * TILE, (tile + 1) * TILE)
            source = out_ref if side else total_ref
            add_products(source, out_ref, a_refs[mine], w_ref, starts[mine], cols)
    copies[2].wait()


def side_mix(column, w, starts, arrays, total):
    width, depth = w.shape[1], len(SIDES) * HEADS * DH
    return pl.pallas_call(
        functools.partial(side_kernel, starts=starts),
        name="side_mix",
        in_specs=[SMEM] + [VMEM] * len(arrays) + [HBM, VMEM],
        out_specs=[VMEM, VMEM],
        out_shape=[pltpu.VMEM((BLK, width), F32), pltpu.VMEM((depth, width), BF16)],
        scratch_shapes=[pltpu.SemaphoreType.DMA((len(SIDES),))],
        compiler_params=PARAMS,
        cost_estimate=cost(2 * BLK * depth * width, 2 * depth * width),
    )(column, *arrays, in_hbm(w), total)


def mix_kernel(*refs, count, starts, last):
    a_refs, (w_ref, total_ref), rest = refs[:count], refs[count : count + 2], refs[count + 2 :]
    if last:
        out_hbm, out_ref, sems = rest
    else:
        (out_ref,) = rest
    copies = []
    for tile in range(out_ref.shape[1] // TILE):
        cols = slice(tile * TILE, (tile + 1) * TILE)
        add_products(total_ref, out_ref, a_refs, w_ref, starts, cols)
        if last:
            copy = pltpu.make_async_copy(out_ref.at[:, cols], out_hbm.at[:, cols], sems.at[tile])
            copy.start()
            copies.append(copy)
    for copy in copies:
        copy.wait()


def mix(w, starts, arrays, total, last=False):
    width = w.shape[1]
    depth = sum(a.shape[1] for a in arrays)
    if last:
        out_shape = jax.ShapeDtypeStruct((BLK, width), BF16)
        scratch = [pltpu.VMEM((BLK, width), BF16), pltpu.SemaphoreType.DMA((width // TILE,))]
    else:
        out_shape, scratch = pltpu.VMEM((BLK, width), F32), []
    return pl.pallas_call(
        functools.partial(mix_kernel, count=len(arrays), starts=starts, last=last),
        name="mix",
        in_specs=[VMEM] * (len(arrays) + 2),
        out_specs=HBM if last else VMEM,
        out_shape=out_shape,
        scratch_shapes=scratch,
        compiler_params=PARAMS,
        cost_estimate=cost(2 * BLK * depth * width, 2 * depth * width),
    )(*arrays, w, total)


def along(value, shift, count):
    return lax.ppermute(value, "fsdp", [(i, (i + shift) % count) for i in range(count)])


def shards(q, k, v, gain, w):
    chips, ways = lax.axis_size("chip"), lax.axis_size("fsdp")
    core = lax.axis_index("core").reshape(1)
    column = lax.axis_index("fsdp").reshape(1)
    gain_row = gain.reshape(1, -1)
    states = block_states(k, v)
    own = lax.all_to_all(states, "chip", 0, 0, tiled=True)
    other = lax.ppermute(own, "core", [(0, 1), (1, 0)])
    sums = exclusive_sums(core, own, other, chips)
    carried = lax.all_to_all(sums, "chip", 0, 0, tiled=True)
    q, within = within_all(q, k, v)
    carried, q, within = lax.optimization_barrier((carried, q, within))
    (a0, a1), (b0, b1) = CALLS
    mine_a = finish_heads(q, within, carried, gain_row, a0, a1)
    mine_b = finish_heads(q, within, carried, gain_row, b0, b1)
    total = own_mix(column, w, [mine_a, mine_b])
    left_a, right_a, total = lax.optimization_barrier(
        (along(mine_a, 1, ways), along(mine_a, -1, ways), total)
    )
    far_a = along(left_a, 1, ways)
    left_b = along(mine_b, 1, ways)
    right_b = along(mine_b, -1, ways)
    far_b = along(right_b, -1, ways)
    depth = HEADS * DH
    at_a, at_b = a0 * DH, b0 * DH
    total, w = side_mix(column, w, (at_a, depth + at_a), [left_a, right_a], total)
    total = mix(w, (at_b, depth + at_b), [left_b, right_b], total)
    total = mix(w, (2 * depth + at_a,), [far_a], total)
    return mix(w, (2 * depth + at_b,), [far_b], total, True)


def solution(mesh):
    seq, fsdp = mesh.devices.shape
    fine = Mesh(mesh.devices.reshape(seq // CORES, CORES, fsdp), ("chip", "core", "fsdp"))
    rows = ("chip", "core")
    placed = (P(rows, "fsdp"), P(rows, "fsdp"), P(rows, "fsdp"), P("fsdp"), P(None, "fsdp"))
    return jax.shard_map(
        shards, mesh=fine, in_specs=placed, out_specs=P(rows, "fsdp"), check_vma=False
    )
```

```python
import functools

import jax
import jax.numpy as jnp
from jax import lax
from jax.experimental import pallas as pl
from jax.experimental.pallas import tpu as pltpu
from jax.sharding import Mesh
from jax.sharding import PartitionSpec as P

DH = 128
BLK = 512
HALF = BLK // 2
CORES = 2
HEADS = 8
CALLS = ((0, 4), (4, 8))
F32 = jnp.float32
BF16 = jnp.bfloat16
NN, NT, TN = ((1,), (0,)), ((1,), (1,)), ((0,), (0,))
SMEM = pl.BlockSpec(memory_space=pltpu.SMEM)
VMEM = pl.BlockSpec(memory_space=pltpu.VMEM)
HBM = pl.BlockSpec(memory_space=pltpu.HBM)
PARAMS = pltpu.CompilerParams(vmem_limit_bytes=20 * 2**20)


def dot(a, b, dims):
    return lax.dot_general(a, b, (dims, ((), ())), preferred_element_type=F32)


def in_vmem(value):
    return pltpu.with_memory_space_constraint(value, pltpu.VMEM)


def in_hbm(value):
    return pltpu.with_memory_space_constraint(value, pltpu.HBM)


def cost(flops, size):
    return pl.CostEstimate(flops=flops, bytes_accessed=size, transcendentals=0)


def within_block(q_ref, k_ref, v_ref, h, causal):
    cols = slice(h * DH, (h + 1) * DH)
    q0, q1 = q_ref[:HALF, cols], q_ref[HALF:, cols]
    k0, k1 = k_ref[:HALF, cols], k_ref[HALF:, cols]
    v0, v1 = v_ref[:HALF, cols], v_ref[HALF:, cols]
    s00 = jnp.where(causal, dot(q0, k0, NT), 0.0).astype(BF16)
    s10 = dot(q1, k0, NT).astype(BF16)
    s11 = jnp.where(causal, dot(q1, k1, NT), 0.0).astype(BF16)
    return dot(s00, v0, NN), dot(s10, v0, NN) + dot(s11, v1, NN)


def causal_mask():
    row = lax.broadcasted_iota(jnp.int32, (HALF, HALF), 0)
    col = lax.broadcasted_iota(jnp.int32, (HALF, HALF), 1)
    return col <= row


def finish(queries, within, state, gain):
    att = within + dot(queries, state, NN)
    mean = jnp.full((DH, DH), 1.0 / DH, BF16)
    mean_square = dot((att * att).astype(BF16), mean, NN)
    return (att * lax.rsqrt(mean_square + 1e-6) * gain).astype(BF16)


PARTS = 2


def state_kernel(k_hbm, v_hbm, out_ref, k_ref, v_ref, sems):
    width = k_ref.shape[1] // PARTS
    copies = []
    for part in range(PARTS):
        cols = slice(part * width, (part + 1) * width)
        for at, (hbm, ref) in enumerate(((k_hbm, k_ref), (v_hbm, v_ref))):
            copy = pltpu.make_async_copy(hbm.at[:, cols], ref.at[:, cols], sems.at[part, at])
            copy.start()
            copies.append(copy)
    for part in range(PARTS):
        copies[2 * part].wait()
        copies[2 * part + 1].wait()
        for h in range(part * width // DH, (part + 1) * width // DH):
            cols = slice(h * DH, (h + 1) * DH)
            out_ref[cols, :] = dot(k_ref[:, cols], v_ref[:, cols], TN).astype(BF16)


def block_states(k, v):
    width = k.shape[1]
    return pl.pallas_call(
        state_kernel,
        name="block_states",
        in_specs=[HBM, HBM],
        out_specs=VMEM,
        out_shape=jax.ShapeDtypeStruct((width, DH), BF16),
        scratch_shapes=[
            pltpu.VMEM(k.shape, BF16),
            pltpu.VMEM(v.shape, BF16),
            pltpu.SemaphoreType.DMA((PARTS, 2)),
        ],
        compiler_params=PARAMS,
        cost_estimate=cost(2 * BLK * DH * width, 2 * BLK * width * 2),
    )(in_hbm(k), in_hbm(v))


def scan_kernel(core_ref, own_ref, other_ref, out_ref, *, chips):
    rows = own_ref.shape[0] // chips
    second = (core_ref[0] == 1).astype(F32)
    before = jnp.zeros((rows, DH), F32)
    for chip in range(chips):
        at = slice(chip * rows, (chip + 1) * rows)
        other = other_ref[at, :].astype(F32)
        out_ref[at, :] = (before + second * other).astype(BF16)
        before = before + (own_ref[at, :].astype(F32) + other)


def exclusive_sums(core, own, other, chips):
    return pl.pallas_call(
        functools.partial(scan_kernel, chips=chips),
        name="exclusive_sums",
        in_specs=[SMEM, VMEM, VMEM],
        out_specs=VMEM,
        out_shape=jax.ShapeDtypeStruct(own.shape, BF16),
        compiler_params=PARAMS,
        cost_estimate=cost(own.size * 4, own.size * 6),
    )(core, own, other)


def within_kernel(q_hbm, k_hbm, v_hbm, q_ref, out_ref, k_ref, v_ref, sems):
    copies, split = [], CALLS[0][1] * DH
    parts = (slice(0, split), slice(split, HEADS * DH))
    for part, cols in enumerate(parts):
        for at, (hbm, ref) in enumerate(((q_hbm, q_ref), (k_hbm, k_ref), (v_hbm, v_ref))):
            copies.append(
                pltpu.make_async_copy(hbm.at[:, cols], ref.at[:, cols], sems.at[part, at])
            )
            copies[-1].start()
    causal = causal_mask()
    for part, (first, last) in enumerate(CALLS):
        for copy in copies[3 * part : 3 * part + 3]:
            copy.wait()
        for h in range(first, last):
            cols = slice(h * DH, (h + 1) * DH)
            top, bottom = within_block(q_ref, k_ref, v_ref, h, causal)
            out_ref[:HALF, cols] = top
            out_ref[HALF:, cols] = bottom


def within_all(q, k, v):
    shape = (BLK, HEADS * DH)
    return pl.pallas_call(
        within_kernel,
        name="within_all",
        in_specs=[HBM] * 3,
        out_specs=[VMEM, VMEM],
        out_shape=[pltpu.VMEM(shape, BF16), pltpu.VMEM(shape, F32)],
        scratch_shapes=[
            pltpu.VMEM(shape, BF16),
            pltpu.VMEM(shape, BF16),
            pltpu.SemaphoreType.DMA((2, 3)),
        ],
        compiler_params=PARAMS,
        cost_estimate=cost(4 * BLK * BLK * DH * HEADS, BLK * DH * HEADS * 10),
    )(in_hbm(q), in_hbm(k), in_hbm(v))


def finish_kernel(q_ref, within_ref, carried_ref, gain_ref, out_ref, *, first, last):
    for h in range(first, last):
        cols = slice(h * DH, (h + 1) * DH)
        out_cols = slice((h - first) * DH, (h - first + 1) * DH)
        out_ref[:, out_cols] = finish(
            q_ref[:, cols], within_ref[:, cols], carried_ref[cols, :], gain_ref[:, cols]
        )


def finish_heads(q, within, carried, gain, first, last):
    heads = last - first
    return pl.pallas_call(
        functools.partial(finish_kernel, first=first, last=last),
        name="finish_heads",
        in_specs=[VMEM] * 4,
        out_specs=VMEM,
        out_shape=jax.ShapeDtypeStruct((BLK, heads * DH), BF16),
        compiler_params=PARAMS,
        cost_estimate=cost(4 * BLK * DH * DH * heads, BLK * DH * heads * 8),
    )(q, within, carried, gain)


TILE = 256


def weight_rows(w_hbm, column_ref, shift):
    depth = HEADS * DH
    ways = w_hbm.shape[0] // depth
    source = lax.rem(column_ref[0] + (shift + ways), ways)
    return w_hbm.at[pl.ds(pl.multiple_of(source * depth, depth), depth)]


def own_kernel(column_ref, *refs):
    *a_refs, w_hbm, total_ref, w_ref, sems = refs
    source = weight_rows(w_hbm, column_ref, 0)
    copies, rows, at = [], [], 0
    for piece, a_ref in enumerate(a_refs):
        rows.append(slice(at, at + a_ref.shape[1]))
        at += a_ref.shape[1]
        copies.append(
            pltpu.make_async_copy(source.at[rows[-1]], w_ref.at[rows[-1]], sems.at[piece])
        )
        copies[-1].start()
    for piece, a_ref in enumerate(a_refs):
        copies[piece].wait()
        for tile in range(total_ref.shape[1] // TILE):
            cols = slice(tile * TILE, (tile + 1) * TILE)
            term = dot(a_ref[...], w_ref[rows[piece], cols], NN)
            total_ref[:, cols] = term if piece == 0 else total_ref[:, cols] + term


def own_mix(column, w, arrays):
    width, depth = w.shape[1], HEADS * DH
    return pl.pallas_call(
        own_kernel,
        name="own_mix",
        in_specs=[SMEM] + [VMEM] * len(arrays) + [HBM],
        out_specs=VMEM,
        out_shape=pltpu.VMEM((BLK, width), F32),
        scratch_shapes=[
            pltpu.VMEM((depth, width), BF16),
            pltpu.SemaphoreType.DMA((len(arrays),)),
        ],
        compiler_params=PARAMS,
        cost_estimate=cost(2 * BLK * depth * width, 2 * depth * width),
    )(column, *arrays, in_hbm(w))


def add_products(total_ref, out_ref, a_refs, w_ref, starts, cols):
    total = total_ref[:, cols]
    for a_ref, start in zip(a_refs, starts):
        total = total + dot(a_ref[...], w_ref[start : start + a_ref.shape[1], cols], NN)
    out_ref[:, cols] = total.astype(out_ref.dtype)


SIDES = (-1, 1, 2)


def side_kernel(column_ref, *refs, starts):
    *a_refs, w_hbm, total_ref, out_ref, w_ref, sems = refs
    depth = HEADS * DH
    copies = []
    for at, shift in enumerate(SIDES):
        rows = slice(at * depth, (at + 1) * depth)
        copies.append(
            pltpu.make_async_copy(
                weight_rows(w_hbm, column_ref, shift), w_ref.at[rows], sems.at[at]
            )
        )
        copies[-1].start()
    half = len(a_refs) // 2
    for side in range(2):
        copies[side].wait()
        mine = slice(side * half, (side + 1) * half)
        for tile in range(out_ref.shape[1] // TILE):
            cols = slice(tile * TILE, (tile + 1) * TILE)
            source = out_ref if side else total_ref
            add_products(source, out_ref, a_refs[mine], w_ref, starts[mine], cols)
    copies[2].wait()


def side_mix(column, w, starts, arrays, total):
    width, depth = w.shape[1], len(SIDES) * HEADS * DH
    return pl.pallas_call(
        functools.partial(side_kernel, starts=starts),
        name="side_mix",
        in_specs=[SMEM] + [VMEM] * len(arrays) + [HBM, VMEM],
        out_specs=[VMEM, VMEM],
        out_shape=[pltpu.VMEM((BLK, width), F32), pltpu.VMEM((depth, width), BF16)],
        scratch_shapes=[pltpu.SemaphoreType.DMA((len(SIDES),))],
        compiler_params=PARAMS,
        cost_estimate=cost(2 * BLK * depth * width, 2 * depth * width),
    )(column, *arrays, in_hbm(w), total)


def mix_kernel(*refs, count, starts, last):
    a_refs, (w_ref, total_ref), rest = refs[:count], refs[count : count + 2], refs[count + 2 :]
    if last:
        out_hbm, out_ref, sems = rest
    else:
        (out_ref,) = rest
    copies = []
    for tile in range(out_ref.shape[1] // TILE):
        cols = slice(tile * TILE, (tile + 1) * TILE)
        add_products(total_ref, out_ref, a_refs, w_ref, starts, cols)
        if last:
            copy = pltpu.make_async_copy(out_ref.at[:, cols], out_hbm.at[:, cols], sems.at[tile])
            copy.start()
            copies.append(copy)
    for copy in copies:
        copy.wait()


def mix(w, starts, arrays, total, last=False):
    width = w.shape[1]
    depth = sum(a.shape[1] for a in arrays)
    if last:
        out_shape = jax.ShapeDtypeStruct((BLK, width), BF16)
        scratch = [pltpu.VMEM((BLK, width), BF16), pltpu.SemaphoreType.DMA((width // TILE,))]
    else:
        out_shape, scratch = pltpu.VMEM((BLK, width), F32), []
    return pl.pallas_call(
        functools.partial(mix_kernel, count=len(arrays), starts=starts, last=last),
        name="mix",
        in_specs=[VMEM] * (len(arrays) + 2),
        out_specs=HBM if last else VMEM,
        out_shape=out_shape,
        scratch_shapes=scratch,
        compiler_params=PARAMS,
        cost_estimate=cost(2 * BLK * depth * width, 2 * depth * width),
    )(*arrays, w, total)


def along(value, shift, count):
    return lax.ppermute(value, "fsdp", [(i, (i + shift) % count) for i in range(count)])


def shards(q, k, v, gain, w):
    chips, ways = lax.axis_size("chip"), lax.axis_size("fsdp")
    core = lax.axis_index("core").reshape(1)
    column = lax.axis_index("fsdp").reshape(1)
    gain_row = gain.reshape(1, -1)
    states = block_states(k, v)
    own = lax.all_to_all(states, "chip", 0, 0, tiled=True)
    other = lax.ppermute(own, "core", [(0, 1), (1, 0)])
    sums = exclusive_sums(core, own, other, chips)
    carried = lax.all_to_all(sums, "chip", 0, 0, tiled=True)
    q, within = within_all(q, k, v)
    carried, q, within = lax.optimization_barrier((carried, q, within))
    heads = (0, 2, 4, 6)
    mine = [finish_heads(q, within, carried, gain_row, h, h + 2) for h in heads]
    left = [along(value, 1, ways) for value in mine]
    right = [along(value, -1, ways) for value in mine]
    total = own_mix(column, w, mine)
    left[0], right[1], total = lax.optimization_barrier((left[0], right[1], total))
    far = [
        along(left[0], 1, ways),
        along(right[1], -1, ways),
        along(left[2], 1, ways),
        along(right[3], -1, ways),
    ]
    depth = HEADS * DH
    at = [h * DH for h in heads]
    side = [depth + start for start in at]
    across = [2 * depth + start for start in at]
    total, w = side_mix(column, w, (*at[:2], *side[:2]), left[:2] + right[:2], total)
    total = mix(w, (*at[2:], *side[2:]), left[2:] + right[2:], total)
    total = mix(w, tuple(across[:2]), far[:2], total)
    return mix(w, tuple(across[2:]), far[2:], total, True)


def solution(mesh):
    seq, fsdp = mesh.devices.shape
    fine = Mesh(mesh.devices.reshape(seq // CORES, CORES, fsdp), ("chip", "core", "fsdp"))
    rows = ("chip", "core")
    placed = (P(rows, "fsdp"), P(rows, "fsdp"), P(rows, "fsdp"), P("fsdp"), P(None, "fsdp"))
    return jax.shard_map(
        shards, mesh=fine, in_specs=placed, out_specs=P(rows, "fsdp"), check_vma=False
    )
```

```python
import functools

import jax
import jax.numpy as jnp
from jax import lax
from jax.experimental import pallas as pl
from jax.experimental.pallas import tpu as pltpu
from jax.sharding import Mesh
from jax.sharding import PartitionSpec as P

DH = 128
BLK = 512
HALF = BLK // 2
CORES = 2
HEADS = 8
CALLS = ((0, 4), (4, 8))
F32 = jnp.float32
BF16 = jnp.bfloat16
NN, NT, TN = ((1,), (0,)), ((1,), (1,)), ((0,), (0,))
SMEM = pl.BlockSpec(memory_space=pltpu.SMEM)
VMEM = pl.BlockSpec(memory_space=pltpu.VMEM)
HBM = pl.BlockSpec(memory_space=pltpu.HBM)
PARAMS = pltpu.CompilerParams(vmem_limit_bytes=20 * 2**20)


def dot(a, b, dims):
    return lax.dot_general(a, b, (dims, ((), ())), preferred_element_type=F32)


def in_vmem(value):
    return pltpu.with_memory_space_constraint(value, pltpu.VMEM)


def in_hbm(value):
    return pltpu.with_memory_space_constraint(value, pltpu.HBM)


def cost(flops, size):
    return pl.CostEstimate(flops=flops, bytes_accessed=size, transcendentals=0)


def within_block(q_ref, k_ref, v_ref, h, causal):
    cols = slice(h * DH, (h + 1) * DH)
    q0, q1 = q_ref[:HALF, cols], q_ref[HALF:, cols]
    k0, k1 = k_ref[:HALF, cols], k_ref[HALF:, cols]
    v0, v1 = v_ref[:HALF, cols], v_ref[HALF:, cols]
    s00 = jnp.where(causal, dot(q0, k0, NT), 0.0).astype(BF16)
    s10 = dot(q1, k0, NT).astype(BF16)
    s11 = jnp.where(causal, dot(q1, k1, NT), 0.0).astype(BF16)
    return dot(s00, v0, NN), dot(s10, v0, NN) + dot(s11, v1, NN)


def causal_mask():
    row = lax.broadcasted_iota(jnp.int32, (HALF, HALF), 0)
    col = lax.broadcasted_iota(jnp.int32, (HALF, HALF), 1)
    return col <= row


def finish(queries, within, state, gain):
    att = within + dot(queries, state, NN)
    mean = jnp.full((DH, DH), 1.0 / DH, BF16)
    mean_square = dot((att * att).astype(BF16), mean, NN)
    return (att * lax.rsqrt(mean_square + 1e-6) * gain).astype(BF16)


PARTS = 2


def state_kernel(k_hbm, v_hbm, out_ref, k_ref, v_ref, sems):
    width = k_ref.shape[1] // PARTS
    copies = []
    for part in range(PARTS):
        cols = slice(part * width, (part + 1) * width)
        for at, (hbm, ref) in enumerate(((k_hbm, k_ref), (v_hbm, v_ref))):
            copy = pltpu.make_async_copy(hbm.at[:, cols], ref.at[:, cols], sems.at[part, at])
            copy.start()
            copies.append(copy)
    for part in range(PARTS):
        copies[2 * part].wait()
        copies[2 * part + 1].wait()
        for h in range(part * width // DH, (part + 1) * width // DH):
            cols = slice(h * DH, (h + 1) * DH)
            out_ref[cols, :] = dot(k_ref[:, cols], v_ref[:, cols], TN).astype(BF16)


def block_states(k, v):
    width = k.shape[1]
    return pl.pallas_call(
        state_kernel,
        name="block_states",
        in_specs=[HBM, HBM],
        out_specs=VMEM,
        out_shape=jax.ShapeDtypeStruct((width, DH), BF16),
        scratch_shapes=[
            pltpu.VMEM(k.shape, BF16),
            pltpu.VMEM(v.shape, BF16),
            pltpu.SemaphoreType.DMA((PARTS, 2)),
        ],
        compiler_params=PARAMS,
        cost_estimate=cost(2 * BLK * DH * width, 2 * BLK * width * 2),
    )(in_hbm(k), in_hbm(v))


def scan_kernel(core_ref, own_ref, other_ref, out_ref, *, chips):
    rows = own_ref.shape[0] // chips
    second = (core_ref[0] == 1).astype(F32)
    before = jnp.zeros((rows, DH), F32)
    for chip in range(chips):
        at = slice(chip * rows, (chip + 1) * rows)
        other = other_ref[at, :].astype(F32)
        out_ref[at, :] = (before + second * other).astype(BF16)
        before = before + (own_ref[at, :].astype(F32) + other)


def exclusive_sums(core, own, other, chips):
    return pl.pallas_call(
        functools.partial(scan_kernel, chips=chips),
        name="exclusive_sums",
        in_specs=[SMEM, VMEM, VMEM],
        out_specs=VMEM,
        out_shape=jax.ShapeDtypeStruct(own.shape, BF16),
        compiler_params=PARAMS,
        cost_estimate=cost(own.size * 4, own.size * 6),
    )(core, own, other)


def within_kernel(q_hbm, k_hbm, v_hbm, qa_ref, a_ref, b_hbm, q_ref, k_ref, v_ref, b_ref, sems):
    copies, split = [], CALLS[0][1] * DH
    parts = (slice(0, split), slice(split, HEADS * DH))
    for part, cols in enumerate(parts):
        q_part = qa_ref if part == 0 else q_ref
        sources = (q_hbm.at[:, cols], k_hbm.at[:, cols], v_hbm.at[:, cols])
        targets = (q_part, k_ref.at[part], v_ref.at[part])
        for at, (source, target) in enumerate(zip(sources, targets)):
            copies.append(pltpu.make_async_copy(source, target, sems.at[part, at]))
            copies[-1].start()
    causal = causal_mask()
    for part, (first, last) in enumerate(CALLS):
        for copy in copies[3 * part : 3 * part + 3]:
            copy.wait()
        q_part, out_ref = (qa_ref, a_ref) if part == 0 else (q_ref, b_ref)
        for h in range(last - first):
            cols = slice(h * DH, (h + 1) * DH)
            top, bottom = within_block(q_part, k_ref.at[part], v_ref.at[part], h, causal)
            out_ref[:HALF, cols] = top
            out_ref[HALF:, cols] = bottom
    copy = pltpu.make_async_copy(b_ref, b_hbm, sems.at[0, 0])
    copy.start()
    copy.wait()


def within_all(q, k, v):
    shape = (BLK, HEADS // 2 * DH)
    return pl.pallas_call(
        within_kernel,
        name="within_all",
        in_specs=[HBM] * 3,
        out_specs=[VMEM, VMEM, HBM],
        out_shape=[
            pltpu.VMEM(shape, BF16),
            pltpu.VMEM(shape, F32),
            jax.ShapeDtypeStruct(shape, F32),
        ],
        scratch_shapes=[
            pltpu.VMEM(shape, BF16),
            pltpu.VMEM((2, *shape), BF16),
            pltpu.VMEM((2, *shape), BF16),
            pltpu.VMEM(shape, F32),
            pltpu.SemaphoreType.DMA((2, 3)),
        ],
        compiler_params=PARAMS,
        cost_estimate=cost(4 * BLK * BLK * DH * HEADS, BLK * DH * HEADS * 10),
    )(in_hbm(q), in_hbm(k), in_hbm(v))


def finish_kernel(q_ref, within_ref, carried_ref, gain_ref, out_ref, *scratch, first, last):
    if scratch:
        q_hbm, within_hbm = q_ref.at[:, first * DH : last * DH], within_ref
        q_ref, within_ref, sems = scratch
        copies = [
            pltpu.make_async_copy(q_hbm, q_ref, sems.at[0]),
            pltpu.make_async_copy(within_hbm, within_ref, sems.at[1]),
        ]
        for copy in copies:
            copy.start()
        for copy in copies:
            copy.wait()
    for h in range(first, last):
        cols = slice(h * DH, (h + 1) * DH)
        out_cols = slice((h - first) * DH, (h - first + 1) * DH)
        out_ref[:, out_cols] = finish(
            q_ref[:, out_cols], within_ref[:, out_cols], carried_ref[cols, :], gain_ref[:, cols]
        )


def finish_heads(q, within, carried, gain, first, last, fetch=False):
    heads = last - first
    shape = (BLK, heads * DH)
    scratch = [pltpu.VMEM(shape, BF16), pltpu.VMEM(shape, F32), pltpu.SemaphoreType.DMA((2,))]
    if fetch:
        q, within = in_hbm(q), in_hbm(within)
    return pl.pallas_call(
        functools.partial(finish_kernel, first=first, last=last),
        name="finish_heads",
        in_specs=[HBM if fetch else VMEM] * 2 + [VMEM] * 2,
        out_specs=VMEM,
        out_shape=jax.ShapeDtypeStruct(shape, BF16),
        scratch_shapes=scratch if fetch else [],
        compiler_params=PARAMS,
        cost_estimate=cost(4 * BLK * DH * DH * heads, BLK * DH * heads * 8),
    )(q, within, carried, gain)


TILE = 256


def weight_rows(w_hbm, column_ref, shift):
    depth = HEADS * DH
    ways = w_hbm.shape[0] // depth
    source = lax.rem(column_ref[0] + (shift + ways), ways)
    return w_hbm.at[pl.ds(pl.multiple_of(source * depth, depth), depth)]


def own_kernel(column_ref, *refs):
    *a_refs, w_hbm, total_ref, w_ref, sems = refs
    source = weight_rows(w_hbm, column_ref, 0)
    copies, rows, at = [], [], 0
    for piece, a_ref in enumerate(a_refs):
        rows.append(slice(at, at + a_ref.shape[1]))
        at += a_ref.shape[1]
        copies.append(
            pltpu.make_async_copy(source.at[rows[-1]], w_ref.at[rows[-1]], sems.at[piece])
        )
        copies[-1].start()
    for piece, a_ref in enumerate(a_refs):
        copies[piece].wait()
        for tile in range(total_ref.shape[1] // TILE):
            cols = slice(tile * TILE, (tile + 1) * TILE)
            term = dot(a_ref[...], w_ref[rows[piece], cols], NN)
            total_ref[:, cols] = term if piece == 0 else total_ref[:, cols] + term


def own_mix(column, w, arrays):
    width, depth = w.shape[1], HEADS * DH
    return pl.pallas_call(
        own_kernel,
        name="own_mix",
        in_specs=[SMEM] + [VMEM] * len(arrays) + [HBM],
        out_specs=VMEM,
        out_shape=pltpu.VMEM((BLK, width), F32),
        scratch_shapes=[
            pltpu.VMEM((depth, width), BF16),
            pltpu.SemaphoreType.DMA((len(arrays),)),
        ],
        compiler_params=PARAMS,
        cost_estimate=cost(2 * BLK * depth * width, 2 * depth * width),
    )(column, *arrays, in_hbm(w))


def add_products(total_ref, out_ref, a_refs, w_ref, starts, cols):
    total = total_ref[:, cols]
    for a_ref, start in zip(a_refs, starts):
        total = total + dot(a_ref[...], w_ref[start : start + a_ref.shape[1], cols], NN)
    out_ref[:, cols] = total.astype(out_ref.dtype)


SIDES = (-1, 1, 2)


def side_kernel(column_ref, *refs, starts):
    *a_refs, w_hbm, total_ref, out_ref, w_ref, sems = refs
    depth = HEADS * DH
    copies = []
    for at, shift in enumerate(SIDES):
        rows = slice(at * depth, (at + 1) * depth)
        copies.append(
            pltpu.make_async_copy(
                weight_rows(w_hbm, column_ref, shift), w_ref.at[rows], sems.at[at]
            )
        )
        copies[-1].start()
    half = len(a_refs) // 2
    for side in range(2):
        copies[side].wait()
        mine = slice(side * half, (side + 1) * half)
        for tile in range(out_ref.shape[1] // TILE):
            cols = slice(tile * TILE, (tile + 1) * TILE)
            source = out_ref if side else total_ref
            add_products(source, out_ref, a_refs[mine], w_ref, starts[mine], cols)
    copies[2].wait()


def side_mix(column, w, starts, arrays, total):
    width, depth = w.shape[1], len(SIDES) * HEADS * DH
    return pl.pallas_call(
        functools.partial(side_kernel, starts=starts),
        name="side_mix",
        in_specs=[SMEM] + [VMEM] * len(arrays) + [HBM, VMEM],
        out_specs=[VMEM, VMEM],
        out_shape=[pltpu.VMEM((BLK, width), F32), pltpu.VMEM((depth, width), BF16)],
        scratch_shapes=[pltpu.SemaphoreType.DMA((len(SIDES),))],
        compiler_params=PARAMS,
        cost_estimate=cost(2 * BLK * depth * width, 2 * depth * width),
    )(column, *arrays, in_hbm(w), total)


def mix_kernel(*refs, count, starts, last):
    a_refs, (w_ref, total_ref), rest = refs[:count], refs[count : count + 2], refs[count + 2 :]
    if last:
        out_hbm, out_ref, sems = rest
    else:
        (out_ref,) = rest
    copies = []
    for tile in range(out_ref.shape[1] // TILE):
        cols = slice(tile * TILE, (tile + 1) * TILE)
        add_products(total_ref, out_ref, a_refs, w_ref, starts, cols)
        if last:
            copy = pltpu.make_async_copy(out_ref.at[:, cols], out_hbm.at[:, cols], sems.at[tile])
            copy.start()
            copies.append(copy)
    for copy in copies:
        copy.wait()


def mix(w, starts, arrays, total, last=False):
    width = w.shape[1]
    depth = sum(a.shape[1] for a in arrays)
    if last:
        out_shape = jax.ShapeDtypeStruct((BLK, width), BF16)
        scratch = [pltpu.VMEM((BLK, width), BF16), pltpu.SemaphoreType.DMA((width // TILE,))]
    else:
        out_shape, scratch = pltpu.VMEM((BLK, width), F32), []
    return pl.pallas_call(
        functools.partial(mix_kernel, count=len(arrays), starts=starts, last=last),
        name="mix",
        in_specs=[VMEM] * (len(arrays) + 2),
        out_specs=HBM if last else VMEM,
        out_shape=out_shape,
        scratch_shapes=scratch,
        compiler_params=PARAMS,
        cost_estimate=cost(2 * BLK * depth * width, 2 * depth * width),
    )(*arrays, w, total)


def along(value, shift, count):
    return lax.ppermute(value, "fsdp", [(i, (i + shift) % count) for i in range(count)])


def shards(q, k, v, gain, w):
    chips, ways = lax.axis_size("chip"), lax.axis_size("fsdp")
    core = lax.axis_index("core").reshape(1)
    column = lax.axis_index("fsdp").reshape(1)
    gain_row = gain.reshape(1, -1)
    states = block_states(k, v)
    own = lax.all_to_all(states, "chip", 0, 0, tiled=True)
    other = lax.ppermute(own, "core", [(0, 1), (1, 0)])
    sums = exclusive_sums(core, own, other, chips)
    carried = lax.all_to_all(sums, "chip", 0, 0, tiled=True)
    q_a, within_a, within_b = within_all(q, k, v)
    carried, q_a, within_a, within_b = lax.optimization_barrier(
        (carried, q_a, within_a, within_b)
    )
    (a0, a1), (b0, b1) = CALLS
    mine_a = finish_heads(q_a, within_a, carried, gain_row, a0, a1)
    mine_b = finish_heads(q, within_b, carried, gain_row, b0, b1, True)
    total = own_mix(column, w, [mine_a, mine_b])
    left_a, right_a, total = lax.optimization_barrier(
        (along(mine_a, 1, ways), along(mine_a, -1, ways), total)
    )
    far_a = along(left_a, 1, ways)
    left_b = along(mine_b, 1, ways)
    right_b = along(mine_b, -1, ways)
    far_b = along(right_b, -1, ways)
    depth = HEADS * DH
    at_a, at_b = a0 * DH, b0 * DH
    total, w = side_mix(column, w, (at_a, depth + at_a), [left_a, right_a], total)
    total = mix(w, (at_b, depth + at_b), [left_b, right_b], total)
    total = mix(w, (2 * depth + at_a,), [far_a], total)
    return mix(w, (2 * depth + at_b,), [far_b], total, True)


def solution(mesh):
    seq, fsdp = mesh.devices.shape
    fine = Mesh(mesh.devices.reshape(seq // CORES, CORES, fsdp), ("chip", "core", "fsdp"))
    rows = ("chip", "core")
    placed = (P(rows, "fsdp"), P(rows, "fsdp"), P(rows, "fsdp"), P("fsdp"), P(None, "fsdp"))
    return jax.shard_map(
        shards, mesh=fine, in_specs=placed, out_specs=P(rows, "fsdp"), check_vma=False
    )
```

```python
import functools

import jax
import jax.numpy as jnp
from jax import lax
from jax.experimental import pallas as pl
from jax.experimental.pallas import tpu as pltpu
from jax.sharding import Mesh
from jax.sharding import PartitionSpec as P

DH = 128
BLK = 512
HALF = BLK // 2
CORES = 2
HEADS = 8
CALLS = ((0, 4), (4, 8))
F32 = jnp.float32
BF16 = jnp.bfloat16
NN, NT, TN = ((1,), (0,)), ((1,), (1,)), ((0,), (0,))
SMEM = pl.BlockSpec(memory_space=pltpu.SMEM)
VMEM = pl.BlockSpec(memory_space=pltpu.VMEM)
HBM = pl.BlockSpec(memory_space=pltpu.HBM)
PARAMS = pltpu.CompilerParams(vmem_limit_bytes=20 * 2**20)


def dot(a, b, dims):
    return lax.dot_general(a, b, (dims, ((), ())), preferred_element_type=F32)


def in_vmem(value):
    return pltpu.with_memory_space_constraint(value, pltpu.VMEM)


def in_hbm(value):
    return pltpu.with_memory_space_constraint(value, pltpu.HBM)


def cost(flops, size):
    return pl.CostEstimate(flops=flops, bytes_accessed=size, transcendentals=0)


def within_block(q_ref, k_ref, v_ref, h, causal):
    cols = slice(h * DH, (h + 1) * DH)
    q0, q1 = q_ref[:HALF, cols], q_ref[HALF:, cols]
    k0, k1 = k_ref[:HALF, cols], k_ref[HALF:, cols]
    v0, v1 = v_ref[:HALF, cols], v_ref[HALF:, cols]
    s00 = jnp.where(causal, dot(q0, k0, NT), 0.0).astype(BF16)
    s10 = dot(q1, k0, NT).astype(BF16)
    s11 = jnp.where(causal, dot(q1, k1, NT), 0.0).astype(BF16)
    return dot(s00, v0, NN), dot(s10, v0, NN) + dot(s11, v1, NN)


def causal_mask():
    row = lax.broadcasted_iota(jnp.int32, (HALF, HALF), 0)
    col = lax.broadcasted_iota(jnp.int32, (HALF, HALF), 1)
    return col <= row


def finish(queries, within, state, gain):
    att = within + dot(queries, state, NN)
    mean = jnp.full((DH, DH), 1.0 / DH, BF16)
    mean_square = dot((att * att).astype(BF16), mean, NN)
    return (att * lax.rsqrt(mean_square + 1e-6) * gain).astype(BF16)


PARTS = 4


def state_kernel(k_hbm, v_hbm, out_ref, k_ref, v_ref, sems):
    width = k_ref.shape[1] // PARTS
    copies = []
    for part in range(PARTS):
        cols = slice(part * width, (part + 1) * width)
        for at, (hbm, ref) in enumerate(((k_hbm, k_ref), (v_hbm, v_ref))):
            copy = pltpu.make_async_copy(hbm.at[:, cols], ref.at[:, cols], sems.at[part, at])
            copy.start()
            copies.append(copy)
    for part in range(PARTS):
        copies[2 * part].wait()
        copies[2 * part + 1].wait()
        for h in range(part * width // DH, (part + 1) * width // DH):
            cols = slice(h * DH, (h + 1) * DH)
            out_ref[cols, :] = dot(k_ref[:, cols], v_ref[:, cols], TN).astype(BF16)


def block_states(k, v):
    width = k.shape[1]
    return pl.pallas_call(
        state_kernel,
        name="block_states",
        in_specs=[HBM, HBM],
        out_specs=VMEM,
        out_shape=jax.ShapeDtypeStruct((width, DH), BF16),
        scratch_shapes=[
            pltpu.VMEM(k.shape, BF16),
            pltpu.VMEM(v.shape, BF16),
            pltpu.SemaphoreType.DMA((PARTS, 2)),
        ],
        compiler_params=PARAMS,
        cost_estimate=cost(2 * BLK * DH * width, 2 * BLK * width * 2),
    )(in_hbm(k), in_hbm(v))


def scan_kernel(core_ref, own_ref, other_ref, out_ref, *, chips):
    rows = own_ref.shape[0] // chips
    second = (core_ref[0] == 1).astype(F32)
    before = jnp.zeros((rows, DH), F32)
    for chip in range(chips):
        at = slice(chip * rows, (chip + 1) * rows)
        other = other_ref[at, :].astype(F32)
        out_ref[at, :] = (before + second * other).astype(BF16)
        before = before + (own_ref[at, :].astype(F32) + other)


def exclusive_sums(core, own, other, chips):
    return pl.pallas_call(
        functools.partial(scan_kernel, chips=chips),
        name="exclusive_sums",
        in_specs=[SMEM, VMEM, VMEM],
        out_specs=VMEM,
        out_shape=jax.ShapeDtypeStruct(own.shape, BF16),
        compiler_params=PARAMS,
        cost_estimate=cost(own.size * 4, own.size * 6),
    )(core, own, other)


def within_kernel(q_hbm, k_hbm, v_hbm, qa_ref, a_ref, b_hbm, q_ref, k_ref, v_ref, b_ref, sems):
    copies, split = [], CALLS[0][1] * DH
    parts = (slice(0, split), slice(split, HEADS * DH))
    for part, cols in enumerate(parts):
        q_part = qa_ref if part == 0 else q_ref
        sources = (q_hbm.at[:, cols], k_hbm.at[:, cols], v_hbm.at[:, cols])
        targets = (q_part, k_ref.at[part], v_ref.at[part])
        for at, (source, target) in enumerate(zip(sources, targets)):
            copies.append(pltpu.make_async_copy(source, target, sems.at[part, at]))
            copies[-1].start()
    causal = causal_mask()
    for part, (first, last) in enumerate(CALLS):
        for copy in copies[3 * part : 3 * part + 3]:
            copy.wait()
        q_part, out_ref = (qa_ref, a_ref) if part == 0 else (q_ref, b_ref)
        for h in range(last - first):
            cols = slice(h * DH, (h + 1) * DH)
            top, bottom = within_block(q_part, k_ref.at[part], v_ref.at[part], h, causal)
            out_ref[:HALF, cols] = top
            out_ref[HALF:, cols] = bottom
    copy = pltpu.make_async_copy(b_ref, b_hbm, sems.at[0, 0])
    copy.start()
    copy.wait()


def within_all(q, k, v):
    shape = (BLK, HEADS // 2 * DH)
    return pl.pallas_call(
        within_kernel,
        name="within_all",
        in_specs=[HBM] * 3,
        out_specs=[VMEM, VMEM, HBM],
        out_shape=[
            pltpu.VMEM(shape, BF16),
            pltpu.VMEM(shape, F32),
            jax.ShapeDtypeStruct(shape, F32),
        ],
        scratch_shapes=[
            pltpu.VMEM(shape, BF16),
            pltpu.VMEM((2, *shape), BF16),
            pltpu.VMEM((2, *shape), BF16),
            pltpu.VMEM(shape, F32),
            pltpu.SemaphoreType.DMA((2, 3)),
        ],
        compiler_params=PARAMS,
        cost_estimate=cost(4 * BLK * BLK * DH * HEADS, BLK * DH * HEADS * 10),
    )(in_hbm(q), in_hbm(k), in_hbm(v))


def finish_kernel(q_ref, within_ref, carried_ref, gain_ref, out_ref, *scratch, first, last):
    if scratch:
        q_hbm, within_hbm = q_ref.at[:, first * DH : last * DH], within_ref
        q_ref, within_ref, sems = scratch
        copies = [
            pltpu.make_async_copy(q_hbm, q_ref, sems.at[0]),
            pltpu.make_async_copy(within_hbm, within_ref, sems.at[1]),
        ]
        for copy in copies:
            copy.start()
        for copy in copies:
            copy.wait()
    for h in range(first, last):
        cols = slice(h * DH, (h + 1) * DH)
        out_cols = slice((h - first) * DH, (h - first + 1) * DH)
        out_ref[:, out_cols] = finish(
            q_ref[:, out_cols], within_ref[:, out_cols], carried_ref[cols, :], gain_ref[:, cols]
        )


def finish_heads(q, within, carried, gain, first, last, fetch=False):
    heads = last - first
    shape = (BLK, heads * DH)
    scratch = [pltpu.VMEM(shape, BF16), pltpu.VMEM(shape, F32), pltpu.SemaphoreType.DMA((2,))]
    if fetch:
        q, within = in_hbm(q), in_hbm(within)
    return pl.pallas_call(
        functools.partial(finish_kernel, first=first, last=last),
        name="finish_heads",
        in_specs=[HBM if fetch else VMEM] * 2 + [VMEM] * 2,
        out_specs=VMEM,
        out_shape=jax.ShapeDtypeStruct(shape, BF16),
        scratch_shapes=scratch if fetch else [],
        compiler_params=PARAMS,
        cost_estimate=cost(4 * BLK * DH * DH * heads, BLK * DH * heads * 8),
    )(q, within, carried, gain)


TILE = 256


def weight_rows(w_hbm, column_ref, shift):
    depth = HEADS * DH
    ways = w_hbm.shape[0] // depth
    source = lax.rem(column_ref[0] + (shift + ways), ways)
    return w_hbm.at[pl.ds(pl.multiple_of(source * depth, depth), depth)]


def own_kernel(column_ref, *refs):
    *a_refs, w_hbm, total_ref, w_ref, sems = refs
    source = weight_rows(w_hbm, column_ref, 0)
    copies, rows, at = [], [], 0
    for piece, a_ref in enumerate(a_refs):
        rows.append(slice(at, at + a_ref.shape[1]))
        at += a_ref.shape[1]
        copies.append(
            pltpu.make_async_copy(source.at[rows[-1]], w_ref.at[rows[-1]], sems.at[piece])
        )
        copies[-1].start()
    for piece, a_ref in enumerate(a_refs):
        copies[piece].wait()
        for tile in range(total_ref.shape[1] // TILE):
            cols = slice(tile * TILE, (tile + 1) * TILE)
            term = dot(a_ref[...], w_ref[rows[piece], cols], NN)
            total_ref[:, cols] = term if piece == 0 else total_ref[:, cols] + term


def own_mix(column, w, arrays):
    width, depth = w.shape[1], HEADS * DH
    return pl.pallas_call(
        own_kernel,
        name="own_mix",
        in_specs=[SMEM] + [VMEM] * len(arrays) + [HBM],
        out_specs=VMEM,
        out_shape=pltpu.VMEM((BLK, width), F32),
        scratch_shapes=[
            pltpu.VMEM((depth, width), BF16),
            pltpu.SemaphoreType.DMA((len(arrays),)),
        ],
        compiler_params=PARAMS,
        cost_estimate=cost(2 * BLK * depth * width, 2 * depth * width),
    )(column, *arrays, in_hbm(w))


def add_products(total_ref, out_ref, a_refs, w_ref, starts, cols):
    total = total_ref[:, cols]
    for a_ref, start in zip(a_refs, starts):
        total = total + dot(a_ref[...], w_ref[start : start + a_ref.shape[1], cols], NN)
    out_ref[:, cols] = total.astype(out_ref.dtype)


SIDES = (-1, 1, 2)


def side_kernel(column_ref, *refs, starts):
    *a_refs, w_hbm, total_ref, out_ref, w_ref, sems = refs
    depth = HEADS * DH
    copies = []
    for at, shift in enumerate(SIDES):
        rows = slice(at * depth, (at + 1) * depth)
        copies.append(
            pltpu.make_async_copy(
                weight_rows(w_hbm, column_ref, shift), w_ref.at[rows], sems.at[at]
            )
        )
        copies[-1].start()
    half = len(a_refs) // 2
    for side in range(2):
        copies[side].wait()
        mine = slice(side * half, (side + 1) * half)
        for tile in range(out_ref.shape[1] // TILE):
            cols = slice(tile * TILE, (tile + 1) * TILE)
            source = out_ref if side else total_ref
            add_products(source, out_ref, a_refs[mine], w_ref, starts[mine], cols)
    copies[2].wait()


def side_mix(column, w, starts, arrays, total):
    width, depth = w.shape[1], len(SIDES) * HEADS * DH
    return pl.pallas_call(
        functools.partial(side_kernel, starts=starts),
        name="side_mix",
        in_specs=[SMEM] + [VMEM] * len(arrays) + [HBM, VMEM],
        out_specs=[VMEM, VMEM],
        out_shape=[pltpu.VMEM((BLK, width), F32), pltpu.VMEM((depth, width), BF16)],
        scratch_shapes=[pltpu.SemaphoreType.DMA((len(SIDES),))],
        compiler_params=PARAMS,
        cost_estimate=cost(2 * BLK * depth * width, 2 * depth * width),
    )(column, *arrays, in_hbm(w), total)


def mix_kernel(*refs, count, starts, last):
    a_refs, (w_ref, total_ref), rest = refs[:count], refs[count : count + 2], refs[count + 2 :]
    if last:
        out_hbm, out_ref, sems = rest
    else:
        (out_ref,) = rest
    copies = []
    for tile in range(out_ref.shape[1] // TILE):
        cols = slice(tile * TILE, (tile + 1) * TILE)
        add_products(total_ref, out_ref, a_refs, w_ref, starts, cols)
        if last:
            copy = pltpu.make_async_copy(out_ref.at[:, cols], out_hbm.at[:, cols], sems.at[tile])
            copy.start()
            copies.append(copy)
    for copy in copies:
        copy.wait()


def mix(w, starts, arrays, total, last=False):
    width = w.shape[1]
    depth = sum(a.shape[1] for a in arrays)
    if last:
        out_shape = jax.ShapeDtypeStruct((BLK, width), BF16)
        scratch = [pltpu.VMEM((BLK, width), BF16), pltpu.SemaphoreType.DMA((width // TILE,))]
    else:
        out_shape, scratch = pltpu.VMEM((BLK, width), F32), []
    return pl.pallas_call(
        functools.partial(mix_kernel, count=len(arrays), starts=starts, last=last),
        name="mix",
        in_specs=[VMEM] * (len(arrays) + 2),
        out_specs=HBM if last else VMEM,
        out_shape=out_shape,
        scratch_shapes=scratch,
        compiler_params=PARAMS,
        cost_estimate=cost(2 * BLK * depth * width, 2 * depth * width),
    )(*arrays, w, total)


def along(value, shift, count):
    return lax.ppermute(value, "fsdp", [(i, (i + shift) % count) for i in range(count)])


def shards(q, k, v, gain, w):
    chips, ways = lax.axis_size("chip"), lax.axis_size("fsdp")
    core = lax.axis_index("core").reshape(1)
    column = lax.axis_index("fsdp").reshape(1)
    gain_row = gain.reshape(1, -1)
    states = block_states(k, v)
    own = lax.all_to_all(states, "chip", 0, 0, tiled=True)
    other = lax.ppermute(own, "core", [(0, 1), (1, 0)])
    sums = exclusive_sums(core, own, other, chips)
    carried = lax.all_to_all(sums, "chip", 0, 0, tiled=True)
    q_a, within_a, within_b = within_all(q, k, v)
    carried, q_a, within_a, within_b = lax.optimization_barrier(
        (carried, q_a, within_a, within_b)
    )
    (a0, a1), (b0, b1) = CALLS
    mine_a = finish_heads(q_a, within_a, carried, gain_row, a0, a1)
    mine_b = finish_heads(q, within_b, carried, gain_row, b0, b1, True)
    total = own_mix(column, w, [mine_a, mine_b])
    left_a, right_a, total = lax.optimization_barrier(
        (along(mine_a, 1, ways), along(mine_a, -1, ways), total)
    )
    far_a = along(left_a, 1, ways)
    left_b = along(mine_b, 1, ways)
    right_b = along(mine_b, -1, ways)
    far_b = along(right_b, -1, ways)
    depth = HEADS * DH
    at_a, at_b = a0 * DH, b0 * DH
    total, w = side_mix(column, w, (at_a, depth + at_a), [left_a, right_a], total)
    total = mix(w, (at_b, depth + at_b), [left_b, right_b], total)
    total = mix(w, (2 * depth + at_a,), [far_a], total)
    return mix(w, (2 * depth + at_b,), [far_b], total, True)


def solution(mesh):
    seq, fsdp = mesh.devices.shape
    fine = Mesh(mesh.devices.reshape(seq // CORES, CORES, fsdp), ("chip", "core", "fsdp"))
    rows = ("chip", "core")
    placed = (P(rows, "fsdp"), P(rows, "fsdp"), P(rows, "fsdp"), P("fsdp"), P(None, "fsdp"))
    return jax.shard_map(
        shards, mesh=fine, in_specs=placed, out_specs=P(rows, "fsdp"), check_vma=False
    )
```

```python
import functools

import jax
import jax.numpy as jnp
from jax import lax
from jax.experimental import pallas as pl
from jax.experimental.pallas import tpu as pltpu
from jax.sharding import Mesh
from jax.sharding import PartitionSpec as P

DH = 128
BLK = 512
HALF = BLK // 2
CORES = 2
HEADS = 8
CALLS = ((0, 4), (4, 8))
F32 = jnp.float32
BF16 = jnp.bfloat16
NN, NT, TN = ((1,), (0,)), ((1,), (1,)), ((0,), (0,))
SMEM = pl.BlockSpec(memory_space=pltpu.SMEM)
VMEM = pl.BlockSpec(memory_space=pltpu.VMEM)
HBM = pl.BlockSpec(memory_space=pltpu.HBM)
PARAMS = pltpu.CompilerParams(vmem_limit_bytes=20 * 2**20)


def dot(a, b, dims):
    return lax.dot_general(a, b, (dims, ((), ())), preferred_element_type=F32)


def in_vmem(value):
    return pltpu.with_memory_space_constraint(value, pltpu.VMEM)


def in_hbm(value):
    return pltpu.with_memory_space_constraint(value, pltpu.HBM)


def cost(flops, size):
    return pl.CostEstimate(flops=flops, bytes_accessed=size, transcendentals=0)


def within_block(q_ref, k_ref, v_ref, h, causal):
    cols = slice(h * DH, (h + 1) * DH)
    q0, q1 = q_ref[:HALF, cols], q_ref[HALF:, cols]
    k0, k1 = k_ref[:HALF, cols], k_ref[HALF:, cols]
    v0, v1 = v_ref[:HALF, cols], v_ref[HALF:, cols]
    s00 = jnp.where(causal, dot(q0, k0, NT), 0.0).astype(BF16)
    s10 = dot(q1, k0, NT).astype(BF16)
    s11 = jnp.where(causal, dot(q1, k1, NT), 0.0).astype(BF16)
    return dot(s00, v0, NN), dot(s10, v0, NN) + dot(s11, v1, NN)


def causal_mask():
    row = lax.broadcasted_iota(jnp.int32, (HALF, HALF), 0)
    col = lax.broadcasted_iota(jnp.int32, (HALF, HALF), 1)
    return col <= row


def finish(queries, within, state, gain):
    att = within + dot(queries, state, NN)
    mean = jnp.full((DH, DH), 1.0 / DH, BF16)
    mean_square = dot((att * att).astype(BF16), mean, NN)
    return (att * lax.rsqrt(mean_square + 1e-6) * gain).astype(BF16)


PARTS = 1


def state_kernel(k_hbm, v_hbm, out_ref, k_ref, v_ref, sems):
    width = k_ref.shape[1] // PARTS
    copies = []
    for part in range(PARTS):
        cols = slice(part * width, (part + 1) * width)
        for at, (hbm, ref) in enumerate(((k_hbm, k_ref), (v_hbm, v_ref))):
            copy = pltpu.make_async_copy(hbm.at[:, cols], ref.at[:, cols], sems.at[part, at])
            copy.start()
            copies.append(copy)
    for part in range(PARTS):
        copies[2 * part].wait()
        copies[2 * part + 1].wait()
        for h in range(part * width // DH, (part + 1) * width // DH):
            cols = slice(h * DH, (h + 1) * DH)
            out_ref[cols, :] = dot(k_ref[:, cols], v_ref[:, cols], TN).astype(BF16)


def block_states(k, v):
    width = k.shape[1]
    return pl.pallas_call(
        state_kernel,
        name="block_states",
        in_specs=[HBM, HBM],
        out_specs=VMEM,
        out_shape=jax.ShapeDtypeStruct((width, DH), BF16),
        scratch_shapes=[
            pltpu.VMEM(k.shape, BF16),
            pltpu.VMEM(v.shape, BF16),
            pltpu.SemaphoreType.DMA((PARTS, 2)),
        ],
        compiler_params=PARAMS,
        cost_estimate=cost(2 * BLK * DH * width, 2 * BLK * width * 2),
    )(in_hbm(k), in_hbm(v))


def scan_kernel(core_ref, own_ref, other_ref, out_ref, *, chips):
    rows = own_ref.shape[0] // chips
    second = (core_ref[0] == 1).astype(F32)
    before = jnp.zeros((rows, DH), F32)
    for chip in range(chips):
        at = slice(chip * rows, (chip + 1) * rows)
        other = other_ref[at, :].astype(F32)
        out_ref[at, :] = (before + second * other).astype(BF16)
        before = before + (own_ref[at, :].astype(F32) + other)


def exclusive_sums(core, own, other, chips):
    return pl.pallas_call(
        functools.partial(scan_kernel, chips=chips),
        name="exclusive_sums",
        in_specs=[SMEM, VMEM, VMEM],
        out_specs=VMEM,
        out_shape=jax.ShapeDtypeStruct(own.shape, BF16),
        compiler_params=PARAMS,
        cost_estimate=cost(own.size * 4, own.size * 6),
    )(core, own, other)


def within_kernel(q_hbm, k_hbm, v_hbm, qa_ref, a_ref, b_hbm, q_ref, k_ref, v_ref, b_ref, sems):
    copies, split = [], CALLS[0][1] * DH
    parts = (slice(0, split), slice(split, HEADS * DH))
    for part, cols in enumerate(parts):
        q_part = qa_ref if part == 0 else q_ref
        sources = (q_hbm.at[:, cols], k_hbm.at[:, cols], v_hbm.at[:, cols])
        targets = (q_part, k_ref.at[part], v_ref.at[part])
        for at, (source, target) in enumerate(zip(sources, targets)):
            copies.append(pltpu.make_async_copy(source, target, sems.at[part, at]))
            copies[-1].start()
    causal = causal_mask()
    for part, (first, last) in enumerate(CALLS):
        for copy in copies[3 * part : 3 * part + 3]:
            copy.wait()
        q_part, out_ref = (qa_ref, a_ref) if part == 0 else (q_ref, b_ref)
        for h in range(last - first):
            cols = slice(h * DH, (h + 1) * DH)
            top, bottom = within_block(q_part, k_ref.at[part], v_ref.at[part], h, causal)
            out_ref[:HALF, cols] = top
            out_ref[HALF:, cols] = bottom
    copy = pltpu.make_async_copy(b_ref, b_hbm, sems.at[0, 0])
    copy.start()
    copy.wait()


def within_all(q, k, v):
    shape = (BLK, HEADS // 2 * DH)
    return pl.pallas_call(
        within_kernel,
        name="within_all",
        in_specs=[HBM] * 3,
        out_specs=[VMEM, VMEM, HBM],
        out_shape=[
            pltpu.VMEM(shape, BF16),
            pltpu.VMEM(shape, F32),
            jax.ShapeDtypeStruct(shape, F32),
        ],
        scratch_shapes=[
            pltpu.VMEM(shape, BF16),
            pltpu.VMEM((2, *shape), BF16),
            pltpu.VMEM((2, *shape), BF16),
            pltpu.VMEM(shape, F32),
            pltpu.SemaphoreType.DMA((2, 3)),
        ],
        compiler_params=PARAMS,
        cost_estimate=cost(4 * BLK * BLK * DH * HEADS, BLK * DH * HEADS * 10),
    )(in_hbm(q), in_hbm(k), in_hbm(v))


def finish_kernel(q_ref, within_ref, carried_ref, gain_ref, out_ref, *scratch, first, last):
    if scratch:
        q_hbm, within_hbm = q_ref.at[:, first * DH : last * DH], within_ref
        q_ref, within_ref, sems = scratch
        copies = [
            pltpu.make_async_copy(q_hbm, q_ref, sems.at[0]),
            pltpu.make_async_copy(within_hbm, within_ref, sems.at[1]),
        ]
        for copy in copies:
            copy.start()
        for copy in copies:
            copy.wait()
    for h in range(first, last):
        cols = slice(h * DH, (h + 1) * DH)
        out_cols = slice((h - first) * DH, (h - first + 1) * DH)
        out_ref[:, out_cols] = finish(
            q_ref[:, out_cols], within_ref[:, out_cols], carried_ref[cols, :], gain_ref[:, cols]
        )


def finish_heads(q, within, carried, gain, first, last, fetch=False):
    heads = last - first
    shape = (BLK, heads * DH)
    scratch = [pltpu.VMEM(shape, BF16), pltpu.VMEM(shape, F32), pltpu.SemaphoreType.DMA((2,))]
    if fetch:
        q, within = in_hbm(q), in_hbm(within)
    return pl.pallas_call(
        functools.partial(finish_kernel, first=first, last=last),
        name="finish_heads",
        in_specs=[HBM if fetch else VMEM] * 2 + [VMEM] * 2,
        out_specs=VMEM,
        out_shape=jax.ShapeDtypeStruct(shape, BF16),
        scratch_shapes=scratch if fetch else [],
        compiler_params=PARAMS,
        cost_estimate=cost(4 * BLK * DH * DH * heads, BLK * DH * heads * 8),
    )(q, within, carried, gain)


TILE = 256


def weight_rows(w_hbm, column_ref, shift):
    depth = HEADS * DH
    ways = w_hbm.shape[0] // depth
    source = lax.rem(column_ref[0] + (shift + ways), ways)
    return w_hbm.at[pl.ds(pl.multiple_of(source * depth, depth), depth)]


def own_kernel(column_ref, *refs):
    *a_refs, w_hbm, total_ref, w_ref, sems = refs
    source = weight_rows(w_hbm, column_ref, 0)
    copies, rows, at = [], [], 0
    for piece, a_ref in enumerate(a_refs):
        rows.append(slice(at, at + a_ref.shape[1]))
        at += a_ref.shape[1]
        copies.append(
            pltpu.make_async_copy(source.at[rows[-1]], w_ref.at[rows[-1]], sems.at[piece])
        )
        copies[-1].start()
    for piece, a_ref in enumerate(a_refs):
        copies[piece].wait()
        for tile in range(total_ref.shape[1] // TILE):
            cols = slice(tile * TILE, (tile + 1) * TILE)
            term = dot(a_ref[...], w_ref[rows[piece], cols], NN)
            total_ref[:, cols] = term if piece == 0 else total_ref[:, cols] + term


def own_mix(column, w, arrays):
    width, depth = w.shape[1], HEADS * DH
    return pl.pallas_call(
        own_kernel,
        name="own_mix",
        in_specs=[SMEM] + [VMEM] * len(arrays) + [HBM],
        out_specs=VMEM,
        out_shape=pltpu.VMEM((BLK, width), F32),
        scratch_shapes=[
            pltpu.VMEM((depth, width), BF16),
            pltpu.SemaphoreType.DMA((len(arrays),)),
        ],
        compiler_params=PARAMS,
        cost_estimate=cost(2 * BLK * depth * width, 2 * depth * width),
    )(column, *arrays, in_hbm(w))


def add_products(total_ref, out_ref, a_refs, w_ref, starts, cols):
    total = total_ref[:, cols]
    for a_ref, start in zip(a_refs, starts):
        total = total + dot(a_ref[...], w_ref[start : start + a_ref.shape[1], cols], NN)
    out_ref[:, cols] = total.astype(out_ref.dtype)


SIDES = (-1, 1, 2)


def side_kernel(column_ref, *refs, starts):
    *a_refs, w_hbm, total_ref, out_ref, w_ref, sems = refs
    depth = HEADS * DH
    copies = []
    for at, shift in enumerate(SIDES):
        rows = slice(at * depth, (at + 1) * depth)
        copies.append(
            pltpu.make_async_copy(
                weight_rows(w_hbm, column_ref, shift), w_ref.at[rows], sems.at[at]
            )
        )
        copies[-1].start()
    half = len(a_refs) // 2
    for side in range(2):
        copies[side].wait()
        mine = slice(side * half, (side + 1) * half)
        for tile in range(out_ref.shape[1] // TILE):
            cols = slice(tile * TILE, (tile + 1) * TILE)
            source = out_ref if side else total_ref
            add_products(source, out_ref, a_refs[mine], w_ref, starts[mine], cols)
    copies[2].wait()


def side_mix(column, w, starts, arrays, total):
    width, depth = w.shape[1], len(SIDES) * HEADS * DH
    return pl.pallas_call(
        functools.partial(side_kernel, starts=starts),
        name="side_mix",
        in_specs=[SMEM] + [VMEM] * len(arrays) + [HBM, VMEM],
        out_specs=[VMEM, VMEM],
        out_shape=[pltpu.VMEM((BLK, width), F32), pltpu.VMEM((depth, width), BF16)],
        scratch_shapes=[pltpu.SemaphoreType.DMA((len(SIDES),))],
        compiler_params=PARAMS,
        cost_estimate=cost(2 * BLK * depth * width, 2 * depth * width),
    )(column, *arrays, in_hbm(w), total)


def mix_kernel(*refs, count, starts, last):
    a_refs, (w_ref, total_ref), rest = refs[:count], refs[count : count + 2], refs[count + 2 :]
    if last:
        out_hbm, out_ref, sems = rest
    else:
        (out_ref,) = rest
    copies = []
    for tile in range(out_ref.shape[1] // TILE):
        cols = slice(tile * TILE, (tile + 1) * TILE)
        add_products(total_ref, out_ref, a_refs, w_ref, starts, cols)
        if last:
            copy = pltpu.make_async_copy(out_ref.at[:, cols], out_hbm.at[:, cols], sems.at[tile])
            copy.start()
            copies.append(copy)
    for copy in copies:
        copy.wait()


def mix(w, starts, arrays, total, last=False):
    width = w.shape[1]
    depth = sum(a.shape[1] for a in arrays)
    if last:
        out_shape = jax.ShapeDtypeStruct((BLK, width), BF16)
        scratch = [pltpu.VMEM((BLK, width), BF16), pltpu.SemaphoreType.DMA((width // TILE,))]
    else:
        out_shape, scratch = pltpu.VMEM((BLK, width), F32), []
    return pl.pallas_call(
        functools.partial(mix_kernel, count=len(arrays), starts=starts, last=last),
        name="mix",
        in_specs=[VMEM] * (len(arrays) + 2),
        out_specs=HBM if last else VMEM,
        out_shape=out_shape,
        scratch_shapes=scratch,
        compiler_params=PARAMS,
        cost_estimate=cost(2 * BLK * depth * width, 2 * depth * width),
    )(*arrays, w, total)


def along(value, shift, count):
    return lax.ppermute(value, "fsdp", [(i, (i + shift) % count) for i in range(count)])


def shards(q, k, v, gain, w):
    chips, ways = lax.axis_size("chip"), lax.axis_size("fsdp")
    core = lax.axis_index("core").reshape(1)
    column = lax.axis_index("fsdp").reshape(1)
    gain_row = gain.reshape(1, -1)
    states = block_states(k, v)
    own = lax.all_to_all(states, "chip", 0, 0, tiled=True)
    other = lax.ppermute(own, "core", [(0, 1), (1, 0)])
    sums = exclusive_sums(core, own, other, chips)
    carried = lax.all_to_all(sums, "chip", 0, 0, tiled=True)
    q_a, within_a, within_b = within_all(q, k, v)
    carried, q_a, within_a, within_b = lax.optimization_barrier(
        (carried, q_a, within_a, within_b)
    )
    (a0, a1), (b0, b1) = CALLS
    mine_a = finish_heads(q_a, within_a, carried, gain_row, a0, a1)
    mine_b = finish_heads(q, within_b, carried, gain_row, b0, b1, True)
    total = own_mix(column, w, [mine_a, mine_b])
    left_a, right_a, total = lax.optimization_barrier(
        (along(mine_a, 1, ways), along(mine_a, -1, ways), total)
    )
    far_a = along(left_a, 1, ways)
    left_b = along(mine_b, 1, ways)
    right_b = along(mine_b, -1, ways)
    far_b = along(right_b, -1, ways)
    depth = HEADS * DH
    at_a, at_b = a0 * DH, b0 * DH
    total, w = side_mix(column, w, (at_a, depth + at_a), [left_a, right_a], total)
    total = mix(w, (at_b, depth + at_b), [left_b, right_b], total)
    total = mix(w, (2 * depth + at_a,), [far_a], total)
    return mix(w, (2 * depth + at_b,), [far_b], total, True)


def solution(mesh):
    seq, fsdp = mesh.devices.shape
    fine = Mesh(mesh.devices.reshape(seq // CORES, CORES, fsdp), ("chip", "core", "fsdp"))
    rows = ("chip", "core")
    placed = (P(rows, "fsdp"), P(rows, "fsdp"), P(rows, "fsdp"), P("fsdp"), P(None, "fsdp"))
    return jax.shard_map(
        shards, mesh=fine, in_specs=placed, out_specs=P(rows, "fsdp"), check_vma=False
    )
```
